32 devices in a mesh: groups: 2 (over x), chan: 16 (over z, y, core).
Axes of the slice: x: 2, y: 2, z: 4, core: 2. Of those that a mesh axis runs over, the one named last changes fastest.
Arguments:
- data: bfloat16 [28672, 4096], P(('groups', 'chan')), parts along dimension 0, as said below
- alive: int32 [8192], P(('groups', 'chan')), parts along dimension 0, may hold values 0 or 1
- sources: int32 [2, 16], replicated, may hold values from 0 to 4095, as said below
Outputs:
- correlations: bfloat16 [4, 16, 256, 4096], P('groups', None, None, 'chan'), parts along dimension 0
The draws below stay inside these ranges and needn't reach their ends.
There are 2 independent parts, one for each index of `groups`. The reference program is written for one: setup_inputs(seed, part) draws one part's arguments, and reference() takes and returns one part's arrays. A program takes and returns all parts, laid end to end along the dimension named above; an argument that names none is the same for every part. Nothing has to cross between parts.
Inputs may be any that keep to these rules, and one draw needn't show every extreme that they name: `sources`: no channel number appears twice in the array, and channel 4096 - 1 is always one of them. `data`: samples have channel and time-block scales of their own.
All inputs are finite; a program needn't handle non-finite values. No bound on the sum of `alive` on one device may be relied on, other than what follows from the above.
Results may differ from the reference program's by a relative error of at most 0.0076.
Values may be sent and summed in bfloat16 or wider, within the bound.
No kernel may reach another device: no remote copies, remote signals or barrier semaphores. Data moves between devices by JAX's collectives and lax.ppermute only.
A program may use at most 128 MiB of HBM per device.

```python
import math
import jax
import jax.numpy as jnp
from jax import lax

SEGMENT_LENGTH = 512
NF = 128
LAGS = 256
SRC = 16
ROUNDS = 2
SEGMENT_TALLY = 28
CH = 4096
SAMPLES = 14336


def draw_data(key, part):
    stochastic_seeds = jax.random.split(key, 3)
    sensor_scaling = jnp.exp(jax.random.uniform(stochastic_seeds[0], (1, CH), jnp.float32, math.log(0.05), math.log(5.0)))
    transient_spikes = jnp.exp(jax.random.uniform(stochastic_seeds[1], (SEGMENT_TALLY * 8, 1), jnp.float32, math.log(0.3), math.log(3.0)))
    transient_spikes = jnp.repeat(transient_spikes, SEGMENT_LENGTH // 8, axis=0)
    background_wavefield = jax.random.normal(stochastic_seeds[2], (SAMPLES, CH), jnp.float32)
    return (background_wavefield * sensor_scaling * transient_spikes).astype(jnp.bfloat16)


def draw_sources(key, part):
    total = ROUNDS * SRC
    picked = jax.random.permutation(key, CH - 1)[:total].astype(jnp.int32)
    position = jax.random.randint(jax.random.fold_in(key, 7), (), 0, total)
    picked = jnp.where(jnp.arange(total) == position, CH - 1, picked).astype(jnp.int32)
    return picked.reshape(ROUNDS, SRC)


def plant(entries, key, low, high):
    place = [jax.random.randint(jax.random.fold_in(key, axis), (), 0, length) for axis, length in enumerate(entries.shape)]
    widest = entries.shape.index(max(entries.shape))
    beside = place[:widest] + [(place[widest] + 1) % entries.shape[widest]] + place[widest + 1:]
    return entries.at[tuple(place)].set(low).at[tuple(beside)].set(high)


def setup_inputs(seed: int = 0, part: int = 0) -> dict:
    key_list = jax.random.split(jax.random.key(seed), 4)
    part_splits = jax.random.split(jax.random.fold_in(key_list[3], part), 4)
    return {
        "data": draw_data(jax.random.fold_in(jax.random.fold_in(key_list[3], part), 71), part),
        "alive": plant((jax.random.randint(part_splits[1], (CH,), 0, 10) < 9).astype(jnp.int32), jax.random.fold_in(part_splits[1], 1), 0, 1),
        "sources": draw_sources(jax.random.fold_in(key_list[3], 71), part),
    }


def forward_table():
    times = jnp.arange(SEGMENT_LENGTH, dtype=jnp.int32)[:, None]
    bins = jnp.arange(NF, dtype=jnp.int32)[None, :] + 1
    angle = 2.0 * math.pi / SEGMENT_LENGTH * (bins * times % SEGMENT_LENGTH).astype(jnp.float32)
    table = jnp.concatenate([jnp.cos(angle), -jnp.sin(angle)], axis=1) / math.sqrt(SEGMENT_LENGTH)
    return table.astype(jnp.bfloat16)

def inverse_table():
    shifts = jnp.arange(LAGS, dtype=jnp.int32)[:, None] - LAGS // 2
    bins = jnp.arange(NF, dtype=jnp.int32)[None, :] + 1
    angle = 2.0 * math.pi / SEGMENT_LENGTH * (bins * shifts % SEGMENT_LENGTH).astype(jnp.float32)
    return jnp.concatenate([jnp.cos(angle), -jnp.sin(angle)], axis=1).astype(jnp.bfloat16)

def reference(data, alive, sources):
    blocks = data.reshape(SEGMENT_TALLY, SEGMENT_LENGTH, data.shape[1]).astype(jnp.float32)
    spectra = jnp.einsum('tk,wtc->wkc', forward_table().astype(jnp.float32), blocks)
    level = lax.optimization_barrier(jnp.mean(spectra[:, :NF] ** 2 + spectra[:, NF:] ** 2, axis=0))
    factor = alive.astype(jnp.float32)[None, :] / jnp.sqrt(level + 0.01)
    factor = jnp.concatenate([factor, factor], axis=0)
    whitened = (spectra * factor[None]).astype(jnp.bfloat16)
    ids = sources.reshape(-1).astype(jnp.int32)
    src = jnp.transpose(jnp.take(whitened, ids, axis=2), (2, 0, 1)).astype(jnp.float32)
    wide = whitened.astype(jnp.float32)
    src_re, src_im = (src[:, :, :NF], src[:, :, NF:])
    own_re, own_im = (wide[:, :NF], wide[:, NF:])
    correlogram_realpart = jnp.einsum('qwf,wfc->qfc', src_re, own_re) + jnp.einsum('qwf,wfc->qfc', src_im, own_im)
    cross_imaginary = jnp.einsum('qwf,wfc->qfc', src_re, own_im) - jnp.einsum('qwf,wfc->qfc', src_im, own_re)
    cross = jnp.concatenate([correlogram_realpart, cross_imaginary], axis=1).astype(jnp.bfloat16)
    lagged = jnp.einsum('lk,qkc->qlc', inverse_table().astype(jnp.float32), cross.astype(jnp.float32))
    lagged = lagged / math.sqrt(NF * SEGMENT_TALLY)
    return lagged.reshape(ROUNDS, SRC, LAGS, data.shape[1]).astype(jnp.bfloat16)
```

```python
import math

import jax
import jax.numpy as jnp
from jax import lax
from jax.experimental import pallas as pl
from jax.experimental.pallas import tpu as pltpu
from jax.sharding import PartitionSpec as P

SEGMENT_LENGTH = 512
NF = 128
LAGS = 256
SRC = 16
ROUNDS = 2
SEGMENT_TALLY = 28

SOURCES = SRC * ROUNDS
BINS = 2 * NF
SUB = 8
TILES = NF // SUB
TEAM = 4
TEAM_WINDOWS = 7
STEP = 128
HELD = TEAM_WINDOWS * SEGMENT_LENGTH // TEAM
STRADDLE = HELD - SEGMENT_LENGTH
WHOLE = 16
SPLIT = 12
PACKED = 1024


def tile_order(table):
    table = table.reshape(2, TILES, SUB, table.shape[1])
    return jnp.transpose(table, (1, 0, 2, 3)).reshape(BINS, table.shape[3])


def forward_table():
    times = jnp.arange(SEGMENT_LENGTH, dtype=jnp.int32)[None, :]
    bins = jnp.arange(NF, dtype=jnp.int32)[:, None] + 1
    angle = 2.0 * math.pi / SEGMENT_LENGTH * (bins * times % SEGMENT_LENGTH).astype(jnp.float32)
    table = jnp.concatenate([jnp.cos(angle), -jnp.sin(angle)], axis=0) / math.sqrt(SEGMENT_LENGTH)
    return tile_order(table).astype(jnp.bfloat16)


def inverse_table():
    shifts = jnp.arange(LAGS, dtype=jnp.int32)[None, :] - LAGS // 2
    bins = jnp.arange(NF, dtype=jnp.int32)[:, None] + 1
    angle = 2.0 * math.pi / SEGMENT_LENGTH * (bins * shifts % SEGMENT_LENGTH).astype(jnp.float32)
    table = jnp.concatenate([jnp.cos(angle), -jnp.sin(angle)], axis=0)
    return tile_order(table).T.astype(jnp.bfloat16)


def prepare_kernel(place_ref, data_ref, table_ref, ids_ref, flags_ref, whole_ref, rows_ref, picked_ref, acc_ref):
    step = pl.program_id(0)
    place = place_ref[0]
    columns = data_ref.shape[1]
    width = columns // TEAM
    start = pl.multiple_of(place * STEP, STEP)
    block = data_ref[pl.ds(start, SEGMENT_LENGTH), :]
    spectra = jnp.dot(table_ref[...], block, preferred_element_type=jnp.float32).astype(jnp.bfloat16)
    for k in range(TEAM):
        whole_ref[k] = spectra[:, k * width : (k + 1) * width]
    for j in range(STRADDLE // STEP):
        source = pl.multiple_of(jnp.where(j < place, j, j + SEGMENT_LENGTH // STEP) * STEP, STEP)
        piece = data_ref[pl.ds(source, STEP), :]
        for k in range(TEAM):
            rows_ref[k, 0, j * STEP : (j + 1) * STEP, :] = piece[:, k * width : (k + 1) * width]
    channel = lax.broadcasted_iota(jnp.int32, (columns, 128), 0) + step * columns
    chosen = jnp.where(channel == ids_ref[...], 1.0, 0.0).astype(jnp.bfloat16)
    part = jnp.dot(data_ref[...], chosen, preferred_element_type=jnp.float32)

    @pl.when(step == 0)
    def _():
        acc_ref[...] = part

    @pl.when(step > 0)
    def _():
        acc_ref[...] += part

    @pl.when(step == pl.num_programs(0) - 1)
    def _():
        picked_ref[:, :HELD] = acc_ref[...].T[:SOURCES, :].astype(jnp.bfloat16)
        picked_ref[:, HELD:] = flags_ref[...]


def prepare(place, data, table, ids, flags, count):
    columns = data.shape[1] // count * TEAM
    steps = count // TEAM
    width = columns // TEAM
    return pl.pallas_call(
        prepare_kernel,
        grid_spec=pltpu.PrefetchScalarGridSpec(
            num_scalar_prefetch=1,
            grid=(steps,),
            in_specs=[
                pl.BlockSpec((HELD, columns), lambda i, p: (0, i)),
                pl.BlockSpec((BINS, SEGMENT_LENGTH), lambda i, p: (0, 0)),
                pl.BlockSpec((1, 128), lambda i, p: (0, 0)),
                pl.BlockSpec((SOURCES, PACKED - HELD), lambda i, p: (0, 0)),
            ],
            out_specs=[
                pl.BlockSpec((TEAM, BINS, width), lambda i, p: (i, 0, 0)),
                pl.BlockSpec((TEAM, 1, STRADDLE, width), lambda i, p: (0, i, 0, 0)),
                pl.BlockSpec((SOURCES, PACKED), lambda i, p: (0, 0)),
            ],
            scratch_shapes=[pltpu.VMEM((HELD, 128), jnp.float32)],
        ),
        out_shape=[
            jax.ShapeDtypeStruct((count, BINS, width), jnp.bfloat16),
            jax.ShapeDtypeStruct((TEAM, steps, STRADDLE, width), jnp.bfloat16),
            jax.ShapeDtypeStruct((SOURCES, PACKED), jnp.bfloat16),
        ],
        compiler_params=pltpu.CompilerParams(vmem_limit_bytes=24 << 20),
    )(place, data, table, ids, flags)


def straddle_kernel(rows_ref, table_ref, out_ref):
    width = rows_ref.shape[3]
    rows = rows_ref[...].reshape(TEAM * STRADDLE, width)
    for k in range(TEAM * STRADDLE // SEGMENT_LENGTH):
        block = rows[k * SEGMENT_LENGTH : (k + 1) * SEGMENT_LENGTH]
        spectra = jnp.dot(table_ref[...], block, preferred_element_type=jnp.float32)
        out_ref[0, k * BINS : (k + 1) * BINS, :] = spectra.astype(jnp.bfloat16)


def straddle(rows, table):
    _, steps, _, width = rows.shape
    depth = TEAM * STRADDLE // SEGMENT_LENGTH * BINS
    return pl.pallas_call(
        straddle_kernel,
        grid=(steps,),
        in_specs=[
            pl.BlockSpec((TEAM, 1, STRADDLE, width), lambda i: (0, i, 0, 0)),
            pl.BlockSpec((BINS, SEGMENT_LENGTH), lambda i: (0, 0)),
        ],
        out_specs=pl.BlockSpec((1, depth, width), lambda i: (i, 0, 0)),
        out_shape=jax.ShapeDtypeStruct((steps, depth, width), jnp.bfloat16),
        compiler_params=pltpu.CompilerParams(vmem_limit_bytes=16 << 20),
    )(rows, table)


PHASES = 4
BATCH = TILES // PHASES
QUERIES = SOURCES // PHASES


def correlate_kernel(left_ref, whole_ref, split_ref, alive_ref, inverse_ref, out_ref, cross_ref):
    step = pl.program_id(0)
    width = whole_ref.shape[2]
    rows = 2 * SUB
    cut = WHOLE * rows

    @pl.when(step < PHASES)
    def _():
        alive = alive_ref[...]
        for k in range(BATCH):
            whole = whole_ref[:, k * rows : (k + 1) * rows, :]
            split = split_ref[:, k * rows : (k + 1) * rows, :]
            power = jnp.sum(jnp.square(whole.astype(jnp.float32)), axis=0)
            power += jnp.sum(jnp.square(split.astype(jnp.float32)), axis=0)
            level = (power[:SUB] + power[SUB:]) / SEGMENT_TALLY
            factor = alive / jnp.sqrt(level + 0.01)
            factor = jnp.concatenate([factor, factor], axis=0)[None]
            cross = jnp.dot(
                left_ref[k, :, :cut], whole.reshape(WHOLE * rows, width), preferred_element_type=jnp.float32
            )
            cross += jnp.dot(
                left_ref[k, :, cut:], split.reshape(SPLIT * rows, width), preferred_element_type=jnp.float32
            )
            cross = cross.reshape(SOURCES, rows, width)
            cross = jnp.where(factor > 0.0, cross * factor, 0.0).astype(jnp.bfloat16)
            start = pl.multiple_of((step * BATCH + k) * rows, rows)
            cross_ref[:, pl.ds(start, rows), :] = cross

    @pl.when(step >= PHASES)
    def _():
        first = (step - PHASES) * QUERIES
        for k in range(QUERIES):
            lagged = jnp.dot(inverse_ref[...], cross_ref[first + k], preferred_element_type=jnp.float32)
            out_ref[k] = (lagged / math.sqrt(NF * SEGMENT_TALLY)).astype(jnp.bfloat16)


def correlate(left, whole, split, alive, inverse):
    width = whole.shape[2]
    depth = left.shape[2]
    return pl.pallas_call(
        correlate_kernel,
        grid=(2 * PHASES,),
        in_specs=[
            pl.BlockSpec((BATCH, SOURCES * 2 * SUB, depth), lambda i: (jnp.minimum(i, PHASES - 1), 0, 0)),
            pl.BlockSpec((WHOLE, BATCH * 2 * SUB, width), lambda i: (0, jnp.minimum(i, PHASES - 1), 0)),
            pl.BlockSpec((SPLIT, BATCH * 2 * SUB, width), lambda i: (0, jnp.minimum(i, PHASES - 1), 0)),
            pl.BlockSpec((1, width), lambda i: (0, 0)),
            pl.BlockSpec((LAGS, BINS), lambda i: (0, 0)),
        ],
        out_specs=pl.BlockSpec((QUERIES, LAGS, width), lambda i: (jnp.maximum(i - PHASES, 0), 0, 0)),
        out_shape=jax.ShapeDtypeStruct((SOURCES, LAGS, width), jnp.bfloat16),
        scratch_shapes=[pltpu.VMEM((SOURCES, BINS, width), jnp.bfloat16)],
        compiler_params=pltpu.CompilerParams(vmem_limit_bytes=32 << 20),
    )(left, whole, split, alive, inverse)


def source_matrix(samples, alive, table):
    samples = samples.reshape(SOURCES, TEAM, TEAM_WINDOWS, SEGMENT_LENGTH)
    whole = samples[:, :, 0::2].reshape(SOURCES, WHOLE, SEGMENT_LENGTH)
    split = samples[:, :, 1::2].reshape(SOURCES, SPLIT, SEGMENT_LENGTH)
    samples = jnp.concatenate([whole, split], axis=1)
    spectra = jnp.einsum("qwt,kt->qwk", samples, table, preferred_element_type=jnp.float32)
    spectra = spectra.reshape(SOURCES, SEGMENT_TALLY, TILES, 2, SUB)
    level = jnp.mean(spectra[:, :, :, 0] ** 2 + spectra[:, :, :, 1] ** 2, axis=1)
    factor = alive[:, None, None] / jnp.sqrt(level + 0.01)
    src = (spectra * factor[:, None, :, None, :]).astype(jnp.bfloat16)
    src = jnp.transpose(src, (2, 0, 1, 3, 4))
    turned = jnp.stack([-src[:, :, :, 1], src[:, :, :, 0]], axis=3)
    depth = SEGMENT_TALLY * 2 * SUB
    both = jnp.stack([src, turned], axis=2).reshape(TILES, SOURCES, 2, 1, depth)
    row = jnp.arange(SUB, dtype=jnp.int32)[:, None]
    column = jnp.arange(depth, dtype=jnp.int32)[None, :]
    left = jnp.where(column % SUB == row, both, jnp.bfloat16(0.0))
    return left.reshape(TILES, SOURCES * 2 * SUB, depth)


def body(data, alive, sources):
    count = lax.axis_size("chan")
    me = lax.axis_index("chan")
    width = data.shape[1] // count
    table = forward_table()
    ids = sources.reshape(-1)
    near = ids[:, None] == me * width + jnp.arange(width, dtype=jnp.int32)[None, :]
    flags = jnp.sum(jnp.where(near, alive[None, :], 0), axis=1).astype(jnp.bfloat16)
    if data.shape[0] == HELD and count == TEAM * TEAM:
        lanes = jnp.concatenate([ids, jnp.full((128 - SOURCES,), -1, jnp.int32)])[None, :]
        flags = jnp.broadcast_to(flags[:, None], (SOURCES, PACKED - HELD))
        place = (me % TEAM).astype(jnp.int32)[None]
        whole, rows, picked = prepare(place, data, table, lanes, flags, count)
        planes = range(count // TEAM)
        teams = [[z * TEAM + p for p in range(TEAM)] for z in planes]
        across = [[z * TEAM + p for z in planes] for p in range(TEAM)]
        picked = lax.all_gather(picked, "chan", axis=0)
        rows = lax.all_to_all(rows, "chan", 0, 0, tiled=True, axis_index_groups=teams)
        whole = lax.all_to_all(whole, "chan", 0, 0, tiled=True)
        split = straddle(rows, table)
        split = lax.all_to_all(split, "chan", 0, 0, tiled=True, axis_index_groups=across)
        split = split.reshape(SPLIT, BINS, width)
        alive_sources = jnp.sum(picked[:, :, HELD].astype(jnp.float32), axis=0)
        samples = jnp.transpose(picked[:, :, :HELD], (1, 0, 2))
    else:
        chosen = jnp.where(jnp.arange(data.shape[1], dtype=jnp.int32)[:, None] == ids[None, :], 1.0, 0.0)
        picked = jnp.dot(data, chosen.astype(jnp.bfloat16), preferred_element_type=jnp.float32)
        picked = lax.all_gather(picked.astype(jnp.bfloat16), "chan", axis=0)
        samples = jnp.transpose(picked, (2, 0, 1))
        alive_sources = lax.psum(flags.astype(jnp.float32), "chan")
        blocks = data.reshape(data.shape[0], count, width)
        blocks = lax.all_to_all(blocks, "chan", split_axis=1, concat_axis=0, tiled=True)
        blocks = blocks.reshape(SEGMENT_TALLY, SEGMENT_LENGTH, width)
        spectra = jnp.einsum("kt,wtc->wkc", table, blocks, preferred_element_type=jnp.float32)
        spectra = spectra.astype(jnp.bfloat16).reshape(TEAM, TEAM_WINDOWS, BINS, width)
        whole = spectra[:, 0::2].reshape(WHOLE, BINS, width)
        split = spectra[:, 1::2].reshape(SPLIT, BINS, width)
    left = source_matrix(samples, alive_sources, table)
    out = correlate(left, whole, split, alive.astype(jnp.float32)[None, :], inverse_table())
    return out.reshape(ROUNDS, SRC, LAGS, width)


def solution(mesh):
    return jax.shard_map(
        body,
        mesh=mesh,
        in_specs=(P(("groups", "chan"), None), P(("groups", "chan")), P()),
        out_specs=P("groups", None, None, "chan"),
        check_vma=False,
    )
```

```python
import functools
import math

import jax
import jax.numpy as jnp
import ml_dtypes
import numpy as np
from jax import lax
from jax.experimental import pallas as pl
from jax.experimental.pallas import tpu as pltpu
from jax.sharding import PartitionSpec as P

SEGMENT_LENGTH = 512
NF = 128
LAGS = 256
SRC = 16
ROUNDS = 2
SEGMENT_TALLY = 28

SOURCES = SRC * ROUNDS
BINS = 2 * NF
SUB = 8
TILES = NF // SUB
TEAM = 4
TEAM_WINDOWS = 7
STEP = 128
HELD = TEAM_WINDOWS * SEGMENT_LENGTH // TEAM
STRADDLE = HELD - SEGMENT_LENGTH
HALF = SEGMENT_LENGTH // 2
WHOLE = 16
SPLIT = 12
PACKED = 1024
SHARE = SOURCES // TEAM
DEPTH = 512
LARGE = 56 << 20


def angles(times):
    bins = np.arange(NF)[:, None] + 1
    turn = bins * times[None, :] % SEGMENT_LENGTH * (2.0 * np.pi / SEGMENT_LENGTH)
    table = np.stack([np.cos(turn), -np.sin(turn)])
    table = table.reshape(2, TILES, SUB, times.size).transpose(1, 0, 2, 3)
    return table.reshape(BINS, times.size)


def forward_table():
    table = angles(np.arange(SEGMENT_LENGTH)) / math.sqrt(SEGMENT_LENGTH)
    return jnp.asarray(table.astype(ml_dtypes.bfloat16))


def inverse_table():
    table = angles(np.arange(LAGS) - LAGS // 2)
    return jnp.asarray(np.ascontiguousarray(table.T).astype(ml_dtypes.bfloat16))


def position():
    me = lax.axis_index("chan")
    return me // TEAM, me % TEAM


def straddling(data_ref, j, place, column, width):
    row = pl.multiple_of(jnp.where(j < place, j, j + SEGMENT_LENGTH // STEP) * STEP, STEP)
    return data_ref[pl.ds(row, STEP), pl.ds(pl.multiple_of(column * width, width), width)]


def transform(table_ref, block):
    return jnp.dot(table_ref[...], block, preferred_element_type=jnp.float32).astype(jnp.bfloat16)


def prepare_kernel(sources_ref, alive_ref, data_ref, table_ref, whole_ref, acc_ref):
    step = pl.program_id(0)
    _, place = position()
    columns = data_ref.shape[1]
    width = columns // TEAM
    start = pl.multiple_of(place * STEP, STEP)
    for k in range(TEAM):
        lanes = slice(k * width, (k + 1) * width)
        whole_ref[step * TEAM + k, :BINS, :] = transform(table_ref, data_ref[pl.ds(start, SEGMENT_LENGTH), lanes])
    lane = lax.broadcasted_iota(jnp.int32, (1, 128), 1)
    ids = jnp.full((1, 128), -1, jnp.int32)
    for q in range(SOURCES):
        ids = jnp.where(lane == q, sources_ref[q // SRC, q % SRC], ids)
    channel = lax.broadcasted_iota(jnp.int32, (columns, 128), 0)
    chosen = jnp.where(channel == ids - step * columns, 1.0, 0.0).astype(jnp.bfloat16)
    part = jnp.dot(data_ref[...], chosen, preferred_element_type=jnp.float32)

    @pl.when(step == 0)
    def _():
        acc_ref[...] = part

    @pl.when(step > 0)
    def _():
        acc_ref[...] += part

    @pl.when(step == pl.num_programs(0) - 1)
    def _():
        row = lax.broadcasted_iota(jnp.int32, (SOURCES, PACKED - HELD), 0)
        flags = jnp.zeros((SOURCES, PACKED - HELD), jnp.float32)
        for q in range(SOURCES):
            local = sources_ref[q // SRC, q % SRC] - lax.axis_index("chan") * width
            inside = (local >= 0) & (local < width)
            flag = jnp.where(inside, alive_ref[jnp.clip(local, 0, width - 1)], 0)
            flags = jnp.where(row == q, flag.astype(jnp.float32), flags)
        picked = jnp.concatenate([acc_ref[...].T[:SOURCES, :], flags], axis=1)
        for k in range(TEAM):
            quarter = picked[k * SHARE : (k + 1) * SHARE]
            rows = [quarter[:, c * width : (c + 1) * width] for c in range(PACKED // width)]
            rows = jnp.concatenate(rows, axis=0).astype(jnp.bfloat16)
            for plane in range(whole_ref.shape[0] // TEAM):
                whole_ref[plane * TEAM + k, BINS:, :] = rows


def prepare(sources, alive, data, table, count):
    columns = data.shape[1] // count * TEAM
    width = columns // TEAM
    depth = BINS + SHARE * PACKED // width
    return pl.pallas_call(
        prepare_kernel,
        grid=(count // TEAM,),
        in_specs=[
            pl.BlockSpec(memory_space=pltpu.SMEM),
            pl.BlockSpec(memory_space=pltpu.SMEM),
            pl.BlockSpec((HELD, columns), lambda i: (0, i)),
            pl.BlockSpec((BINS, SEGMENT_LENGTH), lambda i: (0, 0)),
        ],
        out_specs=pl.BlockSpec((count, depth, width), lambda i: (0, 0, 0)),
        scratch_shapes=[pltpu.VMEM((HELD, 128), jnp.float32)],
        out_shape=jax.ShapeDtypeStruct((count, depth, width), jnp.bfloat16),
        compiler_params=pltpu.CompilerParams(vmem_limit_bytes=LARGE),
        name="prepare",
    )(sources, alive, data, table)


def lend_kernel(data_ref, out_ref):
    _, place = position()
    width = out_ref.shape[2]
    for side in range(2):
        for j in range(STRADDLE // STEP):
            piece = straddling(data_ref, j, place, side * 2 + 1 - place % 2, width)
            out_ref[side, j * STEP : (j + 1) * STEP, :] = piece


def lend(data, count):
    width = data.shape[1] // count
    return pl.pallas_call(
        lend_kernel,
        grid=(count // TEAM,),
        in_specs=[pl.BlockSpec((HELD, TEAM * width), lambda i: (0, i))],
        out_specs=pl.BlockSpec((2, STRADDLE, width), lambda i: (i, 0, 0)),
        out_shape=jax.ShapeDtypeStruct((count // 2, STRADDLE, width), jnp.bfloat16),
        compiler_params=pltpu.CompilerParams(vmem_limit_bytes=LARGE),
        cost_estimate=pl.CostEstimate(flops=0, bytes_accessed=1 << 20, transcendentals=0),
        name="lend",
    )(data)


def halves_kernel(data_ref, lent_ref, table_ref, keep_ref, give_ref, scratch_ref):
    _, place = position()
    side, core = place // 2, place % 2
    width = keep_ref.shape[2]
    for slot, (out_ref, target) in enumerate(((keep_ref, side), (give_ref, 1 - side))):
        chip_ref = scratch_ref.at[slot]
        for j in range(STRADDLE // STEP):
            start = pl.multiple_of(core * STRADDLE + j * STEP, STEP)
            chip_ref[pl.ds(start, STEP), :] = straddling(data_ref, j, place, target * 2 + core, width)
        chip_ref[pl.ds(pl.multiple_of((1 - core) * STRADDLE, STEP), STRADDLE), :] = lent_ref[target]
        start = pl.multiple_of(side * HALF, HALF)
        out_ref[0, :BINS, :] = transform(table_ref, chip_ref[pl.ds(start, SEGMENT_LENGTH), :])
        start = pl.multiple_of((1 - side) * SEGMENT_LENGTH, HALF)
        out_ref[0, BINS:, :] = chip_ref[pl.ds(start, HALF), :]


def halves(data, lent, table, count):
    width = data.shape[1] // count
    planes = count // TEAM
    shape = jax.ShapeDtypeStruct((planes, BINS + HALF, width), jnp.bfloat16)
    return pl.pallas_call(
        halves_kernel,
        grid=(planes,),
        in_specs=[
            pl.BlockSpec((HELD, TEAM * width), lambda i: (0, i)),
            pl.BlockSpec((2, STRADDLE, width), lambda i: (i, 0, 0)),
            pl.BlockSpec((BINS, SEGMENT_LENGTH), lambda i: (0, 0)),
        ],
        out_specs=[pl.BlockSpec((1, BINS + HALF, width), lambda i: (i, 0, 0))] * 2,
        scratch_shapes=[pltpu.VMEM((2, 2 * STRADDLE, width), jnp.bfloat16)],
        out_shape=[shape, shape],
        compiler_params=pltpu.CompilerParams(vmem_limit_bytes=LARGE),
        cost_estimate=pl.CostEstimate(flops=0, bytes_accessed=1 << 20, transcendentals=0),
        name="halves",
    )(data, lent, table)


def straddle_kernel(keep_ref, got_ref, table_ref, *refs):
    out_refs, scratch_ref = refs[:-1], refs[-1]
    mine, place = position()
    side = place // 2
    for k, out_ref in enumerate(out_refs):
        plane = mine ^ k
        out_ref[2 * side] = keep_ref[plane, :BINS, :]
        out_ref[2 - 2 * side] = got_ref[plane, :BINS, :]
        scratch_ref[k, pl.ds(pl.multiple_of(side * HALF, HALF), HALF), :] = keep_ref[plane, BINS:, :]
        scratch_ref[k, pl.ds(pl.multiple_of((1 - side) * HALF, HALF), HALF), :] = got_ref[plane, BINS:, :]
        out_ref[1] = transform(table_ref, scratch_ref[k])


def straddle(keep, got, table):
    planes, _, width = keep.shape
    shape = jax.ShapeDtypeStruct((SPLIT // TEAM, BINS, width), jnp.bfloat16)
    return pl.pallas_call(
        straddle_kernel,
        out_shape=[shape] * planes,
        scratch_shapes=[pltpu.VMEM((planes, SEGMENT_LENGTH, width), jnp.bfloat16)],
        compiler_params=pltpu.CompilerParams(vmem_limit_bytes=16 << 20),
        cost_estimate=pl.CostEstimate(flops=0, bytes_accessed=1 << 20, transcendentals=0),
        name="straddle",
    )(keep, got, table)


def whiten_kernel(picked_ref, table_ref, out_ref, samples_ref):
    width = picked_ref.shape[2]
    flags = jnp.zeros((SHARE, PACKED - HELD), jnp.float32)
    for j in range(picked_ref.shape[0]):
        rows = picked_ref[j].astype(jnp.float32)
        for block in range(PACKED // 128):
            lane = block * 128 % width
            piece = rows[block * 128 // width * SHARE :][:SHARE, lane : lane + 128]
            if block * 128 < HELD:
                window, lane = divmod(j * HELD + block * 128, SEGMENT_LENGTH)
                samples_ref[window * SHARE : (window + 1) * SHARE, lane : lane + 128] = piece
            else:
                flags += piece
    spectra = lax.dot_general(
        samples_ref[...].astype(jnp.bfloat16),
        table_ref[...],
        (((1,), (1,)), ((), ())),
        preferred_element_type=jnp.float32,
    ).reshape(SEGMENT_TALLY, SHARE, BINS)
    power = jnp.sum(jnp.square(spectra), axis=0)
    lane = lax.broadcasted_iota(jnp.int32, (SHARE, BINS), 1)
    other = jnp.where(lane % (2 * SUB) < SUB, pltpu.roll(power, BINS - SUB, 1), pltpu.roll(power, SUB, 1))
    level = (power + other) / SEGMENT_TALLY
    factor = jnp.concatenate([flags] * (BINS // 128), axis=1) / jnp.sqrt(level + 0.01)
    src = (spectra * factor[None]).astype(jnp.bfloat16).astype(jnp.float32)
    lane = lax.broadcasted_iota(jnp.int32, (SHARE, 128), 1) // (2 * SUB)
    each = 128 // (2 * SUB)
    for tile in range(TILES):
        half, at = divmod(tile, each)
        for group in range(DEPTH // 128):
            out = jnp.zeros((SHARE, 128), jnp.float32)
            for k in range(each):
                window = group * each + k
                if window < SEGMENT_TALLY:
                    piece = src[window, :, half * 128 : (half + 1) * 128]
                    shift = (k - at) * 2 * SUB % 128
                    piece = pltpu.roll(piece, shift, 1) if shift else piece
                    out = jnp.where(lane == k, piece, out)
            out_ref[tile, :, group * 128 : (group + 1) * 128] = out.astype(jnp.bfloat16)


def whiten(whole, table):
    count, depth, width = whole.shape
    rows = depth - BINS
    return pl.pallas_call(
        whiten_kernel,
        grid=(1,),
        in_specs=[
            pl.BlockSpec((count, rows, width), lambda i: (0, BINS // rows, 0)),
            pl.BlockSpec((BINS, SEGMENT_LENGTH), lambda i: (0, 0)),
        ],
        out_specs=pl.BlockSpec((TILES, SHARE, DEPTH), lambda i: (0, 0, 0)),
        scratch_shapes=[pltpu.VMEM((SEGMENT_TALLY * SHARE, SEGMENT_LENGTH), jnp.float32)],
        out_shape=jax.ShapeDtypeStruct((TILES, SHARE, DEPTH), jnp.bfloat16),
        compiler_params=pltpu.CompilerParams(vmem_limit_bytes=16 << 20),
        cost_estimate=pl.CostEstimate(flops=0, bytes_accessed=1 << 18, transcendentals=0),
        name="whiten",
    )(whole, table)


def left_kernel(*refs):
    src_refs, left_ref = refs[:-1], refs[-1]
    src = jnp.concatenate([ref[0].astype(jnp.float32) for ref in src_refs], axis=0)
    lane = lax.broadcasted_iota(jnp.int32, (SOURCES, DEPTH), 1)
    turned = jnp.where(lane % (2 * SUB) < SUB, -pltpu.roll(src, DEPTH - SUB, 1), pltpu.roll(src, SUB, 1))
    row = lax.broadcasted_iota(jnp.int32, (1, 2 * SUB, DEPTH), 1)
    lane = lax.broadcasted_iota(jnp.int32, (1, 2 * SUB, DEPTH), 2)
    both = jnp.where(row < SUB, src[:, None, :], turned[:, None, :])
    both = jnp.where(lane % SUB == row % SUB, both, 0.0)
    left_ref[0] = both.reshape(SOURCES * 2 * SUB, DEPTH).astype(jnp.bfloat16)


def left_factor(src):
    return pl.pallas_call(
        left_kernel,
        grid=(TILES,),
        in_specs=[pl.BlockSpec((1, SHARE, DEPTH), lambda i: (i, 0, 0))] * TEAM,
        out_specs=pl.BlockSpec((1, SOURCES * 2 * SUB, DEPTH), lambda i: (i, 0, 0)),
        out_shape=jax.ShapeDtypeStruct((TILES, SOURCES * 2 * SUB, DEPTH), jnp.bfloat16),
        compiler_params=pltpu.CompilerParams(vmem_limit_bytes=16 << 20),
        cost_estimate=pl.CostEstimate(flops=0, bytes_accessed=1 << 20, transcendentals=0),
        name="left",
    )(*src)


def whiten_all(samples, alive, table):
    samples = samples.reshape(SOURCES, SEGMENT_TALLY, SEGMENT_LENGTH)
    spectra = jnp.einsum("qwt,kt->qwk", samples, table, preferred_element_type=jnp.float32)
    power = jnp.mean(spectra**2, axis=1).reshape(SOURCES, TILES, 2, SUB)
    level = power[:, :, :1] + power[:, :, 1:]
    factor = alive[:, None, None, None] / jnp.sqrt(level + 0.01)
    factor = jnp.broadcast_to(factor, (SOURCES, TILES, 2, SUB)).reshape(SOURCES, BINS)
    src = (spectra * factor[:, None, :]).astype(jnp.bfloat16)
    src = jnp.transpose(src.reshape(SOURCES, SEGMENT_TALLY, TILES, 2 * SUB), (2, 0, 1, 3))
    src = src.reshape(TILES, SOURCES, SEGMENT_TALLY * 2 * SUB)
    src = jnp.pad(src, ((0, 0), (0, 0), (0, DEPTH - SEGMENT_TALLY * 2 * SUB)))
    return [src[:, k * SHARE : (k + 1) * SHARE] for k in range(TEAM)]


PHASES = 4
BATCH = TILES // PHASES


def correlate_kernel(relative, left_ref, whole_ref, *refs):
    split_refs, (alive_ref, inverse_ref, out_ref, right_ref, cross_ref) = refs[:TEAM], refs[TEAM:]
    step = pl.program_id(0)
    mine, place = position() if relative else (0, 0)
    width = whole_ref.shape[2]
    rows = 2 * SUB
    span = TEAM_WINDOWS * rows

    @pl.when(step == 0)
    def _():
        pad = DEPTH - SEGMENT_TALLY * rows
        right_ref[:, DEPTH - pad :, :] = jnp.zeros((BATCH, pad, width), jnp.bfloat16)

    @pl.when(step < PHASES)
    def _():
        alive = alive_ref[...].astype(jnp.float32)
        for k in range(BATCH):
            tile = slice(k * rows, (k + 1) * rows)
            for j in range(WHOLE):
                start = j // TEAM * span + j % TEAM * 2 * rows
                right_ref[k, start : start + rows, :] = whole_ref[j, tile, :]
            for plane in range(TEAM):
                for j in range(SPLIT // TEAM):
                    start = pl.multiple_of((plane ^ mine) * span + (2 * j + 1) * rows, rows)
                    right_ref[k, pl.ds(start, rows), :] = split_refs[plane][j, tile, :]
            right = right_ref[k]
            power = jnp.square(right.astype(jnp.float32)).reshape(DEPTH // rows, rows, width)
            power = jnp.sum(power, axis=0)
            level = (power[:SUB] + power[SUB:]) / SEGMENT_TALLY
            factor = alive / jnp.sqrt(level + 0.01)
            factor = jnp.concatenate([factor, factor], axis=0)[None]
            cross = jnp.dot(left_ref[k], right, preferred_element_type=jnp.float32)
            cross = cross.reshape(SOURCES, rows, width)
            cross = jnp.where(factor > 0.0, cross * factor, 0.0).astype(jnp.bfloat16)
            start = pl.multiple_of((step * BATCH + k) * rows, rows)
            cross_ref[:, pl.ds(start, rows), :] = cross

    @pl.when(step >= PHASES)
    def _():
        first = ((step - PHASES) ^ place) * SHARE
        for k in range(SHARE):
            lagged = jnp.dot(inverse_ref[...], cross_ref[first + k], preferred_element_type=jnp.float32)
            out_ref[k] = (lagged / math.sqrt(NF * SEGMENT_TALLY)).astype(jnp.bfloat16)


def correlate(relative, left, whole, split, alive, inverse):
    width = whole.shape[2]
    early = lambda i: jnp.minimum(i, PHASES - 1)
    return pl.pallas_call(
        functools.partial(correlate_kernel, relative),
        grid=(2 * PHASES,),
        in_specs=[
            pl.BlockSpec((BATCH, SOURCES * 2 * SUB, DEPTH), lambda i: (early(i), 0, 0)),
            pl.BlockSpec((WHOLE, BATCH * 2 * SUB, width), lambda i: (0, early(i), 0)),
        ]
        + [pl.BlockSpec((SPLIT // TEAM, BATCH * 2 * SUB, width), lambda i: (0, early(i), 0))] * TEAM
        + [
            pl.BlockSpec((1, width), lambda i: (0, 0)),
            pl.BlockSpec((LAGS, BINS), lambda i: (0, 0)),
        ],
        out_specs=pl.BlockSpec((SHARE, LAGS, width), lambda i: (jnp.maximum(i - PHASES, 0), 0, 0)),
        scratch_shapes=[
            pltpu.VMEM((BATCH, DEPTH, width), jnp.bfloat16),
            pltpu.VMEM((SOURCES, BINS, width), jnp.bfloat16),
        ],
        out_shape=jax.ShapeDtypeStruct((SOURCES, LAGS, width), jnp.bfloat16),
        compiler_params=pltpu.CompilerParams(vmem_limit_bytes=24 << 20),
        name="correlate",
    )(left, whole, *split, alive, inverse)


def body(data, alive, sources):
    count = lax.axis_size("chan")
    width = data.shape[1] // count
    table = forward_table()
    relative = data.shape[0] == HELD and count == TEAM * TEAM
    if relative:
        swap = lambda x, k: lax.ppermute(x, "chan", [(i, i ^ k) for i in range(count)])
        whole = prepare(sources, alive, data, table, count)
        data, whole = lax.optimization_barrier((data, whole))
        lent = swap(lend(data, count), 1)
        whole = lax.all_to_all(whole, "chan", 0, 0, tiled=True)
        keep, give = halves(data, lent, table, count)
        split = straddle(keep, swap(give, 2), table)
        whole, _ = lax.optimization_barrier((whole, split[1]))
        split = [split[0]] + [swap(split[k], k * TEAM) for k in range(1, TEAM)]
        src = whiten(whole, table)
        src = [src] + [swap(src, k) for k in range(1, TEAM)]
    else:
        me = lax.axis_index("chan")
        ids = sources.reshape(-1)
        near = ids[:, None] == me * width + jnp.arange(width, dtype=jnp.int32)[None, :]
        flags = jnp.sum(jnp.where(near, alive[None, :], 0), axis=1).astype(jnp.float32)
        chosen = jnp.where(jnp.arange(data.shape[1], dtype=jnp.int32)[:, None] == ids[None, :], 1.0, 0.0)
        picked = jnp.dot(data, chosen.astype(jnp.bfloat16), preferred_element_type=jnp.float32)
        picked = lax.all_gather(picked.astype(jnp.bfloat16), "chan", axis=0)
        alive_sources = lax.psum(flags, "chan")
        blocks = data.reshape(data.shape[0], count, width)
        blocks = lax.all_to_all(blocks, "chan", split_axis=1, concat_axis=0, tiled=True)
        blocks = blocks.reshape(SEGMENT_TALLY, SEGMENT_LENGTH, width)
        spectra = jnp.einsum("kt,wtc->wkc", table, blocks, preferred_element_type=jnp.float32)
        spectra = spectra.astype(jnp.bfloat16).reshape(TEAM, TEAM_WINDOWS, BINS, width)
        whole = spectra[:, 0::2].reshape(WHOLE, BINS, width)
        split = [spectra[z, 1::2] for z in range(TEAM)]
        src = whiten_all(jnp.transpose(picked, (2, 0, 1)), alive_sources, table)
    left = left_factor(src)
    out = correlate(relative, left, whole, split, alive[None, :], inverse_table())
    return out.reshape(ROUNDS, SRC, LAGS, width)


def solution(mesh):
    return jax.shard_map(
        body,
        mesh=mesh,
        in_specs=(P(("groups", "chan"), None), P(("groups", "chan")), P()),
        out_specs=P("groups", None, None, "chan"),
        check_vma=False,
    )
```

```python
import functools
import math

import jax
import jax.numpy as jnp
import ml_dtypes
import numpy as np
from jax import lax
from jax.experimental import pallas as pl
from jax.experimental.pallas import tpu as pltpu
from jax.sharding import PartitionSpec as P

SEGMENT_LENGTH = 512
NF = 128
LAGS = 256
SRC = 16
ROUNDS = 2
SEGMENT_TALLY = 28

SOURCES = SRC * ROUNDS
BINS = 2 * NF
SUB = 8
TILES = NF // SUB
TEAM = 4
TEAM_WINDOWS = 7
STEP = 128
HELD = TEAM_WINDOWS * SEGMENT_LENGTH // TEAM
STRADDLE = HELD - SEGMENT_LENGTH
HALF = SEGMENT_LENGTH // 2
WHOLE = 16
SPLIT = 12
PACKED = 1024
SHARE = SOURCES // TEAM
DEPTH = 512
LARGE = 56 << 20


def angles(times):
    bins = np.arange(NF)[:, None] + 1
    turn = bins * times[None, :] % SEGMENT_LENGTH * (2.0 * np.pi / SEGMENT_LENGTH)
    table = np.stack([np.cos(turn), -np.sin(turn)])
    table = table.reshape(2, TILES, SUB, times.size).transpose(1, 0, 2, 3)
    return table.reshape(BINS, times.size)


def forward_table():
    table = angles(np.arange(SEGMENT_LENGTH)) / math.sqrt(SEGMENT_LENGTH)
    return jnp.asarray(table.astype(ml_dtypes.bfloat16))


def inverse_table():
    table = angles(np.arange(LAGS) - LAGS // 2)
    return jnp.asarray(np.ascontiguousarray(table.T).astype(ml_dtypes.bfloat16))


def position():
    me = lax.axis_index("chan")
    return me // TEAM, me % TEAM


def transform(table_ref, block):
    return jnp.dot(table_ref[...], block, preferred_element_type=jnp.float32).astype(jnp.bfloat16)


def free(size):
    return pl.CostEstimate(flops=0, bytes_accessed=0, transcendentals=0)


def window(data_ref, row, column, depth, width):
    row = pl.ds(pl.multiple_of(row, STEP), depth)
    return data_ref.at[row, pl.ds(pl.multiple_of(column, 128), width)]


def straddling(data_ref, j, place, column, width):
    row = jnp.where(j < place, j, j + SEGMENT_LENGTH // STEP) * STEP
    return window(data_ref, row, column * width, STEP, width)


def prepare_kernel(data_ref, table_ref, out_ref, block_ref, sems):
    _, place = position()
    planes, _, _, width = out_ref.shape
    copies = []
    for plane in range(planes):
        source = window(data_ref, place * STEP, plane * TEAM * width, SEGMENT_LENGTH, TEAM * width)
        copies.append(pltpu.make_async_copy(source, block_ref.at[plane], sems.at[plane]))
        copies[plane].start()
    for plane in range(planes):
        copies[plane].wait()
        for member in range(TEAM):
            column = pl.ds(pl.multiple_of((place ^ member) * width, width), width)
            out_ref[plane, member] = transform(table_ref, block_ref[plane, :, column])


def prepare(data, table, count):
    width = data.shape[1] // count
    planes = count // TEAM
    return pl.pallas_call(
        prepare_kernel,
        in_specs=[pl.BlockSpec(memory_space=pl.ANY), pl.BlockSpec(memory_space=pltpu.VMEM)],
        scratch_shapes=[
            pltpu.VMEM((planes, SEGMENT_LENGTH, TEAM * width), jnp.bfloat16),
            pltpu.SemaphoreType.DMA((planes,)),
        ],
        out_shape=jax.ShapeDtypeStruct((planes, TEAM, BINS, width), jnp.bfloat16),
        compiler_params=pltpu.CompilerParams(vmem_limit_bytes=LARGE),
        name="prepare",
    )(data, table)


def regroup_kernel(whole_ref, *out_refs):
    for member, out_ref in enumerate(out_refs, 1):
        out_ref[...] = whole_ref[:, member]


def regroup(whole):
    planes, _, rows, width = whole.shape
    return pl.pallas_call(
        regroup_kernel,
        out_shape=[jax.ShapeDtypeStruct((planes, rows, width), jnp.bfloat16)] * (TEAM - 1),
        compiler_params=pltpu.CompilerParams(vmem_limit_bytes=16 << 20),
        cost_estimate=free(1 << 20),
        name="regroup",
    )(whole)


def lend_kernel(data_ref, out_ref, sems):
    _, place = position()
    width = out_ref.shape[2]
    copies = []
    for target in range(out_ref.shape[0]):
        column = target // 2 * TEAM + target % 2 * 2 + 1 - place % 2
        for j in range(STRADDLE // STEP):
            source = straddling(data_ref, j, place, column, width)
            copy = pltpu.make_async_copy(source, out_ref.at[target, pl.ds(j * STEP, STEP)], sems.at[target, j])
            copy.start()
            copies.append(copy)
    for copy in copies:
        copy.wait()


def lend(data, count):
    width = data.shape[1] // count
    return pl.pallas_call(
        lend_kernel,
        in_specs=[pl.BlockSpec(memory_space=pl.ANY)],
        scratch_shapes=[pltpu.SemaphoreType.DMA((count // 2, STRADDLE // STEP))],
        out_shape=jax.ShapeDtypeStruct((count // 2, STRADDLE, width), jnp.bfloat16),
        compiler_params=pltpu.CompilerParams(vmem_limit_bytes=LARGE),
        cost_estimate=free(1 << 20),
        name="lend",
    )(data)


def halves_kernel(planes, data_ref, lent_ref, table_ref, keep_ref, give_ref, chip_ref, sems):
    mine, place = position()
    side, core = place // 2, place % 2
    width = keep_ref.shape[2]
    copies = []
    for i, k in enumerate(planes):
        plane = mine ^ k
        for t, target in enumerate((side, 1 - side)):
            for j in range(STRADDLE // STEP):
                source = straddling(data_ref, j, place, plane * TEAM + target * 2 + core, width)
                start = pl.multiple_of(core * STRADDLE + j * STEP, STEP)
                copies.append(pltpu.make_async_copy(source, chip_ref.at[i, t, pl.ds(start, STEP)], sems.at[i, t, j]))
            start = pl.multiple_of((1 - core) * STRADDLE, STEP)
            part = chip_ref.at[i, t, pl.ds(start, STRADDLE)]
            copies.append(pltpu.make_async_copy(lent_ref.at[plane * 2 + target], part, sems.at[i, t, STRADDLE // STEP]))
    for copy in copies:
        copy.start()
    for copy in copies:
        copy.wait()
    for i in range(len(planes)):
        for t, out_ref in enumerate((keep_ref, give_ref)):
            start = pl.multiple_of(side * HALF, HALF)
            out_ref[i, :BINS, :] = transform(table_ref, chip_ref[i, t, pl.ds(start, SEGMENT_LENGTH), :])
            start = pl.multiple_of((1 - side) * SEGMENT_LENGTH, HALF)
            out_ref[i, BINS:, :] = chip_ref[i, t, pl.ds(start, HALF), :]


def halves(planes, data, lent, table, count):
    width = data.shape[1] // count
    shape = jax.ShapeDtypeStruct((len(planes), BINS + HALF, width), jnp.bfloat16)
    return pl.pallas_call(
        functools.partial(halves_kernel, planes),
        in_specs=[
            pl.BlockSpec(memory_space=pl.ANY),
            pl.BlockSpec(memory_space=pl.ANY),
            pl.BlockSpec(memory_space=pltpu.VMEM),
        ],
        scratch_shapes=[
            pltpu.VMEM((len(planes), 2, 2 * STRADDLE, width), jnp.bfloat16),
            pltpu.SemaphoreType.DMA((len(planes), 2, STRADDLE // STEP + 1)),
        ],
        out_shape=[shape, shape],
        compiler_params=pltpu.CompilerParams(vmem_limit_bytes=LARGE),
        cost_estimate=free(1 << 20),
        name="halves",
    )(data, lent, table)


def straddle_kernel(keep_ref, got_ref, table_ref, *refs):
    out_refs, scratch_ref = refs[:-1], refs[-1]
    side = position()[1] // 2
    for k, out_ref in enumerate(out_refs):
        out_ref[2 * side] = keep_ref[k, :BINS, :]
        out_ref[2 - 2 * side] = got_ref[k, :BINS, :]
        scratch_ref[k, pl.ds(pl.multiple_of(side * HALF, HALF), HALF), :] = keep_ref[k, BINS:, :]
        scratch_ref[k, pl.ds(pl.multiple_of((1 - side) * HALF, HALF), HALF), :] = got_ref[k, BINS:, :]
        out_ref[1] = transform(table_ref, scratch_ref[k])


def straddle(keep, got, table):
    planes, _, width = keep.shape
    shape = jax.ShapeDtypeStruct((SPLIT // TEAM, BINS, width), jnp.bfloat16)
    return pl.pallas_call(
        straddle_kernel,
        out_shape=[shape] * planes,
        scratch_shapes=[pltpu.VMEM((planes, SEGMENT_LENGTH, width), jnp.bfloat16)],
        compiler_params=pltpu.CompilerParams(vmem_limit_bytes=16 << 20),
        cost_estimate=free(1 << 20),
        name="straddle",
    )(keep, got, table)


def pick_kernel(width, sources_ref, alive_ref, data_ref, *refs):
    out_refs, acc_ref, picked_ref = refs[:-2], refs[-2], refs[-1]
    step = pl.program_id(0)
    columns = data_ref.shape[1]
    lane = lax.broadcasted_iota(jnp.int32, (1, 128), 1)
    ids = jnp.full((1, 128), -1, jnp.int32)
    for q in range(SOURCES):
        ids = jnp.where(lane == q, sources_ref[q // SRC, q % SRC], ids)
    channel = lax.broadcasted_iota(jnp.int32, (columns, 128), 0)
    chosen = jnp.where(channel == ids - step * columns, 1.0, 0.0).astype(jnp.bfloat16)
    part = jnp.dot(data_ref[...], chosen, preferred_element_type=jnp.float32)

    @pl.when(step == 0)
    def _():
        acc_ref[...] = part

    @pl.when(step > 0)
    def _():
        acc_ref[...] += part

    @pl.when(step == pl.num_programs(0) - 1)
    def _():
        row = lax.broadcasted_iota(jnp.int32, (SOURCES, PACKED - HELD), 0)
        flags = jnp.zeros((SOURCES, PACKED - HELD), jnp.float32)
        for q in range(SOURCES):
            local = sources_ref[q // SRC, q % SRC] - lax.axis_index("chan") * width
            inside = (local >= 0) & (local < width)
            flag = jnp.where(inside, alive_ref[jnp.clip(local, 0, width - 1)], 0)
            flags = jnp.where(row == q, flag.astype(jnp.float32), flags)
        picked_ref[:, :HELD] = acc_ref[...].T[:SOURCES, :]
        picked_ref[:, HELD:] = flags
        for k, out_ref in enumerate(out_refs):
            start = pl.multiple_of((position()[1] ^ k) * SHARE, SHARE)
            out_ref[...] = picked_ref[pl.ds(start, SHARE), :].astype(jnp.bfloat16)


def pick(sources, alive, data, count):
    width = data.shape[1] // count
    columns = TEAM * width
    return pl.pallas_call(
        functools.partial(pick_kernel, width),
        grid=(count // TEAM,),
        in_specs=[
            pl.BlockSpec(memory_space=pltpu.SMEM),
            pl.BlockSpec(memory_space=pltpu.SMEM),
            pl.BlockSpec((HELD, columns), lambda i: (0, i)),
        ],
        out_specs=[pl.BlockSpec((SHARE, PACKED), lambda i: (0, 0))] * TEAM,
        scratch_shapes=[pltpu.VMEM((HELD, 128), jnp.float32), pltpu.VMEM((SOURCES, PACKED), jnp.float32)],
        out_shape=[jax.ShapeDtypeStruct((SHARE, PACKED), jnp.bfloat16)] * TEAM,
        compiler_params=pltpu.CompilerParams(vmem_limit_bytes=LARGE),
        cost_estimate=free(1 << 20),
        name="pick",
    )(sources, alive, data)


def sources_kernel(*refs):
    picked_refs, table_ref, out_ref, samples_ref = refs[:TEAM], refs[TEAM], refs[TEAM + 1], refs[TEAM + 2]
    place = position()[1]
    flags = jnp.zeros((SHARE, PACKED - HELD), jnp.float32)
    for k, picked_ref in enumerate(picked_refs):
        picked = picked_ref[...].astype(jnp.float32)
        flags += picked[:, HELD:]
        samples_ref[:, pl.ds(pl.multiple_of((place ^ k) * HELD, 128), HELD)] = picked[:, :HELD]
    samples = [samples_ref[:, w * SEGMENT_LENGTH : (w + 1) * SEGMENT_LENGTH] for w in range(TEAM_WINDOWS)]
    spectra = lax.dot_general(
        jnp.concatenate(samples, axis=0).astype(jnp.bfloat16),
        table_ref[...],
        (((1,), (1,)), ((), ())),
        preferred_element_type=jnp.float32,
    )
    flags = jnp.concatenate([flags] * (BINS // 128), axis=1)
    out_ref[...] = jnp.concatenate([spectra, flags], axis=0).astype(jnp.bfloat16)


def source_spectra(picked, table):
    return pl.pallas_call(
        sources_kernel,
        scratch_shapes=[pltpu.VMEM((SHARE, TEAM * HELD), jnp.float32)],
        out_shape=jax.ShapeDtypeStruct(((TEAM_WINDOWS + 1) * SHARE, BINS), jnp.bfloat16),
        cost_estimate=free(1 << 18),
        name="source_spectra",
    )(*picked, table)


def whiten_kernel(*refs):
    spectra_refs, out_ref, planes_ref = refs[:TEAM], refs[TEAM], refs[TEAM + 1]
    mine, _ = position()
    flags = jnp.zeros((SHARE, BINS), jnp.float32)
    for k, spectra_ref in enumerate(spectra_refs):
        spectra = spectra_ref[...].astype(jnp.float32)
        flags += spectra[TEAM_WINDOWS * SHARE :]
        planes_ref[mine ^ k] = spectra[: TEAM_WINDOWS * SHARE]
    spectra = planes_ref[...].reshape(SEGMENT_TALLY, SHARE, BINS)
    power = jnp.sum(jnp.square(spectra), axis=0)
    lane = lax.broadcasted_iota(jnp.int32, (SHARE, BINS), 1)
    other = jnp.where(lane % (2 * SUB) < SUB, pltpu.roll(power, BINS - SUB, 1), pltpu.roll(power, SUB, 1))
    level = (power + other) / SEGMENT_TALLY
    factor = flags / jnp.sqrt(level + 0.01)
    src = (spectra * factor[None]).astype(jnp.bfloat16).astype(jnp.float32)
    lane = lax.broadcasted_iota(jnp.int32, (SHARE, 128), 1) // (2 * SUB)
    each = 128 // (2 * SUB)
    for tile in range(TILES):
        half, at = divmod(tile, each)
        for group in range(DEPTH // 128):
            out = jnp.zeros((SHARE, 128), jnp.float32)
            for k in range(each):
                window = group * each + k
                if window < SEGMENT_TALLY:
                    piece = src[window, :, half * 128 : (half + 1) * 128]
                    shift = (k - at) * 2 * SUB % 128
                    piece = pltpu.roll(piece, shift, 1) if shift else piece
                    out = jnp.where(lane == k, piece, out)
            out_ref[tile, :, group * 128 : (group + 1) * 128] = out.astype(jnp.bfloat16)


def whiten(spectra):
    return pl.pallas_call(
        whiten_kernel,
        scratch_shapes=[pltpu.VMEM((TEAM, TEAM_WINDOWS * SHARE, BINS), jnp.float32)],
        out_shape=jax.ShapeDtypeStruct((TILES, SHARE, DEPTH), jnp.bfloat16),
        compiler_params=pltpu.CompilerParams(vmem_limit_bytes=16 << 20),
        cost_estimate=free(1 << 18),
        name="whiten",
    )(*spectra)


def left_kernel(*refs):
    src_refs, left_ref = refs[:-1], refs[-1]
    src = jnp.concatenate([ref[0].astype(jnp.float32) for ref in src_refs], axis=0)
    lane = lax.broadcasted_iota(jnp.int32, (SOURCES, DEPTH), 1)
    turned = jnp.where(lane % (2 * SUB) < SUB, -pltpu.roll(src, DEPTH - SUB, 1), pltpu.roll(src, SUB, 1))
    row = lax.broadcasted_iota(jnp.int32, (1, 2 * SUB, DEPTH), 1)
    lane = lax.broadcasted_iota(jnp.int32, (1, 2 * SUB, DEPTH), 2)
    both = jnp.where(row < SUB, src[:, None, :], turned[:, None, :])
    both = jnp.where(lane % SUB == row % SUB, both, 0.0)
    left_ref[0] = both.reshape(SOURCES * 2 * SUB, DEPTH).astype(jnp.bfloat16)


def left_factor(src):
    return pl.pallas_call(
        left_kernel,
        grid=(TILES,),
        in_specs=[pl.BlockSpec((1, SHARE, DEPTH), lambda i: (i, 0, 0))] * TEAM,
        out_specs=pl.BlockSpec((1, SOURCES * 2 * SUB, DEPTH), lambda i: (i, 0, 0)),
        out_shape=jax.ShapeDtypeStruct((TILES, SOURCES * 2 * SUB, DEPTH), jnp.bfloat16),
        compiler_params=pltpu.CompilerParams(vmem_limit_bytes=16 << 20),
        cost_estimate=pl.CostEstimate(flops=0, bytes_accessed=1 << 20, transcendentals=0),
        name="left",
    )(*src)


def whiten_all(samples, alive, table):
    samples = samples.reshape(SOURCES, SEGMENT_TALLY, SEGMENT_LENGTH)
    spectra = jnp.einsum("qwt,kt->qwk", samples, table, preferred_element_type=jnp.float32)
    power = jnp.mean(spectra**2, axis=1).reshape(SOURCES, TILES, 2, SUB)
    level = power[:, :, :1] + power[:, :, 1:]
    factor = alive[:, None, None, None] / jnp.sqrt(level + 0.01)
    factor = jnp.broadcast_to(factor, (SOURCES, TILES, 2, SUB)).reshape(SOURCES, BINS)
    src = (spectra * factor[:, None, :]).astype(jnp.bfloat16)
    src = jnp.transpose(src.reshape(SOURCES, SEGMENT_TALLY, TILES, 2 * SUB), (2, 0, 1, 3))
    src = src.reshape(TILES, SOURCES, SEGMENT_TALLY * 2 * SUB)
    src = jnp.pad(src, ((0, 0), (0, 0), (0, DEPTH - SEGMENT_TALLY * 2 * SUB)))
    return [src[:, k * SHARE : (k + 1) * SHARE] for k in range(TEAM)]


BATCH = 4


def correlate_kernel(relative, left_ref, whole_ref, *refs):
    other_refs, split_refs = refs[: TEAM - 1], refs[TEAM - 1 : 2 * TEAM - 1]
    alive_ref, inverse_ref, out_ref, right_ref, cross_ref, done_ref, sems = refs[2 * TEAM - 1 :]
    mine, place = position() if relative else (0, 0)
    width = right_ref.shape[2]
    rows = 2 * SUB
    span = TEAM_WINDOWS * rows
    pad = DEPTH - SEGMENT_TALLY * rows
    alive = alive_ref[...].astype(jnp.float32)

    @pl.loop(0, TILES // BATCH)
    def _(step):
        for k in range(BATCH):
            index = step * BATCH + k
            start = pl.multiple_of(index * rows, rows)
            tile = pl.ds(start, rows)
            right_ref[index, DEPTH - pad :, :] = jnp.zeros((pad, width), jnp.bfloat16)
            for plane in range(TEAM):
                for member in range(TEAM):
                    at = pl.multiple_of(plane * span + (member ^ place) * 2 * rows, rows)
                    piece = other_refs[member - 1][plane, tile, :] if member else whole_ref[plane, 0, tile, :]
                    right_ref[index, pl.ds(at, rows), :] = piece
                for j in range(SPLIT // TEAM):
                    at = pl.multiple_of((plane ^ mine) * span + (2 * j + 1) * rows, rows)
                    right_ref[index, pl.ds(at, rows), :] = split_refs[plane][j, tile, :]
            right = right_ref[index]
            power = jnp.square(right.astype(jnp.float32)).reshape(DEPTH // rows, rows, width)
            power = jnp.sum(power, axis=0)
            level = (power[:SUB] + power[SUB:]) / SEGMENT_TALLY
            factor = alive / jnp.sqrt(level + 0.01)
            factor = jnp.concatenate([factor, factor], axis=0)[None]
            cross = jnp.dot(left_ref[index], right, preferred_element_type=jnp.float32)
            cross = cross.reshape(SOURCES, rows, width)
            cross_ref[:, tile, :] = jnp.where(factor > 0.0, cross * factor, 0.0).astype(jnp.bfloat16)

    def copy(step):
        part = pl.ds(step * BATCH, BATCH)
        return pltpu.make_async_copy(done_ref.at[part], out_ref.at[part], sems.at[step])

    @pl.loop(0, SOURCES // BATCH)
    def _(step):
        for k in range(BATCH):
            index = step * BATCH + k
            held = (index // SHARE ^ place) * SHARE + index % SHARE
            lagged = jnp.dot(inverse_ref[...], cross_ref[held], preferred_element_type=jnp.float32)
            done_ref[index] = (lagged * (1.0 / math.sqrt(NF * SEGMENT_TALLY))).astype(jnp.bfloat16)
        copy(step).start()

    @pl.loop(0, SOURCES // BATCH)
    def _(step):
        copy(step).wait()


def correlate(relative, left, whole, others, split, alive, inverse):
    width = whole.shape[3]
    return pl.pallas_call(
        functools.partial(correlate_kernel, relative),
        out_specs=pl.BlockSpec(memory_space=pl.ANY),
        scratch_shapes=[
            pltpu.VMEM((TILES, DEPTH, width), jnp.bfloat16),
            pltpu.VMEM((SOURCES, BINS, width), jnp.bfloat16),
            pltpu.VMEM((SOURCES, LAGS, width), jnp.bfloat16),
            pltpu.SemaphoreType.DMA((SOURCES // BATCH,)),
        ],
        out_shape=jax.ShapeDtypeStruct((SOURCES, LAGS, width), jnp.bfloat16),
        compiler_params=pltpu.CompilerParams(vmem_limit_bytes=18 << 20),
        name="correlate",
    )(left, whole, *others, *split, alive, inverse)


def body(data, alive, sources):
    count = lax.axis_size("chan")
    width = data.shape[1] // count
    table = forward_table()
    relative = data.shape[0] == HELD and count == TEAM * TEAM
    if relative:
        swap = lambda x, k: lax.ppermute(x, "chan", [(i, i ^ k) for i in range(count)])
        team = range(1, TEAM)
        across = [[z * TEAM + p for z in range(count // TEAM)] for p in range(TEAM)]
        whole = prepare(data, table, count)
        data, whole = lax.optimization_barrier((data, whole))
        lent = lend(data, count)
        data, lent = lax.optimization_barrier((data, lent))
        lent = swap(lent, 1)
        whole = lax.all_to_all(whole, "chan", 0, 0, tiled=True, axis_index_groups=across)
        picked = pick(sources, alive, data, count)
        data, picked = lax.optimization_barrier((data, picked))
        picked = [picked[0]] + [swap(picked[k], k) for k in team]
        spectra = source_spectra(picked, table)
        keep_far, give_far = halves((2, 3), data, lent, table, count)
        give_far, spectra, data = lax.optimization_barrier((give_far, spectra, data))
        arrived = [swap(spectra, k * TEAM) for k in team]
        keep_near, give_near = halves((0, 1), data, lent, table, count)
        far = straddle(keep_far, swap(give_far, 2), table)
        arrived, whole, far = lax.optimization_barrier((arrived, whole, far))
        others = regroup(whole)
        src = whiten([spectra] + arrived)
        keep_near, src, others = lax.optimization_barrier((keep_near, src, others))
        others = [swap(others[k - 1], k) for k in team]
        near = straddle(keep_near, swap(give_near, 2), table)
        split = [near[0], swap(near[1], TEAM), swap(far[0], 2 * TEAM), swap(far[1], 3 * TEAM)]
        src = [src] + [swap(src, k) for k in team]
    else:
        me = lax.axis_index("chan")
        ids = sources.reshape(-1)
        near = ids[:, None] == me * width + jnp.arange(width, dtype=jnp.int32)[None, :]
        flags = jnp.sum(jnp.where(near, alive[None, :], 0), axis=1).astype(jnp.float32)
        chosen = jnp.where(jnp.arange(data.shape[1], dtype=jnp.int32)[:, None] == ids[None, :], 1.0, 0.0)
        picked = jnp.dot(data, chosen.astype(jnp.bfloat16), preferred_element_type=jnp.float32)
        picked = lax.all_gather(picked.astype(jnp.bfloat16), "chan", axis=0)
        alive_sources = lax.psum(flags, "chan")
        blocks = data.reshape(data.shape[0], count, width)
        blocks = lax.all_to_all(blocks, "chan", split_axis=1, concat_axis=0, tiled=True)
        blocks = blocks.reshape(SEGMENT_TALLY, SEGMENT_LENGTH, width)
        spectra = jnp.einsum("kt,wtc->wkc", table, blocks, preferred_element_type=jnp.float32)
        spectra = spectra.astype(jnp.bfloat16).reshape(TEAM, TEAM_WINDOWS, BINS, width)
        whole = spectra[:, 0:1]
        others = [spectra[:, 2 * k] for k in range(1, TEAM)]
        split = [spectra[z, 1::2] for z in range(TEAM)]
        src = whiten_all(jnp.transpose(picked, (2, 0, 1)), alive_sources, table)
    left = left_factor(src)
    out = correlate(relative, left, whole, others, split, alive[None, :], inverse_table())
    return out.reshape(ROUNDS, SRC, LAGS, width)


def solution(mesh):
    return jax.shard_map(
        body,
        mesh=mesh,
        in_specs=(P(("groups", "chan"), None), P(("groups", "chan")), P()),
        out_specs=P("groups", None, None, "chan"),
        check_vma=False,
    )
```

```python
import functools
import math

import jax
import jax.numpy as jnp
import ml_dtypes
import numpy as np
from jax import lax
from jax.experimental import pallas as pl
from jax.experimental.pallas import tpu as pltpu
from jax.sharding import PartitionSpec as P

SEGMENT_LENGTH = 512
NF = 128
LAGS = 256
SRC = 16
ROUNDS = 2
SEGMENT_TALLY = 28

SOURCES = SRC * ROUNDS
BINS = 2 * NF
SUB = 8
TILES = NF // SUB
TEAM = 4
TEAM_WINDOWS = 7
STEP = 128
HELD = TEAM_WINDOWS * SEGMENT_LENGTH // TEAM
STRADDLE = HELD - SEGMENT_LENGTH
HALF = SEGMENT_LENGTH // 2
WHOLE = 16
SPLIT = 12
PACKED = 1024
SHARE = SOURCES // TEAM
DEPTH = 512
LARGE = 56 << 20


def angles(times):
    bins = np.arange(NF)[:, None] + 1
    turn = bins * times[None, :] % SEGMENT_LENGTH * (2.0 * np.pi / SEGMENT_LENGTH)
    table = np.stack([np.cos(turn), -np.sin(turn)])
    table = table.reshape(2, TILES, SUB, times.size).transpose(1, 0, 2, 3)
    return table.reshape(BINS, times.size)


def forward_table():
    table = angles(np.arange(SEGMENT_LENGTH)) / math.sqrt(SEGMENT_LENGTH)
    return jnp.asarray(table.astype(ml_dtypes.bfloat16))


def inverse_table():
    table = angles(np.arange(LAGS) - LAGS // 2)
    return jnp.asarray(np.ascontiguousarray(table.T).astype(ml_dtypes.bfloat16))


def position():
    me = lax.axis_index("chan")
    return me // TEAM, me % TEAM


def transform(table_ref, block):
    return jnp.dot(table_ref[...], block, preferred_element_type=jnp.float32).astype(jnp.bfloat16)


def free(size):
    return pl.CostEstimate(flops=0, bytes_accessed=0, transcendentals=0)


def window(data_ref, row, column, depth, width):
    row = pl.ds(pl.multiple_of(row, STEP), depth)
    return data_ref.at[row, pl.ds(pl.multiple_of(column, 128), width)]


def straddling(data_ref, j, place, column, width):
    row = jnp.where(j < place, j, j + SEGMENT_LENGTH // STEP) * STEP
    return window(data_ref, row, column * width, STEP, width)


def prepare_kernel(data_ref, table_ref, whole_ref, block_ref, out_ref, in_sems, out_sems):
    _, place = position()
    planes, _, _, width = out_ref.shape
    copies = []
    for plane in range(planes):
        source = window(data_ref, place * STEP, plane * TEAM * width, SEGMENT_LENGTH, TEAM * width)
        copies.append(pltpu.make_async_copy(source, block_ref.at[plane], in_sems.at[plane]))
        copies[plane].start()
    for plane in range(planes):
        copies[plane].wait()
        for member in range(TEAM):
            column = pl.ds(pl.multiple_of((place ^ member) * width, width), width)
            out_ref[plane, member] = transform(table_ref, block_ref[plane, :, column])
        copies.append(pltpu.make_async_copy(out_ref.at[plane], whole_ref.at[plane], out_sems.at[plane]))
        copies[-1].start()
    for copy in copies[planes:]:
        copy.wait()


def prepare(data, table, count):
    width = data.shape[1] // count
    planes = count // TEAM
    return pl.pallas_call(
        prepare_kernel,
        in_specs=[pl.BlockSpec(memory_space=pl.ANY), pl.BlockSpec(memory_space=pltpu.VMEM)],
        scratch_shapes=[
            pltpu.VMEM((planes, SEGMENT_LENGTH, TEAM * width), jnp.bfloat16),
            pltpu.VMEM((planes, TEAM, BINS, width), jnp.bfloat16),
            pltpu.SemaphoreType.DMA((planes,)),
            pltpu.SemaphoreType.DMA((planes,)),
        ],
        out_specs=pl.BlockSpec(memory_space=pl.ANY),
        out_shape=jax.ShapeDtypeStruct((planes, TEAM, BINS, width), jnp.bfloat16),
        compiler_params=pltpu.CompilerParams(vmem_limit_bytes=LARGE),
        name="prepare",
    )(data, table)


def regroup_kernel(whole_ref, *out_refs):
    for member, out_ref in enumerate(out_refs, 1):
        out_ref[...] = whole_ref[:, member]


def regroup(whole):
    planes, _, rows, width = whole.shape
    return pl.pallas_call(
        regroup_kernel,
        out_shape=[jax.ShapeDtypeStruct((planes, rows, width), jnp.bfloat16)] * (TEAM - 1),
        compiler_params=pltpu.CompilerParams(vmem_limit_bytes=16 << 20),
        cost_estimate=free(1 << 20),
        name="regroup",
    )(whole)


def lend_kernel(data_ref, out_ref, sems):
    _, place = position()
    width = out_ref.shape[2]
    copies = []
    for target in range(out_ref.shape[0]):
        column = target // 2 * TEAM + target % 2 * 2 + 1 - place % 2
        for j in range(STRADDLE // STEP):
            source = straddling(data_ref, j, place, column, width)
            copy = pltpu.make_async_copy(source, out_ref.at[target, pl.ds(j * STEP, STEP)], sems.at[target, j])
            copy.start()
            copies.append(copy)
    for copy in copies:
        copy.wait()


def lend(data, count):
    width = data.shape[1] // count
    return pl.pallas_call(
        lend_kernel,
        in_specs=[pl.BlockSpec(memory_space=pl.ANY)],
        scratch_shapes=[pltpu.SemaphoreType.DMA((count // 2, STRADDLE // STEP))],
        out_shape=jax.ShapeDtypeStruct((count // 2, STRADDLE, width), jnp.bfloat16),
        compiler_params=pltpu.CompilerParams(vmem_limit_bytes=LARGE),
        cost_estimate=free(1 << 20),
        name="lend",
    )(data)


def halves_kernel(planes, data_ref, lent_ref, table_ref, keep_ref, give_ref, chip_ref, sems):
    mine, place = position()
    side, core = place // 2, place % 2
    width = keep_ref.shape[2]
    copies = []
    for i, k in enumerate(planes):
        plane = mine ^ k
        for t, target in enumerate((side, 1 - side)):
            for j in range(STRADDLE // STEP):
                source = straddling(data_ref, j, place, plane * TEAM + target * 2 + core, width)
                start = pl.multiple_of(core * STRADDLE + j * STEP, STEP)
                copies.append(pltpu.make_async_copy(source, chip_ref.at[i, t, pl.ds(start, STEP)], sems.at[i, t, j]))
            start = pl.multiple_of((1 - core) * STRADDLE, STEP)
            part = chip_ref.at[i, t, pl.ds(start, STRADDLE)]
            copies.append(pltpu.make_async_copy(lent_ref.at[plane * 2 + target], part, sems.at[i, t, STRADDLE // STEP]))
    for copy in copies:
        copy.start()
    for copy in copies:
        copy.wait()
    for i in range(len(planes)):
        for t, out_ref in enumerate((keep_ref, give_ref)):
            start = pl.multiple_of(side * HALF, HALF)
            out_ref[i, :BINS, :] = transform(table_ref, chip_ref[i, t, pl.ds(start, SEGMENT_LENGTH), :])
            start = pl.multiple_of((1 - side) * SEGMENT_LENGTH, HALF)
            out_ref[i, BINS:, :] = chip_ref[i, t, pl.ds(start, HALF), :]


def halves(planes, data, lent, table, count):
    width = data.shape[1] // count
    shape = jax.ShapeDtypeStruct((len(planes), BINS + HALF, width), jnp.bfloat16)
    return pl.pallas_call(
        functools.partial(halves_kernel, planes),
        in_specs=[
            pl.BlockSpec(memory_space=pl.ANY),
            pl.BlockSpec(memory_space=pl.ANY),
            pl.BlockSpec(memory_space=pltpu.VMEM),
        ],
        scratch_shapes=[
            pltpu.VMEM((len(planes), 2, 2 * STRADDLE, width), jnp.bfloat16),
            pltpu.SemaphoreType.DMA((len(planes), 2, STRADDLE // STEP + 1)),
        ],
        out_shape=[shape, shape],
        compiler_params=pltpu.CompilerParams(vmem_limit_bytes=LARGE),
        cost_estimate=free(1 << 20),
        name="halves",
    )(data, lent, table)


def straddle_kernel(keep_ref, got_ref, table_ref, *refs):
    out_refs, scratch_ref = refs[:-1], refs[-1]
    side = position()[1] // 2
    for k, out_ref in enumerate(out_refs):
        out_ref[2 * side] = keep_ref[k, :BINS, :]
        out_ref[2 - 2 * side] = got_ref[k, :BINS, :]
        scratch_ref[k, pl.ds(pl.multiple_of(side * HALF, HALF), HALF), :] = keep_ref[k, BINS:, :]
        scratch_ref[k, pl.ds(pl.multiple_of((1 - side) * HALF, HALF), HALF), :] = got_ref[k, BINS:, :]
        out_ref[1] = transform(table_ref, scratch_ref[k])


def straddle(keep, got, table):
    planes, _, width = keep.shape
    shape = jax.ShapeDtypeStruct((SPLIT // TEAM, BINS, width), jnp.bfloat16)
    return pl.pallas_call(
        straddle_kernel,
        out_shape=[shape] * planes,
        scratch_shapes=[pltpu.VMEM((planes, SEGMENT_LENGTH, width), jnp.bfloat16)],
        compiler_params=pltpu.CompilerParams(vmem_limit_bytes=16 << 20),
        cost_estimate=free(1 << 20),
        name="straddle",
    )(keep, got, table)


def pick_kernel(width, sources_ref, alive_ref, data_ref, *refs):
    out_refs, acc_ref, picked_ref = refs[:-2], refs[-2], refs[-1]
    step = pl.program_id(0)
    columns = data_ref.shape[1]
    lane = lax.broadcasted_iota(jnp.int32, (1, 128), 1)
    ids = jnp.full((1, 128), -1, jnp.int32)
    for q in range(SOURCES):
        ids = jnp.where(lane == q, sources_ref[q // SRC, q % SRC], ids)
    channel = lax.broadcasted_iota(jnp.int32, (columns, 128), 0)
    chosen = jnp.where(channel == ids - step * columns, 1.0, 0.0).astype(jnp.bfloat16)
    part = jnp.dot(data_ref[...], chosen, preferred_element_type=jnp.float32)

    @pl.when(step == 0)
    def _():
        acc_ref[...] = part

    @pl.when(step > 0)
    def _():
        acc_ref[...] += part

    @pl.when(step == pl.num_programs(0) - 1)
    def _():
        row = lax.broadcasted_iota(jnp.int32, (SOURCES, PACKED - HELD), 0)
        flags = jnp.zeros((SOURCES, PACKED - HELD), jnp.float32)
        for q in range(SOURCES):
            local = sources_ref[q // SRC, q % SRC] - lax.axis_index("chan") * width
            inside = (local >= 0) & (local < width)
            flag = jnp.where(inside, alive_ref[jnp.clip(local, 0, width - 1)], 0)
            flags = jnp.where(row == q, flag.astype(jnp.float32), flags)
        picked_ref[:, :HELD] = acc_ref[...].T[:SOURCES, :]
        picked_ref[:, HELD:] = flags
        for k, out_ref in enumerate(out_refs):
            start = pl.multiple_of((position()[1] ^ k) * SHARE, SHARE)
            out_ref[...] = picked_ref[pl.ds(start, SHARE), :].astype(jnp.bfloat16)


def pick(sources, alive, data, count):
    width = data.shape[1] // count
    columns = TEAM * width
    return pl.pallas_call(
        functools.partial(pick_kernel, width),
        grid=(count // TEAM,),
        in_specs=[
            pl.BlockSpec(memory_space=pltpu.SMEM),
            pl.BlockSpec(memory_space=pltpu.SMEM),
            pl.BlockSpec((HELD, columns), lambda i: (0, i)),
        ],
        out_specs=[pl.BlockSpec((SHARE, PACKED), lambda i: (0, 0))] * TEAM,
        scratch_shapes=[pltpu.VMEM((HELD, 128), jnp.float32), pltpu.VMEM((SOURCES, PACKED), jnp.float32)],
        out_shape=[jax.ShapeDtypeStruct((SHARE, PACKED), jnp.bfloat16)] * TEAM,
        compiler_params=pltpu.CompilerParams(vmem_limit_bytes=LARGE),
        cost_estimate=free(1 << 20),
        name="pick",
    )(sources, alive, data)


def sources_kernel(*refs):
    picked_refs, table_ref, out_ref, samples_ref = refs[:TEAM], refs[TEAM], refs[TEAM + 1], refs[TEAM + 2]
    place = position()[1]
    flags = jnp.zeros((SHARE, PACKED - HELD), jnp.float32)
    for k, picked_ref in enumerate(picked_refs):
        picked = picked_ref[...].astype(jnp.float32)
        flags += picked[:, HELD:]
        samples_ref[:, pl.ds(pl.multiple_of((place ^ k) * HELD, 128), HELD)] = picked[:, :HELD]
    samples = [samples_ref[:, w * SEGMENT_LENGTH : (w + 1) * SEGMENT_LENGTH] for w in range(TEAM_WINDOWS)]
    spectra = lax.dot_general(
        jnp.concatenate(samples, axis=0).astype(jnp.bfloat16),
        table_ref[...],
        (((1,), (1,)), ((), ())),
        preferred_element_type=jnp.float32,
    )
    flags = jnp.concatenate([flags] * (BINS // 128), axis=1)
    out_ref[...] = jnp.concatenate([spectra, flags], axis=0).astype(jnp.bfloat16)


def source_spectra(picked, table):
    return pl.pallas_call(
        sources_kernel,
        scratch_shapes=[pltpu.VMEM((SHARE, TEAM * HELD), jnp.float32)],
        out_shape=jax.ShapeDtypeStruct(((TEAM_WINDOWS + 1) * SHARE, BINS), jnp.bfloat16),
        cost_estimate=free(1 << 18),
        name="source_spectra",
    )(*picked, table)


def whiten_kernel(*refs):
    spectra_refs, out_ref, planes_ref = refs[:TEAM], refs[TEAM], refs[TEAM + 1]
    mine, _ = position()
    flags = jnp.zeros((SHARE, BINS), jnp.float32)
    for k, spectra_ref in enumerate(spectra_refs):
        spectra = spectra_ref[...].astype(jnp.float32)
        flags += spectra[TEAM_WINDOWS * SHARE :]
        planes_ref[mine ^ k] = spectra[: TEAM_WINDOWS * SHARE]
    spectra = planes_ref[...].reshape(SEGMENT_TALLY, SHARE, BINS)
    power = jnp.sum(jnp.square(spectra), axis=0)
    lane = lax.broadcasted_iota(jnp.int32, (SHARE, BINS), 1)
    other = jnp.where(lane % (2 * SUB) < SUB, pltpu.roll(power, BINS - SUB, 1), pltpu.roll(power, SUB, 1))
    level = (power + other) / SEGMENT_TALLY
    factor = flags / jnp.sqrt(level + 0.01)
    src = (spectra * factor[None]).astype(jnp.bfloat16).astype(jnp.float32)
    lane = lax.broadcasted_iota(jnp.int32, (SHARE, 128), 1) // (2 * SUB)
    each = 128 // (2 * SUB)
    for tile in range(TILES):
        half, at = divmod(tile, each)
        for group in range(DEPTH // 128):
            out = jnp.zeros((SHARE, 128), jnp.float32)
            for k in range(each):
                window = group * each + k
                if window < SEGMENT_TALLY:
                    piece = src[window, :, half * 128 : (half + 1) * 128]
                    shift = (k - at) * 2 * SUB % 128
                    piece = pltpu.roll(piece, shift, 1) if shift else piece
                    out = jnp.where(lane == k, piece, out)
            out_ref[tile, :, group * 128 : (group + 1) * 128] = out.astype(jnp.bfloat16)


def whiten(spectra):
    return pl.pallas_call(
        whiten_kernel,
        scratch_shapes=[pltpu.VMEM((TEAM, TEAM_WINDOWS * SHARE, BINS), jnp.float32)],
        out_shape=jax.ShapeDtypeStruct((TILES, SHARE, DEPTH), jnp.bfloat16),
        compiler_params=pltpu.CompilerParams(vmem_limit_bytes=16 << 20),
        cost_estimate=free(1 << 18),
        name="whiten",
    )(*spectra)


def left_kernel(*refs):
    src_refs, left_ref = refs[:-1], refs[-1]
    src = jnp.concatenate([ref[0].astype(jnp.float32) for ref in src_refs], axis=0)
    lane = lax.broadcasted_iota(jnp.int32, (SOURCES, DEPTH), 1)
    turned = jnp.where(lane % (2 * SUB) < SUB, -pltpu.roll(src, DEPTH - SUB, 1), pltpu.roll(src, SUB, 1))
    row = lax.broadcasted_iota(jnp.int32, (1, 2 * SUB, DEPTH), 1)
    lane = lax.broadcasted_iota(jnp.int32, (1, 2 * SUB, DEPTH), 2)
    both = jnp.where(row < SUB, src[:, None, :], turned[:, None, :])
    both = jnp.where(lane % SUB == row % SUB, both, 0.0)
    left_ref[0] = both.reshape(SOURCES * 2 * SUB, DEPTH).astype(jnp.bfloat16)


def left_factor(src):
    return pl.pallas_call(
        left_kernel,
        grid=(TILES,),
        in_specs=[pl.BlockSpec((1, SHARE, DEPTH), lambda i: (i, 0, 0))] * TEAM,
        out_specs=pl.BlockSpec((1, SOURCES * 2 * SUB, DEPTH), lambda i: (i, 0, 0)),
        out_shape=jax.ShapeDtypeStruct((TILES, SOURCES * 2 * SUB, DEPTH), jnp.bfloat16),
        compiler_params=pltpu.CompilerParams(vmem_limit_bytes=16 << 20),
        cost_estimate=pl.CostEstimate(flops=0, bytes_accessed=1 << 20, transcendentals=0),
        name="left",
    )(*src)


def whiten_all(samples, alive, table):
    samples = samples.reshape(SOURCES, SEGMENT_TALLY, SEGMENT_LENGTH)
    spectra = jnp.einsum("qwt,kt->qwk", samples, table, preferred_element_type=jnp.float32)
    power = jnp.mean(spectra**2, axis=1).reshape(SOURCES, TILES, 2, SUB)
    level = power[:, :, :1] + power[:, :, 1:]
    factor = alive[:, None, None, None] / jnp.sqrt(level + 0.01)
    factor = jnp.broadcast_to(factor, (SOURCES, TILES, 2, SUB)).reshape(SOURCES, BINS)
    src = (spectra * factor[:, None, :]).astype(jnp.bfloat16)
    src = jnp.transpose(src.reshape(SOURCES, SEGMENT_TALLY, TILES, 2 * SUB), (2, 0, 1, 3))
    src = src.reshape(TILES, SOURCES, SEGMENT_TALLY * 2 * SUB)
    src = jnp.pad(src, ((0, 0), (0, 0), (0, DEPTH - SEGMENT_TALLY * 2 * SUB)))
    return [src[:, k * SHARE : (k + 1) * SHARE] for k in range(TEAM)]


BATCH = 8


def correlate_kernel(relative, left_ref, whole_ref, *refs):
    other_refs, split_refs = refs[: TEAM - 1], refs[TEAM - 1 : 2 * TEAM - 1]
    alive_ref, inverse_ref, out_ref, right_ref, cross_ref, done_ref, sems = refs[2 * TEAM - 1 :]
    mine, place = position() if relative else (0, 0)
    width = right_ref.shape[2]
    rows = 2 * SUB
    span = TEAM_WINDOWS * rows
    pad = DEPTH - SEGMENT_TALLY * rows
    alive = alive_ref[...].astype(jnp.float32)

    for index in range(TILES):
        tile = slice(index * rows, (index + 1) * rows)
        right_ref[index, DEPTH - pad :, :] = jnp.zeros((pad, width), jnp.bfloat16)
        for plane in range(TEAM):
            for member in range(TEAM):
                at = pl.multiple_of(plane * span + (member ^ place) * 2 * rows, rows)
                piece = other_refs[member - 1][plane, tile, :] if member else whole_ref[plane, 0, tile, :]
                right_ref[index, pl.ds(at, rows), :] = piece
            for j in range(SPLIT // TEAM):
                at = pl.multiple_of((plane ^ mine) * span + (2 * j + 1) * rows, rows)
                right_ref[index, pl.ds(at, rows), :] = split_refs[plane][j, tile, :]
        right = right_ref[index]
        power = jnp.square(right.astype(jnp.float32)).reshape(DEPTH // rows, rows, width)
        power = jnp.sum(power, axis=0)
        level = (power[:SUB] + power[SUB:]) / SEGMENT_TALLY
        factor = alive / jnp.sqrt(level + 0.01)
        factor = jnp.concatenate([factor, factor], axis=0)[None]
        cross = jnp.dot(left_ref[index], right, preferred_element_type=jnp.float32)
        cross = cross.reshape(SOURCES, rows, width)
        cross_ref[:, tile, :] = jnp.where(factor > 0.0, cross * factor, 0.0).astype(jnp.bfloat16)

    def copy(step):
        part = pl.ds(step * BATCH, BATCH)
        return pltpu.make_async_copy(done_ref.at[part], out_ref.at[part], sems.at[step])

    @pl.loop(0, SOURCES // BATCH)
    def _(step):
        for k in range(BATCH):
            index = step * BATCH + k
            held = (index // SHARE ^ place) * SHARE + index % SHARE
            lagged = jnp.dot(inverse_ref[...], cross_ref[held], preferred_element_type=jnp.float32)
            done_ref[index] = (lagged * (1.0 / math.sqrt(NF * SEGMENT_TALLY))).astype(jnp.bfloat16)
        copy(step).start()

    @pl.loop(0, SOURCES // BATCH)
    def _(step):
        copy(step).wait()


def correlate(relative, left, whole, others, split, alive, inverse):
    width = whole.shape[3]
    return pl.pallas_call(
        functools.partial(correlate_kernel, relative),
        out_specs=pl.BlockSpec(memory_space=pl.ANY),
        scratch_shapes=[
            pltpu.VMEM((TILES, DEPTH, width), jnp.bfloat16),
            pltpu.VMEM((SOURCES, BINS, width), jnp.bfloat16),
            pltpu.VMEM((SOURCES, LAGS, width), jnp.bfloat16),
            pltpu.SemaphoreType.DMA((SOURCES // BATCH,)),
        ],
        out_shape=jax.ShapeDtypeStruct((SOURCES, LAGS, width), jnp.bfloat16),
        compiler_params=pltpu.CompilerParams(vmem_limit_bytes=18 << 20),
        name="correlate",
    )(left, whole, *others, *split, alive, inverse)


def body(data, alive, sources):
    count = lax.axis_size("chan")
    width = data.shape[1] // count
    table = forward_table()
    relative = data.shape[0] == HELD and count == TEAM * TEAM
    if relative:
        swap = lambda x, k: lax.ppermute(x, "chan", [(i, i ^ k) for i in range(count)])
        team = range(1, TEAM)
        across = [[z * TEAM + p for z in range(count // TEAM)] for p in range(TEAM)]
        whole = prepare(data, table, count)
        data, whole = lax.optimization_barrier((data, whole))
        lent = lend(data, count)
        data, lent = lax.optimization_barrier((data, lent))
        lent = swap(lent, 1)
        whole = lax.all_to_all(whole, "chan", 0, 0, tiled=True, axis_index_groups=across)
        picked = pick(sources, alive, data, count)
        data, picked = lax.optimization_barrier((data, picked))
        picked = [picked[0]] + [swap(picked[k], k) for k in team]
        spectra = source_spectra(picked, table)
        keep_far, give_far = halves((2, 3), data, lent, table, count)
        give_far, spectra, data = lax.optimization_barrier((give_far, spectra, data))
        arrived = [swap(spectra, k * TEAM) for k in team]
        keep_near, give_near = halves((0, 1), data, lent, table, count)
        far = straddle(keep_far, swap(give_far, 2), table)
        arrived, whole, far = lax.optimization_barrier((arrived, whole, far))
        others = regroup(whole)
        src = whiten([spectra] + arrived)
        keep_near, src, others = lax.optimization_barrier((keep_near, src, others))
        others = [swap(others[k - 1], k) for k in team]
        near = straddle(keep_near, swap(give_near, 2), table)
        split = [near[0], swap(near[1], TEAM), swap(far[0], 2 * TEAM), swap(far[1], 3 * TEAM)]
        src = [src] + [swap(src, k) for k in team]
    else:
        me = lax.axis_index("chan")
        ids = sources.reshape(-1)
        near = ids[:, None] == me * width + jnp.arange(width, dtype=jnp.int32)[None, :]
        flags = jnp.sum(jnp.where(near, alive[None, :], 0), axis=1).astype(jnp.float32)
        chosen = jnp.where(jnp.arange(data.shape[1], dtype=jnp.int32)[:, None] == ids[None, :], 1.0, 0.0)
        picked = jnp.dot(data, chosen.astype(jnp.bfloat16), preferred_element_type=jnp.float32)
        picked = lax.all_gather(picked.astype(jnp.bfloat16), "chan", axis=0)
        alive_sources = lax.psum(flags, "chan")
        blocks = data.reshape(data.shape[0], count, width)
        blocks = lax.all_to_all(blocks, "chan", split_axis=1, concat_axis=0, tiled=True)
        blocks = blocks.reshape(SEGMENT_TALLY, SEGMENT_LENGTH, width)
        spectra = jnp.einsum("kt,wtc->wkc", table, blocks, preferred_element_type=jnp.float32)
        spectra = spectra.astype(jnp.bfloat16).reshape(TEAM, TEAM_WINDOWS, BINS, width)
        whole = spectra[:, 0:1]
        others = [spectra[:, 2 * k] for k in range(1, TEAM)]
        split = [spectra[z, 1::2] for z in range(TEAM)]
        src = whiten_all(jnp.transpose(picked, (2, 0, 1)), alive_sources, table)
    left = left_factor(src)
    out = correlate(relative, left, whole, others, split, alive[None, :], inverse_table())
    return out.reshape(ROUNDS, SRC, LAGS, width)


def solution(mesh):
    return jax.shard_map(
        body,
        mesh=mesh,
        in_specs=(P(("groups", "chan"), None), P(("groups", "chan")), P()),
        out_specs=P("groups", None, None, "chan"),
        check_vma=False,
    )
```

```python
import functools
import math

import jax
import jax.numpy as jnp
import ml_dtypes
import numpy as np
from jax import lax
from jax.experimental import pallas as pl
from jax.experimental.pallas import tpu as pltpu
from jax.sharding import PartitionSpec as P

SEGMENT_LENGTH = 512
NF = 128
LAGS = 256
SRC = 16
ROUNDS = 2
SEGMENT_TALLY = 28

SOURCES = SRC * ROUNDS
BINS = 2 * NF
SUB = 8
TILES = NF // SUB
TEAM = 4
TEAM_WINDOWS = 7
STEP = 128
HELD = TEAM_WINDOWS * SEGMENT_LENGTH // TEAM
STRADDLE = HELD - SEGMENT_LENGTH
HALF = SEGMENT_LENGTH // 2
WHOLE = 16
SPLIT = 12
PACKED = 1024
SHARE = SOURCES // TEAM
DEPTH = 512
LARGE = 56 << 20


def angles(times):
    bins = np.arange(NF)[:, None] + 1
    turn = bins * times[None, :] % SEGMENT_LENGTH * (2.0 * np.pi / SEGMENT_LENGTH)
    table = np.stack([np.cos(turn), -np.sin(turn)])
    table = table.reshape(2, TILES, SUB, times.size).transpose(1, 0, 2, 3)
    return table.reshape(BINS, times.size)


def forward_table():
    table = angles(np.arange(SEGMENT_LENGTH)) / math.sqrt(SEGMENT_LENGTH)
    return jnp.asarray(table.astype(ml_dtypes.bfloat16))


def inverse_table():
    table = angles(np.arange(LAGS) - LAGS // 2)
    return jnp.asarray(np.ascontiguousarray(table.T).astype(ml_dtypes.bfloat16))


def position():
    me = lax.axis_index("chan")
    return me // TEAM, me % TEAM


def transform(table_ref, block):
    return jnp.dot(table_ref[...], block, preferred_element_type=jnp.float32).astype(jnp.bfloat16)


def free():
    return pl.CostEstimate(flops=0, bytes_accessed=0, transcendentals=0)


def window(data_ref, row, column, depth, width):
    row = pl.ds(pl.multiple_of(row, STEP), depth)
    return data_ref.at[row, pl.ds(pl.multiple_of(column, 128), width)]


def straddling(data_ref, j, place, column, width):
    row = jnp.where(j < place, j, j + SEGMENT_LENGTH // STEP) * STEP
    return window(data_ref, row, column * width, STEP, width)


def prepare_kernel(data_ref, table_ref, whole_ref, block_ref, out_ref, in_sems, out_sems):
    _, place = position()
    planes, width = out_ref.shape[0] // 2, out_ref.shape[3]
    copies = []
    for plane in range(planes):
        source = window(data_ref, place * STEP, plane * TEAM * width, SEGMENT_LENGTH, TEAM * width)
        copies.append(pltpu.make_async_copy(source, block_ref.at[plane], in_sems.at[plane]))
        copies[plane].start()
    for plane in range(planes):
        copies[plane].wait()
        for core in range(2):
            for turn in range(2):
                column = pl.ds(pl.multiple_of(((place // 2 ^ turn) * 2 + core) * width, width), width)
                out_ref[plane * 2 + core, turn] = transform(table_ref, block_ref[plane, :, column])
        part = pl.ds(plane * 2, 2)
        copies.append(pltpu.make_async_copy(out_ref.at[part], whole_ref.at[part], out_sems.at[plane]))
        copies[-1].start()
    for copy in copies[planes:]:
        copy.wait()


def prepare(data, table, count):
    width = data.shape[1] // count
    planes = count // TEAM
    return pl.pallas_call(
        prepare_kernel,
        in_specs=[pl.BlockSpec(memory_space=pl.ANY), pl.BlockSpec(memory_space=pltpu.VMEM)],
        scratch_shapes=[
            pltpu.VMEM((planes, SEGMENT_LENGTH, TEAM * width), jnp.bfloat16),
            pltpu.VMEM((planes * 2, 2, BINS, width), jnp.bfloat16),
            pltpu.SemaphoreType.DMA((planes,)),
            pltpu.SemaphoreType.DMA((planes,)),
        ],
        out_specs=pl.BlockSpec(memory_space=pl.ANY),
        out_shape=jax.ShapeDtypeStruct((planes * 2, 2, BINS, width), jnp.bfloat16),
        compiler_params=pltpu.CompilerParams(vmem_limit_bytes=LARGE),
        name="prepare",
    )(data, table)


def regroup_kernel(whole_ref, out_ref):
    out_ref[...] = whole_ref[:, 1]


def regroup(whole):
    held, _, rows, width = whole.shape
    return pl.pallas_call(
        regroup_kernel,
        out_shape=jax.ShapeDtypeStruct((held, rows, width), jnp.bfloat16),
        compiler_params=pltpu.CompilerParams(vmem_limit_bytes=16 << 20),
        cost_estimate=free(),
        name="regroup",
    )(whole)


def lend_kernel(data_ref, out_ref, sems):
    _, place = position()
    width = out_ref.shape[2]
    copies = []
    for target in range(out_ref.shape[0]):
        column = target // 2 * TEAM + target % 2 * 2 + 1 - place % 2
        for j in range(STRADDLE // STEP):
            source = straddling(data_ref, j, place, column, width)
            copy = pltpu.make_async_copy(source, out_ref.at[target, pl.ds(j * STEP, STEP)], sems.at[target, j])
            copy.start()
            copies.append(copy)
    for copy in copies:
        copy.wait()


def lend(data, count):
    width = data.shape[1] // count
    return pl.pallas_call(
        lend_kernel,
        in_specs=[pl.BlockSpec(memory_space=pl.ANY)],
        scratch_shapes=[pltpu.SemaphoreType.DMA((count // 2, STRADDLE // STEP))],
        out_shape=jax.ShapeDtypeStruct((count // 2, STRADDLE, width), jnp.bfloat16),
        compiler_params=pltpu.CompilerParams(vmem_limit_bytes=LARGE),
        cost_estimate=free(),
        name="lend",
    )(data)


def halves_kernel(planes, data_ref, lent_ref, table_ref, keep_ref, give_ref, chip_ref, sems):
    mine, place = position()
    side, core = place // 2, place % 2
    width = keep_ref.shape[2]
    copies = []
    for i, k in enumerate(planes):
        plane = mine ^ k
        for t, target in enumerate((side, 1 - side)):
            for j in range(STRADDLE // STEP):
                source = straddling(data_ref, j, place, plane * TEAM + target * 2 + core, width)
                start = pl.multiple_of(core * STRADDLE + j * STEP, STEP)
                copies.append(pltpu.make_async_copy(source, chip_ref.at[i, t, pl.ds(start, STEP)], sems.at[i, t, j]))
            start = pl.multiple_of((1 - core) * STRADDLE, STEP)
            part = chip_ref.at[i, t, pl.ds(start, STRADDLE)]
            copies.append(pltpu.make_async_copy(lent_ref.at[plane * 2 + target], part, sems.at[i, t, STRADDLE // STEP]))
    for copy in copies:
        copy.start()
    for copy in copies:
        copy.wait()
    for i in range(len(planes)):
        for t, out_ref in enumerate((keep_ref, give_ref)):
            start = pl.multiple_of(side * HALF, HALF)
            out_ref[i, :BINS, :] = transform(table_ref, chip_ref[i, t, pl.ds(start, SEGMENT_LENGTH), :])
            start = pl.multiple_of((1 - side) * SEGMENT_LENGTH, HALF)
            out_ref[i, BINS:, :] = chip_ref[i, t, pl.ds(start, HALF), :]


def halves(planes, data, lent, table, count):
    width = data.shape[1] // count
    shape = jax.ShapeDtypeStruct((len(planes), BINS + HALF, width), jnp.bfloat16)
    return pl.pallas_call(
        functools.partial(halves_kernel, planes),
        in_specs=[
            pl.BlockSpec(memory_space=pl.ANY),
            pl.BlockSpec(memory_space=pl.ANY),
            pl.BlockSpec(memory_space=pltpu.VMEM),
        ],
        scratch_shapes=[
            pltpu.VMEM((len(planes), 2, 2 * STRADDLE, width), jnp.bfloat16),
            pltpu.SemaphoreType.DMA((len(planes), 2, STRADDLE // STEP + 1)),
        ],
        out_shape=[shape, shape],
        compiler_params=pltpu.CompilerParams(vmem_limit_bytes=LARGE),
        cost_estimate=free(),
        name="halves",
    )(data, lent, table)


def straddle_kernel(keep_ref, got_ref, table_ref, *refs):
    out_refs, scratch_ref = refs[:-1], refs[-1]
    side = position()[1] // 2
    for k, out_ref in enumerate(out_refs):
        out_ref[2 * side] = keep_ref[k, :BINS, :]
        out_ref[2 - 2 * side] = got_ref[k, :BINS, :]
        scratch_ref[k, pl.ds(pl.multiple_of(side * HALF, HALF), HALF), :] = keep_ref[k, BINS:, :]
        scratch_ref[k, pl.ds(pl.multiple_of((1 - side) * HALF, HALF), HALF), :] = got_ref[k, BINS:, :]
        out_ref[1] = transform(table_ref, scratch_ref[k])


def straddle(keep, got, table):
    planes, _, width = keep.shape
    shape = jax.ShapeDtypeStruct((SPLIT // TEAM, BINS, width), jnp.bfloat16)
    return pl.pallas_call(
        straddle_kernel,
        out_shape=[shape] * planes,
        scratch_shapes=[pltpu.VMEM((planes, SEGMENT_LENGTH, width), jnp.bfloat16)],
        compiler_params=pltpu.CompilerParams(vmem_limit_bytes=16 << 20),
        cost_estimate=free(),
        name="straddle",
    )(keep, got, table)


def pick_kernel(width, sources_ref, alive_ref, data_ref, *refs):
    out_refs, acc_ref, picked_ref = refs[:-2], refs[-2], refs[-1]
    step = pl.program_id(0)
    columns = data_ref.shape[1]
    lane = lax.broadcasted_iota(jnp.int32, (1, 128), 1)
    ids = jnp.full((1, 128), -1, jnp.int32)
    for q in range(SOURCES):
        ids = jnp.where(lane == q, sources_ref[q // SRC, q % SRC], ids)
    channel = lax.broadcasted_iota(jnp.int32, (columns, 128), 0)
    chosen = jnp.where(channel == ids - step * columns, 1.0, 0.0).astype(jnp.bfloat16)
    part = jnp.dot(data_ref[...], chosen, preferred_element_type=jnp.float32)

    @pl.when(step == 0)
    def _():
        acc_ref[...] = part

    @pl.when(step > 0)
    def _():
        acc_ref[...] += part

    @pl.when(step == pl.num_programs(0) - 1)
    def _():
        row = lax.broadcasted_iota(jnp.int32, (SOURCES, PACKED - HELD), 0)
        flags = jnp.zeros((SOURCES, PACKED - HELD), jnp.float32)
        for q in range(SOURCES):
            local = sources_ref[q // SRC, q % SRC] - lax.axis_index("chan") * width
            inside = (local >= 0) & (local < width)
            flag = jnp.where(inside, alive_ref[jnp.clip(local, 0, width - 1)], 0)
            flags = jnp.where(row == q, flag.astype(jnp.float32), flags)
        picked_ref[:, :HELD] = acc_ref[...].T[:SOURCES, :]
        picked_ref[:, HELD:] = flags
        for k, out_ref in enumerate(out_refs):
            start = pl.multiple_of((position()[1] ^ k) * SHARE, SHARE)
            out_ref[...] = picked_ref[pl.ds(start, SHARE), :].astype(jnp.bfloat16)


def pick(sources, alive, data, count):
    width = data.shape[1] // count
    columns = TEAM * width
    return pl.pallas_call(
        functools.partial(pick_kernel, width),
        grid=(count // TEAM,),
        in_specs=[
            pl.BlockSpec(memory_space=pltpu.SMEM),
            pl.BlockSpec(memory_space=pltpu.SMEM),
            pl.BlockSpec((HELD, columns), lambda i: (0, i)),
        ],
        out_specs=[pl.BlockSpec((SHARE, PACKED), lambda i: (0, 0))] * TEAM,
        scratch_shapes=[pltpu.VMEM((HELD, 128), jnp.float32), pltpu.VMEM((SOURCES, PACKED), jnp.float32)],
        out_shape=[jax.ShapeDtypeStruct((SHARE, PACKED), jnp.bfloat16)] * TEAM,
        compiler_params=pltpu.CompilerParams(vmem_limit_bytes=LARGE),
        cost_estimate=free(),
        name="pick",
    )(sources, alive, data)


def sources_kernel(*refs):
    picked_refs, table_ref, out_ref, samples_ref = refs[:TEAM], refs[TEAM], refs[TEAM + 1], refs[TEAM + 2]
    place = position()[1]
    flags = jnp.zeros((SHARE, PACKED - HELD), jnp.float32)
    for k, picked_ref in enumerate(picked_refs):
        picked = picked_ref[...].astype(jnp.float32)
        flags += picked[:, HELD:]
        samples_ref[:, pl.ds(pl.multiple_of((place ^ k) * HELD, 128), HELD)] = picked[:, :HELD]
    samples = [samples_ref[:, w * SEGMENT_LENGTH : (w + 1) * SEGMENT_LENGTH] for w in range(TEAM_WINDOWS)]
    spectra = lax.dot_general(
        jnp.concatenate(samples, axis=0).astype(jnp.bfloat16),
        table_ref[...],
        (((1,), (1,)), ((), ())),
        preferred_element_type=jnp.float32,
    )
    flags = jnp.concatenate([flags] * (BINS // 128), axis=1)
    out_ref[...] = jnp.concatenate([spectra, flags], axis=0).astype(jnp.bfloat16)


def source_spectra(picked, table):
    return pl.pallas_call(
        sources_kernel,
        scratch_shapes=[pltpu.VMEM((SHARE, TEAM * HELD), jnp.float32)],
        out_shape=jax.ShapeDtypeStruct(((TEAM_WINDOWS + 1) * SHARE, BINS), jnp.bfloat16),
        cost_estimate=free(),
        name="source_spectra",
    )(*picked, table)


def whiten_kernel(*refs):
    spectra_refs, out_ref, planes_ref = refs[:TEAM], refs[TEAM], refs[TEAM + 1]
    mine, _ = position()
    flags = jnp.zeros((SHARE, BINS), jnp.float32)
    for k, spectra_ref in enumerate(spectra_refs):
        spectra = spectra_ref[...].astype(jnp.float32)
        flags += spectra[TEAM_WINDOWS * SHARE :]
        planes_ref[mine ^ k] = spectra[: TEAM_WINDOWS * SHARE]
    spectra = planes_ref[...].reshape(SEGMENT_TALLY, SHARE, BINS)
    power = jnp.sum(jnp.square(spectra), axis=0)
    lane = lax.broadcasted_iota(jnp.int32, (SHARE, BINS), 1)
    other = jnp.where(lane % (2 * SUB) < SUB, pltpu.roll(power, BINS - SUB, 1), pltpu.roll(power, SUB, 1))
    level = (power + other) / SEGMENT_TALLY
    factor = flags / jnp.sqrt(level + 0.01)
    src = (spectra * factor[None]).astype(jnp.bfloat16).astype(jnp.float32)
    lane = lax.broadcasted_iota(jnp.int32, (SHARE, 128), 1) // (2 * SUB)
    each = 128 // (2 * SUB)
    for tile in range(TILES):
        half, at = divmod(tile, each)
        for group in range(DEPTH // 128):
            out = jnp.zeros((SHARE, 128), jnp.float32)
            for k in range(each):
                window = group * each + k
                if window < SEGMENT_TALLY:
                    piece = src[window, :, half * 128 : (half + 1) * 128]
                    shift = (k - at) * 2 * SUB % 128
                    piece = pltpu.roll(piece, shift, 1) if shift else piece
                    out = jnp.where(lane == k, piece, out)
            out_ref[tile, :, group * 128 : (group + 1) * 128] = out.astype(jnp.bfloat16)


def whiten(spectra):
    return pl.pallas_call(
        whiten_kernel,
        scratch_shapes=[pltpu.VMEM((TEAM, TEAM_WINDOWS * SHARE, BINS), jnp.float32)],
        out_shape=jax.ShapeDtypeStruct((TILES, SHARE, DEPTH), jnp.bfloat16),
        compiler_params=pltpu.CompilerParams(vmem_limit_bytes=16 << 20),
        cost_estimate=free(),
        name="whiten",
    )(*spectra)


def left_kernel(*refs):
    src_refs, left_ref = refs[:-1], refs[-1]
    src = [ref[i, 0].astype(jnp.float32) for ref in src_refs for i in range(ref.shape[0])]
    src = jnp.concatenate(src, axis=0)
    lane = lax.broadcasted_iota(jnp.int32, (SOURCES, DEPTH), 1)
    turned = jnp.where(lane % (2 * SUB) < SUB, -pltpu.roll(src, DEPTH - SUB, 1), pltpu.roll(src, SUB, 1))
    row = lax.broadcasted_iota(jnp.int32, (1, 2 * SUB, DEPTH), 1)
    lane = lax.broadcasted_iota(jnp.int32, (1, 2 * SUB, DEPTH), 2)
    both = jnp.where(row < SUB, src[:, None, :], turned[:, None, :])
    both = jnp.where(lane % SUB == row % SUB, both, 0.0)
    left_ref[0] = both.reshape(SOURCES * 2 * SUB, DEPTH).astype(jnp.bfloat16)


def left_factor(src):
    return pl.pallas_call(
        left_kernel,
        grid=(TILES,),
        in_specs=[pl.BlockSpec((part.shape[0], 1, SHARE, DEPTH), lambda i: (0, i, 0, 0)) for part in src],
        out_specs=pl.BlockSpec((1, SOURCES * 2 * SUB, DEPTH), lambda i: (i, 0, 0)),
        out_shape=jax.ShapeDtypeStruct((TILES, SOURCES * 2 * SUB, DEPTH), jnp.bfloat16),
        compiler_params=pltpu.CompilerParams(vmem_limit_bytes=16 << 20),
        cost_estimate=pl.CostEstimate(flops=0, bytes_accessed=1 << 20, transcendentals=0),
        name="left",
    )(*src)


def whiten_all(samples, alive, table):
    samples = samples.reshape(SOURCES, SEGMENT_TALLY, SEGMENT_LENGTH)
    spectra = jnp.einsum("qwt,kt->qwk", samples, table, preferred_element_type=jnp.float32)
    power = jnp.mean(spectra**2, axis=1).reshape(SOURCES, TILES, 2, SUB)
    level = power[:, :, :1] + power[:, :, 1:]
    factor = alive[:, None, None, None] / jnp.sqrt(level + 0.01)
    factor = jnp.broadcast_to(factor, (SOURCES, TILES, 2, SUB)).reshape(SOURCES, BINS)
    src = (spectra * factor[:, None, :]).astype(jnp.bfloat16)
    src = jnp.transpose(src.reshape(SOURCES, SEGMENT_TALLY, TILES, 2 * SUB), (2, 0, 1, 3))
    src = src.reshape(TILES, SOURCES, SEGMENT_TALLY * 2 * SUB)
    src = jnp.pad(src, ((0, 0), (0, 0), (0, DEPTH - SEGMENT_TALLY * 2 * SUB)))
    return [src[None, :, k * SHARE : (k + 1) * SHARE] for k in range(TEAM)]


BATCH = 8


def correlate_kernel(relative, left_ref, whole_ref, other_ref, *refs):
    split_refs, (alive_ref, inverse_ref, out_ref, right_ref, cross_ref, done_ref, sems) = refs[:TEAM], refs[TEAM:]
    mine, place = position() if relative else (0, 0)
    width = right_ref.shape[2]
    rows = 2 * SUB
    span = TEAM_WINDOWS * rows
    pad = DEPTH - SEGMENT_TALLY * rows
    alive = alive_ref[...].astype(jnp.float32)

    for index in range(TILES):
        tile = slice(index * rows, (index + 1) * rows)
        right_ref[index, DEPTH - pad :, :] = jnp.zeros((pad, width), jnp.bfloat16)
        for plane in range(TEAM):
            for core in range(2):
                at = plane * span + core * 2 * rows
                mine_at = pl.multiple_of(at + place // 2 * 4 * rows, rows)
                other_at = pl.multiple_of(at + (1 - place // 2) * 4 * rows, rows)
                right_ref[index, pl.ds(mine_at, rows), :] = whole_ref[plane * 2 + core, 0, tile, :]
                right_ref[index, pl.ds(other_at, rows), :] = other_ref[plane * 2 + core, tile, :]
            for j in range(SPLIT // TEAM):
                at = pl.multiple_of((plane ^ mine) * span + (2 * j + 1) * rows, rows)
                right_ref[index, pl.ds(at, rows), :] = split_refs[plane][j, tile, :]
        right = right_ref[index]
        power = jnp.square(right.astype(jnp.float32)).reshape(DEPTH // rows, rows, width)
        power = jnp.sum(power, axis=0)
        level = (power[:SUB] + power[SUB:]) / SEGMENT_TALLY
        factor = alive / jnp.sqrt(level + 0.01)
        factor = jnp.concatenate([factor, factor], axis=0)[None]
        cross = jnp.dot(left_ref[index], right, preferred_element_type=jnp.float32)
        cross = cross.reshape(SOURCES, rows, width)
        cross_ref[:, tile, :] = jnp.where(factor > 0.0, cross * factor, 0.0).astype(jnp.bfloat16)

    def copy(step):
        part = pl.ds(step * BATCH, BATCH)
        return pltpu.make_async_copy(done_ref.at[part], out_ref.at[part], sems.at[step])

    @pl.loop(0, SOURCES // BATCH)
    def _(step):
        for k in range(BATCH):
            index = step * BATCH + k
            held = (index // SHARE ^ place) * SHARE + index % SHARE
            lagged = jnp.dot(inverse_ref[...], cross_ref[held], preferred_element_type=jnp.float32)
            done_ref[index] = (lagged * (1.0 / math.sqrt(NF * SEGMENT_TALLY))).astype(jnp.bfloat16)
        copy(step).start()

    @pl.loop(0, SOURCES // BATCH)
    def _(step):
        copy(step).wait()


def correlate(relative, left, whole, other, split, alive, inverse):
    width = whole.shape[3]
    return pl.pallas_call(
        functools.partial(correlate_kernel, relative),
        out_specs=pl.BlockSpec(memory_space=pl.ANY),
        scratch_shapes=[
            pltpu.VMEM((TILES, DEPTH, width), jnp.bfloat16),
            pltpu.VMEM((SOURCES, BINS, width), jnp.bfloat16),
            pltpu.VMEM((SOURCES, LAGS, width), jnp.bfloat16),
            pltpu.SemaphoreType.DMA((SOURCES // BATCH,)),
        ],
        out_shape=jax.ShapeDtypeStruct((SOURCES, LAGS, width), jnp.bfloat16),
        compiler_params=pltpu.CompilerParams(vmem_limit_bytes=18 << 20),
        name="correlate",
    )(left, whole, other, *split, alive, inverse)


def body(data, alive, sources):
    count = lax.axis_size("chan")
    width = data.shape[1] // count
    table = forward_table()
    relative = data.shape[0] == HELD and count == TEAM * TEAM
    if relative:
        swap = lambda x, k: lax.ppermute(x, "chan", [(i, i ^ k) for i in range(count)])
        team = range(1, TEAM)
        across = [[z * TEAM + y * 2 + core for z in range(count // TEAM) for core in range(2)] for y in range(2)]
        whole = prepare(data, table, count)
        data, whole = lax.optimization_barrier((data, whole))
        lent = lend(data, count)
        data, lent = lax.optimization_barrier((data, lent))
        lent = swap(lent, 1)
        whole = lax.all_to_all(whole, "chan", 0, 0, tiled=True, axis_index_groups=across)
        picked = pick(sources, alive, data, count)
        data, picked = lax.optimization_barrier((data, picked))
        picked = [picked[0]] + [swap(picked[k], k) for k in team]
        spectra = source_spectra(picked, table)
        keep_far, give_far = halves((2, 3), data, lent, table, count)
        give_far, spectra, data = lax.optimization_barrier((give_far, spectra, data))
        arrived = [swap(spectra, k * TEAM) for k in team]
        keep_near, give_near = halves((0, 1), data, lent, table, count)
        far = straddle(keep_far, swap(give_far, 2), table)
        got_near = swap(give_near, 2)
        arrived, whole, far, got_near = lax.optimization_barrier((arrived, whole, far, got_near))
        other = regroup(whole)
        src = whiten([spectra] + arrived)[None]
        keep_near, src, other = lax.optimization_barrier((keep_near, src, other))
        src = jnp.concatenate([src, swap(src, 1)])
        near = straddle(keep_near, got_near, table)
        other = swap(other, 2)
        src = [src, swap(src, 2)]
        split = [near[0], swap(near[1], TEAM), swap(far[0], 2 * TEAM), swap(far[1], 3 * TEAM)]
    else:
        me = lax.axis_index("chan")
        ids = sources.reshape(-1)
        near = ids[:, None] == me * width + jnp.arange(width, dtype=jnp.int32)[None, :]
        flags = jnp.sum(jnp.where(near, alive[None, :], 0), axis=1).astype(jnp.float32)
        chosen = jnp.where(jnp.arange(data.shape[1], dtype=jnp.int32)[:, None] == ids[None, :], 1.0, 0.0)
        picked = jnp.dot(data, chosen.astype(jnp.bfloat16), preferred_element_type=jnp.float32)
        picked = lax.all_gather(picked.astype(jnp.bfloat16), "chan", axis=0)
        alive_sources = lax.psum(flags, "chan")
        blocks = data.reshape(data.shape[0], count, width)
        blocks = lax.all_to_all(blocks, "chan", split_axis=1, concat_axis=0, tiled=True)
        blocks = blocks.reshape(SEGMENT_TALLY, SEGMENT_LENGTH, width)
        spectra = jnp.einsum("kt,wtc->wkc", table, blocks, preferred_element_type=jnp.float32)
        spectra = spectra.astype(jnp.bfloat16).reshape(TEAM, TEAM_WINDOWS, BINS, width)
        whole = spectra[:, 0:3:2].reshape(2 * TEAM, 1, BINS, width)
        other = spectra[:, 4:7:2].reshape(2 * TEAM, BINS, width)
        split = [spectra[z, 1::2] for z in range(TEAM)]
        src = whiten_all(jnp.transpose(picked, (2, 0, 1)), alive_sources, table)
    left = left_factor(src)
    out = correlate(relative, left, whole, other, split, alive[None, :], inverse_table())
    return out.reshape(ROUNDS, SRC, LAGS, width)


def solution(mesh):
    return jax.shard_map(
        body,
        mesh=mesh,
        in_specs=(P(("groups", "chan"), None), P(("groups", "chan")), P()),
        out_specs=P("groups", None, None, "chan"),
        check_vma=False,
    )
```

```python
import functools
import math

import jax
import jax.numpy as jnp
import ml_dtypes
import numpy as np
from jax import lax
from jax.experimental import pallas as pl
from jax.experimental.pallas import tpu as pltpu
from jax.sharding import PartitionSpec as P

SEGMENT_LENGTH = 512
NF = 128
LAGS = 256
SRC = 16
ROUNDS = 2
SEGMENT_TALLY = 28

SOURCES = SRC * ROUNDS
BINS = 2 * NF
SUB = 8
TILES = NF // SUB
TEAM = 4
TEAM_WINDOWS = 7
STEP = 128
HELD = TEAM_WINDOWS * SEGMENT_LENGTH // TEAM
STRADDLE = HELD - SEGMENT_LENGTH
HALF = SEGMENT_LENGTH // 2
WHOLE = 16
SPLIT = 12
PACKED = 1024
SHARE = SOURCES // TEAM
DEPTH = 512
LARGE = 56 << 20


def angles(times):
    bins = np.arange(NF)[:, None] + 1
    turn = bins * times[None, :] % SEGMENT_LENGTH * (2.0 * np.pi / SEGMENT_LENGTH)
    table = np.stack([np.cos(turn), -np.sin(turn)])
    table = table.reshape(2, TILES, SUB, times.size).transpose(1, 0, 2, 3)
    return table.reshape(BINS, times.size)


def forward_table():
    table = angles(np.arange(SEGMENT_LENGTH)) / math.sqrt(SEGMENT_LENGTH)
    return jnp.asarray(table.astype(ml_dtypes.bfloat16))


def inverse_table():
    table = angles(np.arange(LAGS) - LAGS // 2)
    return jnp.asarray(np.ascontiguousarray(table.T).astype(ml_dtypes.bfloat16))


def position():
    me = lax.axis_index("chan")
    return me // TEAM, me % TEAM


def transform(table_ref, block):
    return jnp.dot(table_ref[...], block, preferred_element_type=jnp.float32).astype(jnp.bfloat16)


def free(size):
    return pl.CostEstimate(flops=0, bytes_accessed=0, transcendentals=0)


def window(data_ref, row, column, depth, width):
    row = pl.ds(pl.multiple_of(row, STEP), depth)
    return data_ref.at[row, pl.ds(pl.multiple_of(column, 128), width)]


def straddling(data_ref, j, place, column, width):
    row = jnp.where(j < place, j, j + SEGMENT_LENGTH // STEP) * STEP
    return window(data_ref, row, column * width, STEP, width)


def prepare_kernel(data_ref, rows_ref, whole_ref, block_ref, out_ref, table_ref, in_sems, out_sems, sem):
    _, place = position()
    planes, _, _, width = out_ref.shape
    copies = []
    table = pltpu.make_async_copy(rows_ref, table_ref, sem)
    table.start()
    for plane in range(planes):
        source = window(data_ref, place * STEP, plane * TEAM * width, SEGMENT_LENGTH, TEAM * width)
        copies.append(pltpu.make_async_copy(source, block_ref.at[plane], in_sems.at[plane]))
        copies[plane].start()
    table.wait()
    for plane in range(planes):
        copies[plane].wait()
        for member in range(TEAM):
            column = pl.ds(pl.multiple_of((place ^ member) * width, width), width)
            out_ref[plane, member] = transform(table_ref, block_ref[plane, :, column])
        copies.append(pltpu.make_async_copy(out_ref.at[plane], whole_ref.at[plane], out_sems.at[plane]))
        copies[-1].start()
    for copy in copies[planes:]:
        copy.wait()


def prepare(data, table, count):
    width = data.shape[1] // count
    planes = count // TEAM
    return pl.pallas_call(
        prepare_kernel,
        in_specs=[pl.BlockSpec(memory_space=pl.ANY)] * 2,
        scratch_shapes=[
            pltpu.VMEM((planes, SEGMENT_LENGTH, TEAM * width), jnp.bfloat16),
            pltpu.VMEM((planes, TEAM, BINS, width), jnp.bfloat16),
            pltpu.VMEM((BINS, SEGMENT_LENGTH), jnp.bfloat16),
            pltpu.SemaphoreType.DMA((planes,)),
            pltpu.SemaphoreType.DMA((planes,)),
            pltpu.SemaphoreType.DMA,
        ],
        out_specs=pl.BlockSpec(memory_space=pl.ANY),
        out_shape=jax.ShapeDtypeStruct((planes, TEAM, BINS, width), jnp.bfloat16),
        compiler_params=pltpu.CompilerParams(vmem_limit_bytes=LARGE),
        name="prepare",
    )(data, table)


def regroup_kernel(whole_ref, *out_refs):
    for member, out_ref in enumerate(out_refs, 1):
        out_ref[...] = whole_ref[:, member]


def regroup(whole):
    planes, _, rows, width = whole.shape
    return pl.pallas_call(
        regroup_kernel,
        out_shape=[jax.ShapeDtypeStruct((planes, rows, width), jnp.bfloat16)] * (TEAM - 1),
        compiler_params=pltpu.CompilerParams(vmem_limit_bytes=16 << 20),
        cost_estimate=free(1 << 20),
        name="regroup",
    )(whole)


def lend_kernel(data_ref, out_ref, sems):
    _, place = position()
    width = out_ref.shape[2]
    copies = []
    for target in range(out_ref.shape[0]):
        column = target // 2 * TEAM + target % 2 * 2 + 1 - place % 2
        for j in range(STRADDLE // STEP):
            source = straddling(data_ref, j, place, column, width)
            copy = pltpu.make_async_copy(source, out_ref.at[target, pl.ds(j * STEP, STEP)], sems.at[target, j])
            copy.start()
            copies.append(copy)
    for copy in copies:
        copy.wait()


def lend(data, count):
    width = data.shape[1] // count
    return pl.pallas_call(
        lend_kernel,
        in_specs=[pl.BlockSpec(memory_space=pl.ANY)],
        scratch_shapes=[pltpu.SemaphoreType.DMA((count // 2, STRADDLE // STEP))],
        out_shape=jax.ShapeDtypeStruct((count // 2, STRADDLE, width), jnp.bfloat16),
        compiler_params=pltpu.CompilerParams(vmem_limit_bytes=LARGE),
        cost_estimate=free(1 << 20),
        name="lend",
    )(data)


def halves_kernel(planes, data_ref, lent_ref, table_ref, keep_ref, give_ref, chip_ref, sems):
    mine, place = position()
    side, core = place // 2, place % 2
    width = keep_ref.shape[2]
    copies = []
    for i, k in enumerate(planes):
        plane = mine ^ k
        for t, target in enumerate((side, 1 - side)):
            for j in range(STRADDLE // STEP):
                source = straddling(data_ref, j, place, plane * TEAM + target * 2 + core, width)
                start = pl.multiple_of(core * STRADDLE + j * STEP, STEP)
                copies.append(pltpu.make_async_copy(source, chip_ref.at[i, t, pl.ds(start, STEP)], sems.at[i, t, j]))
            start = pl.multiple_of((1 - core) * STRADDLE, STEP)
            part = chip_ref.at[i, t, pl.ds(start, STRADDLE)]
            copies.append(pltpu.make_async_copy(lent_ref.at[plane * 2 + target], part, sems.at[i, t, STRADDLE // STEP]))
    for copy in copies:
        copy.start()
    for copy in copies:
        copy.wait()
    for i in range(len(planes)):
        for t, out_ref in enumerate((keep_ref, give_ref)):
            start = pl.multiple_of(side * HALF, HALF)
            out_ref[i, :BINS, :] = transform(table_ref, chip_ref[i, t, pl.ds(start, SEGMENT_LENGTH), :])
            start = pl.multiple_of((1 - side) * SEGMENT_LENGTH, HALF)
            out_ref[i, BINS:, :] = chip_ref[i, t, pl.ds(start, HALF), :]


def halves(planes, data, lent, table, count):
    width = data.shape[1] // count
    shape = jax.ShapeDtypeStruct((len(planes), BINS + HALF, width), jnp.bfloat16)
    return pl.pallas_call(
        functools.partial(halves_kernel, planes),
        in_specs=[
            pl.BlockSpec(memory_space=pl.ANY),
            pl.BlockSpec(memory_space=pl.ANY),
            pl.BlockSpec(memory_space=pltpu.VMEM),
        ],
        scratch_shapes=[
            pltpu.VMEM((len(planes), 2, 2 * STRADDLE, width), jnp.bfloat16),
            pltpu.SemaphoreType.DMA((len(planes), 2, STRADDLE // STEP + 1)),
        ],
        out_shape=[shape, shape],
        compiler_params=pltpu.CompilerParams(vmem_limit_bytes=LARGE),
        cost_estimate=free(1 << 20),
        name="halves",
    )(data, lent, table)


def straddle_kernel(keep_ref, got_ref, table_ref, *refs):
    out_refs, scratch_ref = refs[:-1], refs[-1]
    side = position()[1] // 2
    for k, out_ref in enumerate(out_refs):
        out_ref[2 * side] = keep_ref[k, :BINS, :]
        out_ref[2 - 2 * side] = got_ref[k, :BINS, :]
        scratch_ref[k, pl.ds(pl.multiple_of(side * HALF, HALF), HALF), :] = keep_ref[k, BINS:, :]
        scratch_ref[k, pl.ds(pl.multiple_of((1 - side) * HALF, HALF), HALF), :] = got_ref[k, BINS:, :]
        out_ref[1] = transform(table_ref, scratch_ref[k])


def straddle(keep, got, table):
    planes, _, width = keep.shape
    shape = jax.ShapeDtypeStruct((SPLIT // TEAM, BINS, width), jnp.bfloat16)
    return pl.pallas_call(
        straddle_kernel,
        out_shape=[shape] * planes,
        scratch_shapes=[pltpu.VMEM((planes, SEGMENT_LENGTH, width), jnp.bfloat16)],
        compiler_params=pltpu.CompilerParams(vmem_limit_bytes=16 << 20),
        cost_estimate=free(1 << 20),
        name="straddle",
    )(keep, got, table)


def pick_kernel(width, sources_ref, alive_ref, data_ref, *refs):
    out_refs, acc_ref, picked_ref = refs[:-2], refs[-2], refs[-1]
    step = pl.program_id(0)
    columns = data_ref.shape[1]
    lane = lax.broadcasted_iota(jnp.int32, (1, 128), 1)
    ids = jnp.full((1, 128), -1, jnp.int32)
    for q in range(SOURCES):
        ids = jnp.where(lane == q, sources_ref[q // SRC, q % SRC], ids)
    channel = lax.broadcasted_iota(jnp.int32, (columns, 128), 0)
    chosen = jnp.where(channel == ids - step * columns, 1.0, 0.0).astype(jnp.bfloat16)
    part = jnp.dot(data_ref[...], chosen, preferred_element_type=jnp.float32)

    @pl.when(step == 0)
    def _():
        acc_ref[...] = part

    @pl.when(step > 0)
    def _():
        acc_ref[...] += part

    @pl.when(step == pl.num_programs(0) - 1)
    def _():
        row = lax.broadcasted_iota(jnp.int32, (SOURCES, PACKED - HELD), 0)
        flags = jnp.zeros((SOURCES, PACKED - HELD), jnp.float32)
        for q in range(SOURCES):
            local = sources_ref[q // SRC, q % SRC] - lax.axis_index("chan") * width
            inside = (local >= 0) & (local < width)
            flag = jnp.where(inside, alive_ref[jnp.clip(local, 0, width - 1)], 0)
            flags = jnp.where(row == q, flag.astype(jnp.float32), flags)
        picked_ref[:, :HELD] = acc_ref[...].T[:SOURCES, :]
        picked_ref[:, HELD:] = flags
        for k, out_ref in enumerate(out_refs):
            start = pl.multiple_of((position()[1] ^ k) * SHARE, SHARE)
            out_ref[...] = picked_ref[pl.ds(start, SHARE), :].astype(jnp.bfloat16)


def pick(sources, alive, data, count):
    width = data.shape[1] // count
    columns = TEAM * width
    return pl.pallas_call(
        functools.partial(pick_kernel, width),
        grid=(count // TEAM,),
        in_specs=[
            pl.BlockSpec(memory_space=pltpu.SMEM),
            pl.BlockSpec(memory_space=pltpu.SMEM),
            pl.BlockSpec((HELD, columns), lambda i: (0, i)),
        ],
        out_specs=[pl.BlockSpec((SHARE, PACKED), lambda i: (0, 0))] * TEAM,
        scratch_shapes=[pltpu.VMEM((HELD, 128), jnp.float32), pltpu.VMEM((SOURCES, PACKED), jnp.float32)],
        out_shape=[jax.ShapeDtypeStruct((SHARE, PACKED), jnp.bfloat16)] * TEAM,
        compiler_params=pltpu.CompilerParams(vmem_limit_bytes=LARGE),
        cost_estimate=free(1 << 20),
        name="pick",
    )(sources, alive, data)


def sources_kernel(*refs):
    picked_refs, table_ref, out_ref, samples_ref = refs[:TEAM], refs[TEAM], refs[TEAM + 1], refs[TEAM + 2]
    place = position()[1]
    flags = jnp.zeros((SHARE, PACKED - HELD), jnp.float32)
    for k, picked_ref in enumerate(picked_refs):
        picked = picked_ref[...].astype(jnp.float32)
        flags += picked[:, HELD:]
        samples_ref[:, pl.ds(pl.multiple_of((place ^ k) * HELD, 128), HELD)] = picked[:, :HELD]
    samples = [samples_ref[:, w * SEGMENT_LENGTH : (w + 1) * SEGMENT_LENGTH] for w in range(TEAM_WINDOWS)]
    spectra = lax.dot_general(
        jnp.concatenate(samples, axis=0).astype(jnp.bfloat16),
        table_ref[...],
        (((1,), (1,)), ((), ())),
        preferred_element_type=jnp.float32,
    )
    flags = jnp.concatenate([flags] * (BINS // 128), axis=1)
    out_ref[...] = jnp.concatenate([spectra, flags], axis=0).astype(jnp.bfloat16)


def source_spectra(picked, table):
    return pl.pallas_call(
        sources_kernel,
        scratch_shapes=[pltpu.VMEM((SHARE, TEAM * HELD), jnp.float32)],
        out_shape=jax.ShapeDtypeStruct(((TEAM_WINDOWS + 1) * SHARE, BINS), jnp.bfloat16),
        cost_estimate=free(1 << 18),
        name="source_spectra",
    )(*picked, table)


def whiten_kernel(*refs):
    spectra_refs, out_ref, planes_ref = refs[:TEAM], refs[TEAM], refs[TEAM + 1]
    mine, _ = position()
    flags = jnp.zeros((SHARE, BINS), jnp.float32)
    for k, spectra_ref in enumerate(spectra_refs):
        spectra = spectra_ref[...].astype(jnp.float32)
        flags += spectra[TEAM_WINDOWS * SHARE :]
        planes_ref[mine ^ k] = spectra[: TEAM_WINDOWS * SHARE]
    spectra = planes_ref[...].reshape(SEGMENT_TALLY, SHARE, BINS)
    power = jnp.sum(jnp.square(spectra), axis=0)
    lane = lax.broadcasted_iota(jnp.int32, (SHARE, BINS), 1)
    other = jnp.where(lane % (2 * SUB) < SUB, pltpu.roll(power, BINS - SUB, 1), pltpu.roll(power, SUB, 1))
    level = (power + other) / SEGMENT_TALLY
    factor = flags / jnp.sqrt(level + 0.01)
    src = (spectra * factor[None]).astype(jnp.bfloat16).astype(jnp.float32)
    lane = lax.broadcasted_iota(jnp.int32, (SHARE, 128), 1) // (2 * SUB)
    each = 128 // (2 * SUB)
    for tile in range(TILES):
        half, at = divmod(tile, each)
        for group in range(DEPTH // 128):
            out = jnp.zeros((SHARE, 128), jnp.float32)
            for k in range(each):
                window = group * each + k
                if window < SEGMENT_TALLY:
                    piece = src[window, :, half * 128 : (half + 1) * 128]
                    shift = (k - at) * 2 * SUB % 128
                    piece = pltpu.roll(piece, shift, 1) if shift else piece
                    out = jnp.where(lane == k, piece, out)
            out_ref[tile, :, group * 128 : (group + 1) * 128] = out.astype(jnp.bfloat16)


def whiten(spectra):
    return pl.pallas_call(
        whiten_kernel,
        scratch_shapes=[pltpu.VMEM((TEAM, TEAM_WINDOWS * SHARE, BINS), jnp.float32)],
        out_shape=jax.ShapeDtypeStruct((TILES, SHARE, DEPTH), jnp.bfloat16),
        compiler_params=pltpu.CompilerParams(vmem_limit_bytes=16 << 20),
        cost_estimate=free(1 << 18),
        name="whiten",
    )(*spectra)


def left_kernel(*refs):
    src_refs, left_ref = refs[:-1], refs[-1]
    src = jnp.concatenate([ref[0].astype(jnp.float32) for ref in src_refs], axis=0)
    lane = lax.broadcasted_iota(jnp.int32, (SOURCES, DEPTH), 1)
    turned = jnp.where(lane % (2 * SUB) < SUB, -pltpu.roll(src, DEPTH - SUB, 1), pltpu.roll(src, SUB, 1))
    row = lax.broadcasted_iota(jnp.int32, (1, 2 * SUB, DEPTH), 1)
    lane = lax.broadcasted_iota(jnp.int32, (1, 2 * SUB, DEPTH), 2)
    both = jnp.where(row < SUB, src[:, None, :], turned[:, None, :])
    both = jnp.where(lane % SUB == row % SUB, both, 0.0)
    left_ref[0] = both.reshape(SOURCES * 2 * SUB, DEPTH).astype(jnp.bfloat16)


def left_factor(src):
    return pl.pallas_call(
        left_kernel,
        grid=(TILES,),
        in_specs=[pl.BlockSpec((1, SHARE, DEPTH), lambda i: (i, 0, 0))] * TEAM,
        out_specs=pl.BlockSpec((1, SOURCES * 2 * SUB, DEPTH), lambda i: (i, 0, 0)),
        out_shape=jax.ShapeDtypeStruct((TILES, SOURCES * 2 * SUB, DEPTH), jnp.bfloat16),
        compiler_params=pltpu.CompilerParams(vmem_limit_bytes=16 << 20),
        cost_estimate=pl.CostEstimate(flops=0, bytes_accessed=1 << 20, transcendentals=0),
        name="left",
    )(*src)


def whiten_all(samples, alive, table):
    samples = samples.reshape(SOURCES, SEGMENT_TALLY, SEGMENT_LENGTH)
    spectra = jnp.einsum("qwt,kt->qwk", samples, table, preferred_element_type=jnp.float32)
    power = jnp.mean(spectra**2, axis=1).reshape(SOURCES, TILES, 2, SUB)
    level = power[:, :, :1] + power[:, :, 1:]
    factor = alive[:, None, None, None] / jnp.sqrt(level + 0.01)
    factor = jnp.broadcast_to(factor, (SOURCES, TILES, 2, SUB)).reshape(SOURCES, BINS)
    src = (spectra * factor[:, None, :]).astype(jnp.bfloat16)
    src = jnp.transpose(src.reshape(SOURCES, SEGMENT_TALLY, TILES, 2 * SUB), (2, 0, 1, 3))
    src = src.reshape(TILES, SOURCES, SEGMENT_TALLY * 2 * SUB)
    src = jnp.pad(src, ((0, 0), (0, 0), (0, DEPTH - SEGMENT_TALLY * 2 * SUB)))
    return [src[:, k * SHARE : (k + 1) * SHARE] for k in range(TEAM)]


BATCH = 8


def correlate_kernel(relative, left_ref, whole_ref, *refs):
    other_refs, split_refs = refs[: TEAM - 1], refs[TEAM - 1 : 2 * TEAM - 1]
    alive_ref, inverse_ref, out_ref, right_ref, cross_ref, done_ref, sems = refs[2 * TEAM - 1 :]
    mine, place = position() if relative else (0, 0)
    width = right_ref.shape[2]
    rows = 2 * SUB
    span = TEAM_WINDOWS * rows
    pad = DEPTH - SEGMENT_TALLY * rows
    alive = alive_ref[...].astype(jnp.float32)

    for index in range(TILES):
        tile = slice(index * rows, (index + 1) * rows)
        right_ref[index, DEPTH - pad :, :] = jnp.zeros((pad, width), jnp.bfloat16)
        for plane in range(TEAM):
            for member in range(TEAM):
                at = pl.multiple_of(plane * span + (member ^ place) * 2 * rows, rows)
                piece = other_refs[member - 1][plane, tile, :] if member else whole_ref[plane, 0, tile, :]
                right_ref[index, pl.ds(at, rows), :] = piece
            for j in range(SPLIT // TEAM):
                at = pl.multiple_of((plane ^ mine) * span + (2 * j + 1) * rows, rows)
                right_ref[index, pl.ds(at, rows), :] = split_refs[plane][j, tile, :]
        right = right_ref[index]
        power = jnp.square(right.astype(jnp.float32)).reshape(DEPTH // rows, rows, width)
        power = jnp.sum(power, axis=0)
        level = (power[:SUB] + power[SUB:]) / SEGMENT_TALLY
        factor = alive / jnp.sqrt(level + 0.01)
        factor = jnp.concatenate([factor, factor], axis=0)[None]
        cross = jnp.dot(left_ref[index], right, preferred_element_type=jnp.float32)
        cross = cross.reshape(SOURCES, rows, width)
        cross_ref[:, tile, :] = jnp.where(factor > 0.0, cross * factor, 0.0).astype(jnp.bfloat16)

    def copy(step):
        part = pl.ds(step * BATCH, BATCH)
        return pltpu.make_async_copy(done_ref.at[part], out_ref.at[part], sems.at[step])

    @pl.loop(0, SOURCES // BATCH)
    def _(step):
        for k in range(BATCH):
            index = step * BATCH + k
            held = (index // SHARE ^ place) * SHARE + index % SHARE
            lagged = jnp.dot(inverse_ref[...], cross_ref[held], preferred_element_type=jnp.float32)
            done_ref[index] = (lagged * (1.0 / math.sqrt(NF * SEGMENT_TALLY))).astype(jnp.bfloat16)
        copy(step).start()

    @pl.loop(0, SOURCES // BATCH)
    def _(step):
        copy(step).wait()


def correlate(relative, left, whole, others, split, alive, inverse):
    width = whole.shape[3]
    return pl.pallas_call(
        functools.partial(correlate_kernel, relative),
        out_specs=pl.BlockSpec(memory_space=pl.ANY),
        scratch_shapes=[
            pltpu.VMEM((TILES, DEPTH, width), jnp.bfloat16),
            pltpu.VMEM((SOURCES, BINS, width), jnp.bfloat16),
            pltpu.VMEM((SOURCES, LAGS, width), jnp.bfloat16),
            pltpu.SemaphoreType.DMA((SOURCES // BATCH,)),
        ],
        out_shape=jax.ShapeDtypeStruct((SOURCES, LAGS, width), jnp.bfloat16),
        compiler_params=pltpu.CompilerParams(vmem_limit_bytes=18 << 20),
        name="correlate",
    )(left, whole, *others, *split, alive, inverse)


def body(data, alive, sources):
    count = lax.axis_size("chan")
    width = data.shape[1] // count
    table = forward_table()
    relative = data.shape[0] == HELD and count == TEAM * TEAM
    if relative:
        swap = lambda x, k: lax.ppermute(x, "chan", [(i, i ^ k) for i in range(count)])
        team = range(1, TEAM)
        across = [[z * TEAM + p for z in range(count // TEAM)] for p in range(TEAM)]
        whole = prepare(data, table, count)
        data, whole = lax.optimization_barrier((data, whole))
        lent = lend(data, count)
        data, lent = lax.optimization_barrier((data, lent))
        lent = swap(lent, 1)
        whole = lax.all_to_all(whole, "chan", 0, 0, tiled=True, axis_index_groups=across)
        picked = pick(sources, alive, data, count)
        data, picked = lax.optimization_barrier((data, picked))
        picked = [picked[0]] + [swap(picked[k], k) for k in team]
        spectra = source_spectra(picked, table)
        keep_far, give_far = halves((2, 3), data, lent, table, count)
        give_far, spectra, data = lax.optimization_barrier((give_far, spectra, data))
        arrived = [swap(spectra, k * TEAM) for k in team]
        keep_near, give_near = halves((0, 1), data, lent, table, count)
        far = straddle(keep_far, swap(give_far, 2), table)
        arrived, whole, far = lax.optimization_barrier((arrived, whole, far))
        others = regroup(whole)
        src = whiten([spectra] + arrived)
        keep_near, src, others = lax.optimization_barrier((keep_near, src, others))
        others = [swap(others[k - 1], k) for k in team]
        near = straddle(keep_near, swap(give_near, 2), table)
        split = [near[0], swap(near[1], TEAM), swap(far[0], 2 * TEAM), swap(far[1], 3 * TEAM)]
        src = [src] + [swap(src, k) for k in team]
    else:
        me = lax.axis_index("chan")
        ids = sources.reshape(-1)
        near = ids[:, None] == me * width + jnp.arange(width, dtype=jnp.int32)[None, :]
        flags = jnp.sum(jnp.where(near, alive[None, :], 0), axis=1).astype(jnp.float32)
        chosen = jnp.where(jnp.arange(data.shape[1], dtype=jnp.int32)[:, None] == ids[None, :], 1.0, 0.0)
        picked = jnp.dot(data, chosen.astype(jnp.bfloat16), preferred_element_type=jnp.float32)
        picked = lax.all_gather(picked.astype(jnp.bfloat16), "chan", axis=0)
        alive_sources = lax.psum(flags, "chan")
        blocks = data.reshape(data.shape[0], count, width)
        blocks = lax.all_to_all(blocks, "chan", split_axis=1, concat_axis=0, tiled=True)
        blocks = blocks.reshape(SEGMENT_TALLY, SEGMENT_LENGTH, width)
        spectra = jnp.einsum("kt,wtc->wkc", table, blocks, preferred_element_type=jnp.float32)
        spectra = spectra.astype(jnp.bfloat16).reshape(TEAM, TEAM_WINDOWS, BINS, width)
        whole = spectra[:, 0:1]
        others = [spectra[:, 2 * k] for k in range(1, TEAM)]
        split = [spectra[z, 1::2] for z in range(TEAM)]
        src = whiten_all(jnp.transpose(picked, (2, 0, 1)), alive_sources, table)
    left = left_factor(src)
    out = correlate(relative, left, whole, others, split, alive[None, :], inverse_table())
    return out.reshape(ROUNDS, SRC, LAGS, width)


def solution(mesh):
    return jax.shard_map(
        body,
        mesh=mesh,
        in_specs=(P(("groups", "chan"), None), P(("groups", "chan")), P()),
        out_specs=P("groups", None, None, "chan"),
        check_vma=False,
    )
```

```python
import functools
import math

import jax
import jax.numpy as jnp
import ml_dtypes
import numpy as np
from jax import lax
from jax.experimental import pallas as pl
from jax.experimental.pallas import tpu as pltpu
from jax.sharding import PartitionSpec as P

SEGMENT_LENGTH = 512
NF = 128
LAGS = 256
SRC = 16
ROUNDS = 2
SEGMENT_TALLY = 28

SOURCES = SRC * ROUNDS
BINS = 2 * NF
SUB = 8
TILES = NF // SUB
TEAM = 4
TEAM_WINDOWS = 7
STEP = 128
HELD = TEAM_WINDOWS * SEGMENT_LENGTH // TEAM
STRADDLE = HELD - SEGMENT_LENGTH
HALF = SEGMENT_LENGTH // 2
WHOLE = 16
SPLIT = 12
PACKED = 1024
SHARE = SOURCES // TEAM
DEPTH = 512
LARGE = 56 << 20


def angles(times):
    bins = np.arange(NF)[:, None] + 1
    turn = bins * times[None, :] % SEGMENT_LENGTH * (2.0 * np.pi / SEGMENT_LENGTH)
    table = np.stack([np.cos(turn), -np.sin(turn)])
    table = table.reshape(2, TILES, SUB, times.size).transpose(1, 0, 2, 3)
    return table.reshape(BINS, times.size)


def forward_table():
    table = angles(np.arange(SEGMENT_LENGTH)) / math.sqrt(SEGMENT_LENGTH)
    return jnp.asarray(table.astype(ml_dtypes.bfloat16))


def inverse_table():
    table = angles(np.arange(LAGS) - LAGS // 2)
    return jnp.asarray(np.ascontiguousarray(table.T).astype(ml_dtypes.bfloat16))


def position():
    me = lax.axis_index("chan")
    return me // TEAM, me % TEAM


def transform(table_ref, block):
    return jnp.dot(table_ref[...], block, preferred_element_type=jnp.float32).astype(jnp.bfloat16)


def free():
    return pl.CostEstimate(flops=0, bytes_accessed=0, transcendentals=0)


def window(data_ref, row, column, depth, width):
    row = pl.ds(pl.multiple_of(row, STEP), depth)
    return data_ref.at[row, pl.ds(pl.multiple_of(column, 128), width)]


def straddling(data_ref, j, place, column, width):
    row = jnp.where(j < place, j, j + SEGMENT_LENGTH // STEP) * STEP
    return window(data_ref, row, column * width, STEP, width)


def prepare_kernel(data_ref, rows_ref, whole_ref, block_ref, out_ref, table_ref, in_sems, out_sems, sem):
    _, place = position()
    planes, width = out_ref.shape[0] // 2, out_ref.shape[3]
    copies = []
    table = pltpu.make_async_copy(rows_ref, table_ref, sem)
    table.start()
    for plane in range(planes):
        source = window(data_ref, place * STEP, plane * TEAM * width, SEGMENT_LENGTH, TEAM * width)
        copies.append(pltpu.make_async_copy(source, block_ref.at[plane], in_sems.at[plane]))
        copies[plane].start()
    table.wait()
    for plane in range(planes):
        copies[plane].wait()
        for core in range(2):
            for turn in range(2):
                column = pl.ds(pl.multiple_of(((place // 2 ^ turn) * 2 + core) * width, width), width)
                out_ref[plane * 2 + core, turn] = transform(table_ref, block_ref[plane, :, column])
        part = pl.ds(plane * 2, 2)
        copies.append(pltpu.make_async_copy(out_ref.at[part], whole_ref.at[part], out_sems.at[plane]))
        copies[-1].start()
    for copy in copies[planes:]:
        copy.wait()


def prepare(data, table, count):
    width = data.shape[1] // count
    planes = count // TEAM
    return pl.pallas_call(
        prepare_kernel,
        in_specs=[pl.BlockSpec(memory_space=pl.ANY)] * 2,
        scratch_shapes=[
            pltpu.VMEM((planes, SEGMENT_LENGTH, TEAM * width), jnp.bfloat16),
            pltpu.VMEM((planes * 2, 2, BINS, width), jnp.bfloat16),
            pltpu.VMEM((BINS, SEGMENT_LENGTH), jnp.bfloat16),
            pltpu.SemaphoreType.DMA((planes,)),
            pltpu.SemaphoreType.DMA((planes,)),
            pltpu.SemaphoreType.DMA,
        ],
        out_specs=pl.BlockSpec(memory_space=pl.ANY),
        out_shape=jax.ShapeDtypeStruct((planes * 2, 2, BINS, width), jnp.bfloat16),
        compiler_params=pltpu.CompilerParams(vmem_limit_bytes=LARGE),
        name="prepare",
    )(data, table)


def regroup_kernel(whole_ref, out_ref):
    out_ref[...] = whole_ref[:, 1]


def regroup(whole):
    held, _, rows, width = whole.shape
    return pl.pallas_call(
        regroup_kernel,
        out_shape=jax.ShapeDtypeStruct((held, rows, width), jnp.bfloat16),
        compiler_params=pltpu.CompilerParams(vmem_limit_bytes=16 << 20),
        cost_estimate=free(),
        name="regroup",
    )(whole)


def lend_kernel(data_ref, out_ref, sems):
    _, place = position()
    width = out_ref.shape[2]
    copies = []
    for target in range(out_ref.shape[0]):
        column = target // 2 * TEAM + target % 2 * 2 + 1 - place % 2
        for j in range(STRADDLE // STEP):
            source = straddling(data_ref, j, place, column, width)
            copy = pltpu.make_async_copy(source, out_ref.at[target, pl.ds(j * STEP, STEP)], sems.at[target, j])
            copy.start()
            copies.append(copy)
    for copy in copies:
        copy.wait()


def lend(data, count):
    width = data.shape[1] // count
    return pl.pallas_call(
        lend_kernel,
        in_specs=[pl.BlockSpec(memory_space=pl.ANY)],
        scratch_shapes=[pltpu.SemaphoreType.DMA((count // 2, STRADDLE // STEP))],
        out_shape=jax.ShapeDtypeStruct((count // 2, STRADDLE, width), jnp.bfloat16),
        compiler_params=pltpu.CompilerParams(vmem_limit_bytes=LARGE),
        cost_estimate=free(),
        name="lend",
    )(data)


def halves_kernel(planes, data_ref, lent_ref, table_ref, keep_ref, give_ref, chip_ref, sems):
    mine, place = position()
    side, core = place // 2, place % 2
    width = keep_ref.shape[2]
    copies = []
    for i, k in enumerate(planes):
        plane = mine ^ k
        for t, target in enumerate((side, 1 - side)):
            for j in range(STRADDLE // STEP):
                source = straddling(data_ref, j, place, plane * TEAM + target * 2 + core, width)
                start = pl.multiple_of(core * STRADDLE + j * STEP, STEP)
                copies.append(pltpu.make_async_copy(source, chip_ref.at[i, t, pl.ds(start, STEP)], sems.at[i, t, j]))
            start = pl.multiple_of((1 - core) * STRADDLE, STEP)
            part = chip_ref.at[i, t, pl.ds(start, STRADDLE)]
            copies.append(pltpu.make_async_copy(lent_ref.at[plane * 2 + target], part, sems.at[i, t, STRADDLE // STEP]))
    for copy in copies:
        copy.start()
    for copy in copies:
        copy.wait()
    for i in range(len(planes)):
        for t, out_ref in enumerate((keep_ref, give_ref)):
            start = pl.multiple_of(side * HALF, HALF)
            out_ref[i, :BINS, :] = transform(table_ref, chip_ref[i, t, pl.ds(start, SEGMENT_LENGTH), :])
            start = pl.multiple_of((1 - side) * SEGMENT_LENGTH, HALF)
            out_ref[i, BINS:, :] = chip_ref[i, t, pl.ds(start, HALF), :]


def halves(planes, data, lent, table, count):
    width = data.shape[1] // count
    shape = jax.ShapeDtypeStruct((len(planes), BINS + HALF, width), jnp.bfloat16)
    return pl.pallas_call(
        functools.partial(halves_kernel, planes),
        in_specs=[
            pl.BlockSpec(memory_space=pl.ANY),
            pl.BlockSpec(memory_space=pl.ANY),
            pl.BlockSpec(memory_space=pltpu.VMEM),
        ],
        scratch_shapes=[
            pltpu.VMEM((len(planes), 2, 2 * STRADDLE, width), jnp.bfloat16),
            pltpu.SemaphoreType.DMA((len(planes), 2, STRADDLE // STEP + 1)),
        ],
        out_shape=[shape, shape],
        compiler_params=pltpu.CompilerParams(vmem_limit_bytes=LARGE),
        cost_estimate=free(),
        name="halves",
    )(data, lent, table)


def straddle_kernel(keep_ref, got_ref, table_ref, *refs):
    out_refs, scratch_ref = refs[:-1], refs[-1]
    side = position()[1] // 2
    for k, out_ref in enumerate(out_refs):
        out_ref[2 * side] = keep_ref[k, :BINS, :]
        out_ref[2 - 2 * side] = got_ref[k, :BINS, :]
        scratch_ref[k, pl.ds(pl.multiple_of(side * HALF, HALF), HALF), :] = keep_ref[k, BINS:, :]
        scratch_ref[k, pl.ds(pl.multiple_of((1 - side) * HALF, HALF), HALF), :] = got_ref[k, BINS:, :]
        out_ref[1] = transform(table_ref, scratch_ref[k])


def straddle(keep, got, table):
    planes, _, width = keep.shape
    shape = jax.ShapeDtypeStruct((SPLIT // TEAM, BINS, width), jnp.bfloat16)
    return pl.pallas_call(
        straddle_kernel,
        out_shape=[shape] * planes,
        scratch_shapes=[pltpu.VMEM((planes, SEGMENT_LENGTH, width), jnp.bfloat16)],
        compiler_params=pltpu.CompilerParams(vmem_limit_bytes=16 << 20),
        cost_estimate=free(),
        name="straddle",
    )(keep, got, table)


def pick_kernel(width, sources_ref, alive_ref, data_ref, *refs):
    out_refs, acc_ref, picked_ref = refs[:-2], refs[-2], refs[-1]
    step = pl.program_id(0)
    columns = data_ref.shape[1]
    lane = lax.broadcasted_iota(jnp.int32, (1, 128), 1)
    ids = jnp.full((1, 128), -1, jnp.int32)
    for q in range(SOURCES):
        ids = jnp.where(lane == q, sources_ref[q // SRC, q % SRC], ids)
    channel = lax.broadcasted_iota(jnp.int32, (columns, 128), 0)
    chosen = jnp.where(channel == ids - step * columns, 1.0, 0.0).astype(jnp.bfloat16)
    part = jnp.dot(data_ref[...], chosen, preferred_element_type=jnp.float32)

    @pl.when(step == 0)
    def _():
        acc_ref[...] = part

    @pl.when(step > 0)
    def _():
        acc_ref[...] += part

    @pl.when(step == pl.num_programs(0) - 1)
    def _():
        row = lax.broadcasted_iota(jnp.int32, (SOURCES, PACKED - HELD), 0)
        flags = jnp.zeros((SOURCES, PACKED - HELD), jnp.float32)
        for q in range(SOURCES):
            local = sources_ref[q // SRC, q % SRC] - lax.axis_index("chan") * width
            inside = (local >= 0) & (local < width)
            flag = jnp.where(inside, alive_ref[jnp.clip(local, 0, width - 1)], 0)
            flags = jnp.where(row == q, flag.astype(jnp.float32), flags)
        picked_ref[:, :HELD] = acc_ref[...].T[:SOURCES, :]
        picked_ref[:, HELD:] = flags
        for k, out_ref in enumerate(out_refs):
            start = pl.multiple_of((position()[1] ^ k) * SHARE, SHARE)
            out_ref[...] = picked_ref[pl.ds(start, SHARE), :].astype(jnp.bfloat16)


def pick(sources, alive, data, count):
    width = data.shape[1] // count
    columns = TEAM * width
    return pl.pallas_call(
        functools.partial(pick_kernel, width),
        grid=(count // TEAM,),
        in_specs=[
            pl.BlockSpec(memory_space=pltpu.SMEM),
            pl.BlockSpec(memory_space=pltpu.SMEM),
            pl.BlockSpec((HELD, columns), lambda i: (0, i)),
        ],
        out_specs=[pl.BlockSpec((SHARE, PACKED), lambda i: (0, 0))] * TEAM,
        scratch_shapes=[pltpu.VMEM((HELD, 128), jnp.float32), pltpu.VMEM((SOURCES, PACKED), jnp.float32)],
        out_shape=[jax.ShapeDtypeStruct((SHARE, PACKED), jnp.bfloat16)] * TEAM,
        compiler_params=pltpu.CompilerParams(vmem_limit_bytes=LARGE),
        cost_estimate=free(),
        name="pick",
    )(sources, alive, data)


def sources_kernel(*refs):
    picked_refs, table_ref, out_ref, samples_ref = refs[:TEAM], refs[TEAM], refs[TEAM + 1], refs[TEAM + 2]
    place = position()[1]
    flags = jnp.zeros((SHARE, PACKED - HELD), jnp.float32)
    for k, picked_ref in enumerate(picked_refs):
        picked = picked_ref[...].astype(jnp.float32)
        flags += picked[:, HELD:]
        samples_ref[:, pl.ds(pl.multiple_of((place ^ k) * HELD, 128), HELD)] = picked[:, :HELD]
    samples = [samples_ref[:, w * SEGMENT_LENGTH : (w + 1) * SEGMENT_LENGTH] for w in range(TEAM_WINDOWS)]
    spectra = lax.dot_general(
        jnp.concatenate(samples, axis=0).astype(jnp.bfloat16),
        table_ref[...],
        (((1,), (1,)), ((), ())),
        preferred_element_type=jnp.float32,
    )
    flags = jnp.concatenate([flags] * (BINS // 128), axis=1)
    out_ref[...] = jnp.concatenate([spectra, flags], axis=0).astype(jnp.bfloat16)


def source_spectra(picked, table):
    return pl.pallas_call(
        sources_kernel,
        scratch_shapes=[pltpu.VMEM((SHARE, TEAM * HELD), jnp.float32)],
        out_shape=jax.ShapeDtypeStruct(((TEAM_WINDOWS + 1) * SHARE, BINS), jnp.bfloat16),
        cost_estimate=free(),
        name="source_spectra",
    )(*picked, table)


def whiten_kernel(*refs):
    spectra_refs, out_ref, planes_ref = refs[:TEAM], refs[TEAM], refs[TEAM + 1]
    mine, _ = position()
    flags = jnp.zeros((SHARE, BINS), jnp.float32)
    for k, spectra_ref in enumerate(spectra_refs):
        spectra = spectra_ref[...].astype(jnp.float32)
        flags += spectra[TEAM_WINDOWS * SHARE :]
        planes_ref[mine ^ k] = spectra[: TEAM_WINDOWS * SHARE]
    spectra = planes_ref[...].reshape(SEGMENT_TALLY, SHARE, BINS)
    power = jnp.sum(jnp.square(spectra), axis=0)
    lane = lax.broadcasted_iota(jnp.int32, (SHARE, BINS), 1)
    other = jnp.where(lane % (2 * SUB) < SUB, pltpu.roll(power, BINS - SUB, 1), pltpu.roll(power, SUB, 1))
    level = (power + other) / SEGMENT_TALLY
    factor = flags / jnp.sqrt(level + 0.01)
    src = (spectra * factor[None]).astype(jnp.bfloat16).astype(jnp.float32)
    lane = lax.broadcasted_iota(jnp.int32, (SHARE, 128), 1) // (2 * SUB)
    each = 128 // (2 * SUB)
    for tile in range(TILES):
        half, at = divmod(tile, each)
        for group in range(DEPTH // 128):
            out = jnp.zeros((SHARE, 128), jnp.float32)
            for k in range(each):
                window = group * each + k
                if window < SEGMENT_TALLY:
                    piece = src[window, :, half * 128 : (half + 1) * 128]
                    shift = (k - at) * 2 * SUB % 128
                    piece = pltpu.roll(piece, shift, 1) if shift else piece
                    out = jnp.where(lane == k, piece, out)
            out_ref[tile, :, group * 128 : (group + 1) * 128] = out.astype(jnp.bfloat16)


def whiten(spectra):
    return pl.pallas_call(
        whiten_kernel,
        scratch_shapes=[pltpu.VMEM((TEAM, TEAM_WINDOWS * SHARE, BINS), jnp.float32)],
        out_shape=jax.ShapeDtypeStruct((TILES, SHARE, DEPTH), jnp.bfloat16),
        compiler_params=pltpu.CompilerParams(vmem_limit_bytes=16 << 20),
        cost_estimate=free(),
        name="whiten",
    )(*spectra)


def left_kernel(*refs):
    src_refs, left_ref = refs[:-1], refs[-1]
    src = jnp.concatenate([ref[0].astype(jnp.float32) for ref in src_refs], axis=0)
    lane = lax.broadcasted_iota(jnp.int32, (SOURCES, DEPTH), 1)
    turned = jnp.where(lane % (2 * SUB) < SUB, -pltpu.roll(src, DEPTH - SUB, 1), pltpu.roll(src, SUB, 1))
    row = lax.broadcasted_iota(jnp.int32, (1, 2 * SUB, DEPTH), 1)
    lane = lax.broadcasted_iota(jnp.int32, (1, 2 * SUB, DEPTH), 2)
    both = jnp.where(row < SUB, src[:, None, :], turned[:, None, :])
    both = jnp.where(lane % SUB == row % SUB, both, 0.0)
    left_ref[0] = both.reshape(SOURCES * 2 * SUB, DEPTH).astype(jnp.bfloat16)


def left_factor(src):
    return pl.pallas_call(
        left_kernel,
        grid=(TILES,),
        in_specs=[pl.BlockSpec((1, SHARE, DEPTH), lambda i: (i, 0, 0))] * TEAM,
        out_specs=pl.BlockSpec((1, SOURCES * 2 * SUB, DEPTH), lambda i: (i, 0, 0)),
        out_shape=jax.ShapeDtypeStruct((TILES, SOURCES * 2 * SUB, DEPTH), jnp.bfloat16),
        compiler_params=pltpu.CompilerParams(vmem_limit_bytes=16 << 20),
        cost_estimate=pl.CostEstimate(flops=0, bytes_accessed=1 << 20, transcendentals=0),
        name="left",
    )(*src)


def whiten_all(samples, alive, table):
    samples = samples.reshape(SOURCES, SEGMENT_TALLY, SEGMENT_LENGTH)
    spectra = jnp.einsum("qwt,kt->qwk", samples, table, preferred_element_type=jnp.float32)
    power = jnp.mean(spectra**2, axis=1).reshape(SOURCES, TILES, 2, SUB)
    level = power[:, :, :1] + power[:, :, 1:]
    factor = alive[:, None, None, None] / jnp.sqrt(level + 0.01)
    factor = jnp.broadcast_to(factor, (SOURCES, TILES, 2, SUB)).reshape(SOURCES, BINS)
    src = (spectra * factor[:, None, :]).astype(jnp.bfloat16)
    src = jnp.transpose(src.reshape(SOURCES, SEGMENT_TALLY, TILES, 2 * SUB), (2, 0, 1, 3))
    src = src.reshape(TILES, SOURCES, SEGMENT_TALLY * 2 * SUB)
    src = jnp.pad(src, ((0, 0), (0, 0), (0, DEPTH - SEGMENT_TALLY * 2 * SUB)))
    return [src[:, k * SHARE : (k + 1) * SHARE] for k in range(TEAM)]


BATCH = 8


def correlate_kernel(relative, left_ref, whole_ref, other_ref, *refs):
    split_refs, (alive_ref, inverse_ref, out_ref, right_ref, cross_ref, done_ref, sems) = refs[:TEAM], refs[TEAM:]
    mine, place = position() if relative else (0, 0)
    width = right_ref.shape[2]
    rows = 2 * SUB
    span = TEAM_WINDOWS * rows
    pad = DEPTH - SEGMENT_TALLY * rows
    alive = alive_ref[...].astype(jnp.float32)

    for index in range(TILES):
        tile = slice(index * rows, (index + 1) * rows)
        right_ref[index, DEPTH - pad :, :] = jnp.zeros((pad, width), jnp.bfloat16)
        for plane in range(TEAM):
            for core in range(2):
                at = plane * span + core * 2 * rows
                mine_at = pl.multiple_of(at + place // 2 * 4 * rows, rows)
                other_at = pl.multiple_of(at + (1 - place // 2) * 4 * rows, rows)
                right_ref[index, pl.ds(mine_at, rows), :] = whole_ref[plane * 2 + core, 0, tile, :]
                right_ref[index, pl.ds(other_at, rows), :] = other_ref[plane * 2 + core, tile, :]
            for j in range(SPLIT // TEAM):
                at = pl.multiple_of((plane ^ mine) * span + (2 * j + 1) * rows, rows)
                right_ref[index, pl.ds(at, rows), :] = split_refs[plane][j, tile, :]
        right = right_ref[index]
        power = jnp.square(right.astype(jnp.float32)).reshape(DEPTH // rows, rows, width)
        power = jnp.sum(power, axis=0)
        level = (power[:SUB] + power[SUB:]) / SEGMENT_TALLY
        factor = alive / jnp.sqrt(level + 0.01)
        factor = jnp.concatenate([factor, factor], axis=0)[None]
        cross = jnp.dot(left_ref[index], right, preferred_element_type=jnp.float32)
        cross = cross.reshape(SOURCES, rows, width)
        cross_ref[:, tile, :] = jnp.where(factor > 0.0, cross * factor, 0.0).astype(jnp.bfloat16)

    def copy(step):
        part = pl.ds(step * BATCH, BATCH)
        return pltpu.make_async_copy(done_ref.at[part], out_ref.at[part], sems.at[step])

    @pl.loop(0, SOURCES // BATCH)
    def _(step):
        for k in range(BATCH):
            index = step * BATCH + k
            held = (index // SHARE ^ place) * SHARE + index % SHARE
            lagged = jnp.dot(inverse_ref[...], cross_ref[held], preferred_element_type=jnp.float32)
            done_ref[index] = (lagged * (1.0 / math.sqrt(NF * SEGMENT_TALLY))).astype(jnp.bfloat16)
        copy(step).start()

    @pl.loop(0, SOURCES // BATCH)
    def _(step):
        copy(step).wait()


def correlate(relative, left, whole, other, split, alive, inverse):
    width = whole.shape[3]
    return pl.pallas_call(
        functools.partial(correlate_kernel, relative),
        out_specs=pl.BlockSpec(memory_space=pl.ANY),
        scratch_shapes=[
            pltpu.VMEM((TILES, DEPTH, width), jnp.bfloat16),
            pltpu.VMEM((SOURCES, BINS, width), jnp.bfloat16),
            pltpu.VMEM((SOURCES, LAGS, width), jnp.bfloat16),
            pltpu.SemaphoreType.DMA((SOURCES // BATCH,)),
        ],
        out_shape=jax.ShapeDtypeStruct((SOURCES, LAGS, width), jnp.bfloat16),
        compiler_params=pltpu.CompilerParams(vmem_limit_bytes=18 << 20),
        name="correlate",
    )(left, whole, other, *split, alive, inverse)


def body(data, alive, sources):
    count = lax.axis_size("chan")
    width = data.shape[1] // count
    table = forward_table()
    relative = data.shape[0] == HELD and count == TEAM * TEAM
    if relative:
        swap = lambda x, k: lax.ppermute(x, "chan", [(i, i ^ k) for i in range(count)])
        team = range(1, TEAM)
        across = [[z * TEAM + y * 2 + core for z in range(count // TEAM) for core in range(2)] for y in range(2)]
        whole = prepare(data, table, count)
        data, whole = lax.optimization_barrier((data, whole))
        lent = lend(data, count)
        data, lent = lax.optimization_barrier((data, lent))
        lent = swap(lent, 1)
        whole = lax.all_to_all(whole, "chan", 0, 0, tiled=True, axis_index_groups=across)
        picked = pick(sources, alive, data, count)
        data, picked = lax.optimization_barrier((data, picked))
        picked = [picked[0]] + [swap(picked[k], k) for k in team]
        spectra = source_spectra(picked, table)
        keep_far, give_far = halves((2, 3), data, lent, table, count)
        give_far, spectra, data = lax.optimization_barrier((give_far, spectra, data))
        arrived = [swap(spectra, k * TEAM) for k in team]
        keep_near, give_near = halves((0, 1), data, lent, table, count)
        far = straddle(keep_far, swap(give_far, 2), table)
        got_near = swap(give_near, 2)
        arrived, whole, far, got_near = lax.optimization_barrier((arrived, whole, far, got_near))
        other = regroup(whole)
        src = whiten([spectra] + arrived)
        keep_near, src, other = lax.optimization_barrier((keep_near, src, other))
        near = straddle(keep_near, got_near, table)
        other = swap(other, 2)
        src = [src] + [swap(src, k) for k in team]
        split = [near[0], swap(near[1], TEAM), swap(far[0], 2 * TEAM), swap(far[1], 3 * TEAM)]
    else:
        me = lax.axis_index("chan")
        ids = sources.reshape(-1)
        near = ids[:, None] == me * width + jnp.arange(width, dtype=jnp.int32)[None, :]
        flags = jnp.sum(jnp.where(near, alive[None, :], 0), axis=1).astype(jnp.float32)
        chosen = jnp.where(jnp.arange(data.shape[1], dtype=jnp.int32)[:, None] == ids[None, :], 1.0, 0.0)
        picked = jnp.dot(data, chosen.astype(jnp.bfloat16), preferred_element_type=jnp.float32)
        picked = lax.all_gather(picked.astype(jnp.bfloat16), "chan", axis=0)
        alive_sources = lax.psum(flags, "chan")
        blocks = data.reshape(data.shape[0], count, width)
        blocks = lax.all_to_all(blocks, "chan", split_axis=1, concat_axis=0, tiled=True)
        blocks = blocks.reshape(SEGMENT_TALLY, SEGMENT_LENGTH, width)
        spectra = jnp.einsum("kt,wtc->wkc", table, blocks, preferred_element_type=jnp.float32)
        spectra = spectra.astype(jnp.bfloat16).reshape(TEAM, TEAM_WINDOWS, BINS, width)
        whole = spectra[:, 0:3:2].reshape(2 * TEAM, 1, BINS, width)
        other = spectra[:, 4:7:2].reshape(2 * TEAM, BINS, width)
        split = [spectra[z, 1::2] for z in range(TEAM)]
        src = whiten_all(jnp.transpose(picked, (2, 0, 1)), alive_sources, table)
    left = left_factor(src)
    out = correlate(relative, left, whole, other, split, alive[None, :], inverse_table())
    return out.reshape(ROUNDS, SRC, LAGS, width)


def solution(mesh):
    return jax.shard_map(
        body,
        mesh=mesh,
        in_specs=(P(("groups", "chan"), None), P(("groups", "chan")), P()),
        out_specs=P("groups", None, None, "chan"),
        check_vma=False,
    )
```

```python
import functools
import math

import jax
import jax.numpy as jnp
import ml_dtypes
import numpy as np
from jax import lax
from jax.experimental import pallas as pl
from jax.experimental.pallas import tpu as pltpu
from jax.sharding import PartitionSpec as P

SEGMENT_LENGTH = 512
NF = 128
LAGS = 256
SRC = 16
ROUNDS = 2
SEGMENT_TALLY = 28

SOURCES = SRC * ROUNDS
BINS = 2 * NF
SUB = 8
TILES = NF // SUB
TEAM = 4
TEAM_WINDOWS = 7
STEP = 128
HELD = TEAM_WINDOWS * SEGMENT_LENGTH // TEAM
STRADDLE = HELD - SEGMENT_LENGTH
HALF = SEGMENT_LENGTH // 2
WHOLE = 16
SPLIT = 12
PACKED = 1024
SHARE = SOURCES // TEAM
DEPTH = 512
LARGE = 56 << 20


def angles(times):
    bins = np.arange(NF)[:, None] + 1
    turn = bins * times[None, :] % SEGMENT_LENGTH * (2.0 * np.pi / SEGMENT_LENGTH)
    table = np.stack([np.cos(turn), -np.sin(turn)])
    table = table.reshape(2, TILES, SUB, times.size).transpose(1, 0, 2, 3)
    return table.reshape(BINS, times.size)


def forward_table():
    table = angles(np.arange(SEGMENT_LENGTH)) / math.sqrt(SEGMENT_LENGTH)
    return jnp.asarray(table.astype(ml_dtypes.bfloat16))


def inverse_table():
    table = angles(np.arange(LAGS) - LAGS // 2)
    return jnp.asarray(np.ascontiguousarray(table.T).astype(ml_dtypes.bfloat16))


def position():
    me = lax.axis_index("chan")
    return me // TEAM, me % TEAM


def transform(table_ref, block):
    return jnp.dot(table_ref[...], block, preferred_element_type=jnp.float32).astype(jnp.bfloat16)


def free(size):
    return pl.CostEstimate(flops=0, bytes_accessed=0, transcendentals=0)


def window(data_ref, row, column, depth, width):
    row = pl.ds(pl.multiple_of(row, STEP), depth)
    return data_ref.at[row, pl.ds(pl.multiple_of(column, 128), width)]


def straddling(data_ref, j, place, column, width):
    row = jnp.where(j < place, j, j + SEGMENT_LENGTH // STEP) * STEP
    return window(data_ref, row, column * width, STEP, width)


def prepare_kernel(data_ref, rows_ref, whole_ref, block_ref, out_ref, table_ref, in_sems, out_sems, sem):
    _, place = position()
    planes, _, _, width = out_ref.shape
    copies = []
    table = pltpu.make_async_copy(rows_ref, table_ref, sem)
    table.start()
    for plane in range(planes):
        source = window(data_ref, place * STEP, plane * TEAM * width, SEGMENT_LENGTH, TEAM * width)
        copies.append(pltpu.make_async_copy(source, block_ref.at[plane], in_sems.at[plane]))
        copies[plane].start()
    table.wait()
    for plane in range(planes):
        copies[plane].wait()
        for member in range(TEAM):
            column = pl.ds(pl.multiple_of((place ^ member) * width, width), width)
            out_ref[plane, member] = transform(table_ref, block_ref[plane, :, column])
        copies.append(pltpu.make_async_copy(out_ref.at[plane], whole_ref.at[plane], out_sems.at[plane]))
        copies[-1].start()
    for copy in copies[planes:]:
        copy.wait()


def prepare(data, table, count):
    width = data.shape[1] // count
    planes = count // TEAM
    return pl.pallas_call(
        prepare_kernel,
        in_specs=[pl.BlockSpec(memory_space=pl.ANY)] * 2,
        scratch_shapes=[
            pltpu.VMEM((planes, SEGMENT_LENGTH, TEAM * width), jnp.bfloat16),
            pltpu.VMEM((planes, TEAM, BINS, width), jnp.bfloat16),
            pltpu.VMEM((BINS, SEGMENT_LENGTH), jnp.bfloat16),
            pltpu.SemaphoreType.DMA((planes,)),
            pltpu.SemaphoreType.DMA((planes,)),
            pltpu.SemaphoreType.DMA,
        ],
        out_specs=pl.BlockSpec(memory_space=pl.ANY),
        out_shape=jax.ShapeDtypeStruct((planes, TEAM, BINS, width), jnp.bfloat16),
        compiler_params=pltpu.CompilerParams(vmem_limit_bytes=LARGE),
        name="prepare",
    )(data, table)


def regroup_kernel(whole_ref, *out_refs):
    for member, out_ref in enumerate(out_refs, 1):
        out_ref[...] = whole_ref[:, member]


def regroup(whole):
    planes, _, rows, width = whole.shape
    return pl.pallas_call(
        regroup_kernel,
        out_shape=[jax.ShapeDtypeStruct((planes, rows, width), jnp.bfloat16)] * (TEAM - 1),
        compiler_params=pltpu.CompilerParams(vmem_limit_bytes=16 << 20),
        cost_estimate=free(1 << 20),
        name="regroup",
    )(whole)


def lend_kernel(data_ref, out_ref, sems):
    _, place = position()
    width = out_ref.shape[2]
    copies = []
    for target in range(out_ref.shape[0]):
        column = target // 2 * TEAM + target % 2 * 2 + 1 - place % 2
        for j in range(STRADDLE // STEP):
            source = straddling(data_ref, j, place, column, width)
            copy = pltpu.make_async_copy(source, out_ref.at[target, pl.ds(j * STEP, STEP)], sems.at[target, j])
            copy.start()
            copies.append(copy)
    for copy in copies:
        copy.wait()


def lend(data, count):
    width = data.shape[1] // count
    return pl.pallas_call(
        lend_kernel,
        in_specs=[pl.BlockSpec(memory_space=pl.ANY)],
        scratch_shapes=[pltpu.SemaphoreType.DMA((count // 2, STRADDLE // STEP))],
        out_shape=jax.ShapeDtypeStruct((count // 2, STRADDLE, width), jnp.bfloat16),
        compiler_params=pltpu.CompilerParams(vmem_limit_bytes=LARGE),
        cost_estimate=free(1 << 20),
        name="lend",
    )(data)


def halves_kernel(planes, data_ref, lent_ref, table_ref, keep_ref, give_ref, chip_ref, sems):
    mine, place = position()
    side, core = place // 2, place % 2
    width = keep_ref.shape[2]
    copies = []
    for i, k in enumerate(planes):
        plane = mine ^ k
        for t, target in enumerate((side, 1 - side)):
            for j in range(STRADDLE // STEP):
                source = straddling(data_ref, j, place, plane * TEAM + target * 2 + core, width)
                start = pl.multiple_of(core * STRADDLE + j * STEP, STEP)
                copies.append(pltpu.make_async_copy(source, chip_ref.at[i, t, pl.ds(start, STEP)], sems.at[i, t, j]))
            start = pl.multiple_of((1 - core) * STRADDLE, STEP)
            part = chip_ref.at[i, t, pl.ds(start, STRADDLE)]
            copies.append(pltpu.make_async_copy(lent_ref.at[plane * 2 + target], part, sems.at[i, t, STRADDLE // STEP]))
    for copy in copies:
        copy.start()
    for copy in copies:
        copy.wait()
    for i in range(len(planes)):
        for t, out_ref in enumerate((keep_ref, give_ref)):
            start = pl.multiple_of(side * HALF, HALF)
            out_ref[i, :BINS, :] = transform(table_ref, chip_ref[i, t, pl.ds(start, SEGMENT_LENGTH), :])
            start = pl.multiple_of((1 - side) * SEGMENT_LENGTH, HALF)
            out_ref[i, BINS:, :] = chip_ref[i, t, pl.ds(start, HALF), :]


def halves(planes, data, lent, table, count):
    width = data.shape[1] // count
    shape = jax.ShapeDtypeStruct((len(planes), BINS + HALF, width), jnp.bfloat16)
    return pl.pallas_call(
        functools.partial(halves_kernel, planes),
        in_specs=[
            pl.BlockSpec(memory_space=pl.ANY),
            pl.BlockSpec(memory_space=pl.ANY),
            pl.BlockSpec(memory_space=pltpu.VMEM),
        ],
        scratch_shapes=[
            pltpu.VMEM((len(planes), 2, 2 * STRADDLE, width), jnp.bfloat16),
            pltpu.SemaphoreType.DMA((len(planes), 2, STRADDLE // STEP + 1)),
        ],
        out_shape=[shape, shape],
        compiler_params=pltpu.CompilerParams(vmem_limit_bytes=LARGE),
        cost_estimate=free(1 << 20),
        name="halves",
    )(data, lent, table)


def straddle_kernel(keep_ref, got_ref, table_ref, *refs):
    out_refs, scratch_ref = refs[:-1], refs[-1]
    side = position()[1] // 2
    for k, out_ref in enumerate(out_refs):
        out_ref[2 * side] = keep_ref[k, :BINS, :]
        out_ref[2 - 2 * side] = got_ref[k, :BINS, :]
        scratch_ref[k, pl.ds(pl.multiple_of(side * HALF, HALF), HALF), :] = keep_ref[k, BINS:, :]
        scratch_ref[k, pl.ds(pl.multiple_of((1 - side) * HALF, HALF), HALF), :] = got_ref[k, BINS:, :]
        out_ref[1] = transform(table_ref, scratch_ref[k])


def straddle(keep, got, table):
    planes, _, width = keep.shape
    shape = jax.ShapeDtypeStruct((SPLIT // TEAM, BINS, width), jnp.bfloat16)
    return pl.pallas_call(
        straddle_kernel,
        out_shape=[shape] * planes,
        scratch_shapes=[pltpu.VMEM((planes, SEGMENT_LENGTH, width), jnp.bfloat16)],
        compiler_params=pltpu.CompilerParams(vmem_limit_bytes=16 << 20),
        cost_estimate=free(1 << 20),
        name="straddle",
    )(keep, got, table)


def pick_kernel(width, sources_ref, alive_ref, data_ref, *refs):
    out_refs, acc_ref, picked_ref = refs[:-2], refs[-2], refs[-1]
    step = pl.program_id(0)
    columns = data_ref.shape[1]
    lane = lax.broadcasted_iota(jnp.int32, (1, 128), 1)
    ids = jnp.full((1, 128), -1, jnp.int32)
    for q in range(SOURCES):
        ids = jnp.where(lane == q, sources_ref[q // SRC, q % SRC], ids)
    channel = lax.broadcasted_iota(jnp.int32, (columns, 128), 0)
    chosen = jnp.where(channel == ids - step * columns, 1.0, 0.0).astype(jnp.bfloat16)
    part = jnp.dot(data_ref[...], chosen, preferred_element_type=jnp.float32)

    @pl.when(step == 0)
    def _():
        acc_ref[...] = part

    @pl.when(step > 0)
    def _():
        acc_ref[...] += part

    @pl.when(step == pl.num_programs(0) - 1)
    def _():
        row = lax.broadcasted_iota(jnp.int32, (SOURCES, PACKED - HELD), 0)
        flags = jnp.zeros((SOURCES, PACKED - HELD), jnp.float32)
        for q in range(SOURCES):
            local = sources_ref[q // SRC, q % SRC] - lax.axis_index("chan") * width
            inside = (local >= 0) & (local < width)
            flag = jnp.where(inside, alive_ref[jnp.clip(local, 0, width - 1)], 0)
            flags = jnp.where(row == q, flag.astype(jnp.float32), flags)
        picked_ref[:, :HELD] = acc_ref[...].T[:SOURCES, :]
        picked_ref[:, HELD:] = flags
        for k, out_ref in enumerate(out_refs):
            start = pl.multiple_of((position()[1] ^ k) * SHARE, SHARE)
            out_ref[...] = picked_ref[pl.ds(start, SHARE), :].astype(jnp.bfloat16)


def pick(sources, alive, data, count):
    width = data.shape[1] // count
    columns = TEAM * width
    return pl.pallas_call(
        functools.partial(pick_kernel, width),
        grid=(count // TEAM,),
        in_specs=[
            pl.BlockSpec(memory_space=pltpu.SMEM),
            pl.BlockSpec(memory_space=pltpu.SMEM),
            pl.BlockSpec((HELD, columns), lambda i: (0, i)),
        ],
        out_specs=[pl.BlockSpec((SHARE, PACKED), lambda i: (0, 0))] * TEAM,
        scratch_shapes=[pltpu.VMEM((HELD, 128), jnp.float32), pltpu.VMEM((SOURCES, PACKED), jnp.float32)],
        out_shape=[jax.ShapeDtypeStruct((SHARE, PACKED), jnp.bfloat16)] * TEAM,
        compiler_params=pltpu.CompilerParams(vmem_limit_bytes=LARGE),
        cost_estimate=free(1 << 20),
        name="pick",
    )(sources, alive, data)


def sources_kernel(*refs):
    picked_refs, table_ref, out_ref, samples_ref = refs[:TEAM], refs[TEAM], refs[TEAM + 1], refs[TEAM + 2]
    place = position()[1]
    flags = jnp.zeros((SHARE, PACKED - HELD), jnp.float32)
    for k, picked_ref in enumerate(picked_refs):
        picked = picked_ref[...].astype(jnp.float32)
        flags += picked[:, HELD:]
        samples_ref[:, pl.ds(pl.multiple_of((place ^ k) * HELD, 128), HELD)] = picked[:, :HELD]
    samples = [samples_ref[:, w * SEGMENT_LENGTH : (w + 1) * SEGMENT_LENGTH] for w in range(TEAM_WINDOWS)]
    spectra = lax.dot_general(
        jnp.concatenate(samples, axis=0).astype(jnp.bfloat16),
        table_ref[...],
        (((1,), (1,)), ((), ())),
        preferred_element_type=jnp.float32,
    )
    flags = jnp.concatenate([flags] * (BINS // 128), axis=1)
    out_ref[...] = jnp.concatenate([spectra, flags], axis=0).astype(jnp.bfloat16)


def source_spectra(picked, table):
    return pl.pallas_call(
        sources_kernel,
        scratch_shapes=[pltpu.VMEM((SHARE, TEAM * HELD), jnp.float32)],
        out_shape=jax.ShapeDtypeStruct(((TEAM_WINDOWS + 1) * SHARE, BINS), jnp.bfloat16),
        cost_estimate=free(1 << 18),
        name="source_spectra",
    )(*picked, table)


def whiten_kernel(*refs):
    spectra_refs, out_ref, planes_ref = refs[:TEAM], refs[TEAM], refs[TEAM + 1]
    mine, _ = position()
    flags = jnp.zeros((SHARE, BINS), jnp.float32)
    for k, spectra_ref in enumerate(spectra_refs):
        spectra = spectra_ref[...].astype(jnp.float32)
        flags += spectra[TEAM_WINDOWS * SHARE :]
        planes_ref[mine ^ k] = spectra[: TEAM_WINDOWS * SHARE]
    spectra = planes_ref[...].reshape(SEGMENT_TALLY, SHARE, BINS)
    power = jnp.sum(jnp.square(spectra), axis=0)
    lane = lax.broadcasted_iota(jnp.int32, (SHARE, BINS), 1)
    other = jnp.where(lane % (2 * SUB) < SUB, pltpu.roll(power, BINS - SUB, 1), pltpu.roll(power, SUB, 1))
    level = (power + other) / SEGMENT_TALLY
    factor = flags / jnp.sqrt(level + 0.01)
    src = (spectra * factor[None]).astype(jnp.bfloat16).astype(jnp.float32)
    lane = lax.broadcasted_iota(jnp.int32, (SHARE, 128), 1) // (2 * SUB)
    each = 128 // (2 * SUB)
    for tile in range(TILES):
        half, at = divmod(tile, each)
        for group in range(DEPTH // 128):
            out = jnp.zeros((SHARE, 128), jnp.float32)
            for k in range(each):
                window = group * each + k
                if window < SEGMENT_TALLY:
                    piece = src[window, :, half * 128 : (half + 1) * 128]
                    shift = (k - at) * 2 * SUB % 128
                    piece = pltpu.roll(piece, shift, 1) if shift else piece
                    out = jnp.where(lane == k, piece, out)
            out_ref[tile, :, group * 128 : (group + 1) * 128] = out.astype(jnp.bfloat16)


def whiten(spectra):
    return pl.pallas_call(
        whiten_kernel,
        scratch_shapes=[pltpu.VMEM((TEAM, TEAM_WINDOWS * SHARE, BINS), jnp.float32)],
        out_shape=jax.ShapeDtypeStruct((TILES, SHARE, DEPTH), jnp.bfloat16),
        compiler_params=pltpu.CompilerParams(vmem_limit_bytes=16 << 20),
        cost_estimate=free(1 << 18),
        name="whiten",
    )(*spectra)


def left_kernel(*refs):
    src_refs, left_ref = refs[:-1], refs[-1]
    src = jnp.concatenate([ref[0].astype(jnp.float32) for ref in src_refs], axis=0)
    lane = lax.broadcasted_iota(jnp.int32, (SOURCES, DEPTH), 1)
    turned = jnp.where(lane % (2 * SUB) < SUB, -pltpu.roll(src, DEPTH - SUB, 1), pltpu.roll(src, SUB, 1))
    row = lax.broadcasted_iota(jnp.int32, (1, 2 * SUB, DEPTH), 1)
    lane = lax.broadcasted_iota(jnp.int32, (1, 2 * SUB, DEPTH), 2)
    both = jnp.where(row < SUB, src[:, None, :], turned[:, None, :])
    both = jnp.where(lane % SUB == row % SUB, both, 0.0)
    left_ref[0] = both.reshape(SOURCES * 2 * SUB, DEPTH).astype(jnp.bfloat16)


def left_factor(src):
    return pl.pallas_call(
        left_kernel,
        grid=(TILES,),
        in_specs=[pl.BlockSpec((1, SHARE, DEPTH), lambda i: (i, 0, 0))] * TEAM,
        out_specs=pl.BlockSpec((1, SOURCES * 2 * SUB, DEPTH), lambda i: (i, 0, 0)),
        out_shape=jax.ShapeDtypeStruct((TILES, SOURCES * 2 * SUB, DEPTH), jnp.bfloat16),
        compiler_params=pltpu.CompilerParams(vmem_limit_bytes=16 << 20),
        cost_estimate=pl.CostEstimate(flops=0, bytes_accessed=1 << 20, transcendentals=0),
        name="left",
    )(*src)


def whiten_all(samples, alive, table):
    samples = samples.reshape(SOURCES, SEGMENT_TALLY, SEGMENT_LENGTH)
    spectra = jnp.einsum("qwt,kt->qwk", samples, table, preferred_element_type=jnp.float32)
    power = jnp.mean(spectra**2, axis=1).reshape(SOURCES, TILES, 2, SUB)
    level = power[:, :, :1] + power[:, :, 1:]
    factor = alive[:, None, None, None] / jnp.sqrt(level + 0.01)
    factor = jnp.broadcast_to(factor, (SOURCES, TILES, 2, SUB)).reshape(SOURCES, BINS)
    src = (spectra * factor[:, None, :]).astype(jnp.bfloat16)
    src = jnp.transpose(src.reshape(SOURCES, SEGMENT_TALLY, TILES, 2 * SUB), (2, 0, 1, 3))
    src = src.reshape(TILES, SOURCES, SEGMENT_TALLY * 2 * SUB)
    src = jnp.pad(src, ((0, 0), (0, 0), (0, DEPTH - SEGMENT_TALLY * 2 * SUB)))
    return [src[:, k * SHARE : (k + 1) * SHARE] for k in range(TEAM)]


BATCH = 8


def correlate_kernel(relative, left_ref, whole_ref, *refs):
    other_refs, split_refs = refs[: TEAM - 1], refs[TEAM - 1 : 2 * TEAM - 1]
    alive_ref, inverse_ref, out_ref, right_ref, cross_ref, done_ref, sems = refs[2 * TEAM - 1 :]
    mine, place = position() if relative else (0, 0)
    width = right_ref.shape[2]
    rows = 2 * SUB
    span = TEAM_WINDOWS * rows
    pad = DEPTH - SEGMENT_TALLY * rows
    alive = alive_ref[...].astype(jnp.float32)

    for index in range(TILES):
        tile = slice(index * rows, (index + 1) * rows)
        right_ref[index, DEPTH - pad :, :] = jnp.zeros((pad, width), jnp.bfloat16)
        for plane in range(TEAM):
            for member in range(TEAM):
                at = pl.multiple_of(plane * span + (member ^ place) * 2 * rows, rows)
                piece = other_refs[member - 1][plane, tile, :] if member else whole_ref[plane, 0, tile, :]
                right_ref[index, pl.ds(at, rows), :] = piece
            for j in range(SPLIT // TEAM):
                at = pl.multiple_of((plane ^ mine) * span + (2 * j + 1) * rows, rows)
                right_ref[index, pl.ds(at, rows), :] = split_refs[plane][j, tile, :]
        right = right_ref[index]
        power = jnp.square(right.astype(jnp.float32)).reshape(DEPTH // rows, rows, width)
        power = jnp.sum(power, axis=0)
        level = (power[:SUB] + power[SUB:]) / SEGMENT_TALLY
        factor = alive / jnp.sqrt(level + 0.01)
        factor = jnp.concatenate([factor, factor], axis=0)[None]
        cross = jnp.dot(left_ref[index], right, preferred_element_type=jnp.float32)
        cross = cross.reshape(SOURCES, rows, width)
        cross_ref[:, tile, :] = jnp.where(factor > 0.0, cross * factor, 0.0).astype(jnp.bfloat16)

    def copy(step):
        part = pl.ds(step * BATCH, BATCH)
        return pltpu.make_async_copy(done_ref.at[part], out_ref.at[part], sems.at[step])

    @pl.loop(0, SOURCES // BATCH)
    def _(step):
        for k in range(BATCH):
            index = step * BATCH + k
            held = (index // SHARE ^ place) * SHARE + index % SHARE
            lagged = jnp.dot(inverse_ref[...], cross_ref[held], preferred_element_type=jnp.float32)
            done_ref[index] = (lagged * (1.0 / math.sqrt(NF * SEGMENT_TALLY))).astype(jnp.bfloat16)
        copy(step).start()

    @pl.loop(0, SOURCES // BATCH)
    def _(step):
        copy(step).wait()


def correlate(relative, left, whole, others, split, alive, inverse):
    width = whole.shape[3]
    return pl.pallas_call(
        functools.partial(correlate_kernel, relative),
        out_specs=pl.BlockSpec(memory_space=pl.ANY),
        scratch_shapes=[
            pltpu.VMEM((TILES, DEPTH, width), jnp.bfloat16),
            pltpu.VMEM((SOURCES, BINS, width), jnp.bfloat16),
            pltpu.VMEM((SOURCES, LAGS, width), jnp.bfloat16),
            pltpu.SemaphoreType.DMA((SOURCES // BATCH,)),
        ],
        out_shape=jax.ShapeDtypeStruct((SOURCES, LAGS, width), jnp.bfloat16),
        compiler_params=pltpu.CompilerParams(vmem_limit_bytes=18 << 20),
        name="correlate",
    )(left, whole, *others, *split, alive, inverse)


def body(data, alive, sources):
    count = lax.axis_size("chan")
    width = data.shape[1] // count
    table = forward_table()
    relative = data.shape[0] == HELD and count == TEAM * TEAM
    if relative:
        swap = lambda x, k: lax.ppermute(x, "chan", [(i, i ^ k) for i in range(count)])
        team = range(1, TEAM)
        across = [[z * TEAM + p for z in range(count // TEAM)] for p in range(TEAM)]
        whole = prepare(data, table, count)
        data, whole = lax.optimization_barrier((data, whole))
        lent = lend(data, count)
        data, lent = lax.optimization_barrier((data, lent))
        lent = swap(lent, 1)
        whole = lax.all_to_all(whole, "chan", 0, 0, tiled=True, axis_index_groups=across)
        picked = pick(sources, alive, data, count)
        data, picked = lax.optimization_barrier((data, picked))
        picked = [picked[0]] + [swap(picked[k], k) for k in team]
        spectra = source_spectra(picked, table)
        keep_far, give_far = halves((2, 3), data, lent, table, count)
        give_far, spectra, data = lax.optimization_barrier((give_far, spectra, data))
        arrived = [swap(spectra, k * TEAM) for k in team]
        keep_near, give_near = halves((0, 1), data, lent, table, count)
        far = straddle(keep_far, swap(give_far, 2), table)
        arrived, whole, far = lax.optimization_barrier((arrived, whole, far))
        others = regroup(whole)
        src = whiten([spectra] + arrived)
        keep_near, others = lax.optimization_barrier((keep_near, others))
        others = [swap(others[k - 1], k) for k in team]
        near = straddle(keep_near, swap(give_near, 2), table)
        split = [near[0], swap(near[1], TEAM), swap(far[0], 2 * TEAM), swap(far[1], 3 * TEAM)]
        src = [src] + [swap(src, k) for k in team]
    else:
        me = lax.axis_index("chan")
        ids = sources.reshape(-1)
        near = ids[:, None] == me * width + jnp.arange(width, dtype=jnp.int32)[None, :]
        flags = jnp.sum(jnp.where(near, alive[None, :], 0), axis=1).astype(jnp.float32)
        chosen = jnp.where(jnp.arange(data.shape[1], dtype=jnp.int32)[:, None] == ids[None, :], 1.0, 0.0)
        picked = jnp.dot(data, chosen.astype(jnp.bfloat16), preferred_element_type=jnp.float32)
        picked = lax.all_gather(picked.astype(jnp.bfloat16), "chan", axis=0)
        alive_sources = lax.psum(flags, "chan")
        blocks = data.reshape(data.shape[0], count, width)
        blocks = lax.all_to_all(blocks, "chan", split_axis=1, concat_axis=0, tiled=True)
        blocks = blocks.reshape(SEGMENT_TALLY, SEGMENT_LENGTH, width)
        spectra = jnp.einsum("kt,wtc->wkc", table, blocks, preferred_element_type=jnp.float32)
        spectra = spectra.astype(jnp.bfloat16).reshape(TEAM, TEAM_WINDOWS, BINS, width)
        whole = spectra[:, 0:1]
        others = [spectra[:, 2 * k] for k in range(1, TEAM)]
        split = [spectra[z, 1::2] for z in range(TEAM)]
        src = whiten_all(jnp.transpose(picked, (2, 0, 1)), alive_sources, table)
    left = left_factor(src)
    out = correlate(relative, left, whole, others, split, alive[None, :], inverse_table())
    return out.reshape(ROUNDS, SRC, LAGS, width)


def solution(mesh):
    return jax.shard_map(
        body,
        mesh=mesh,
        in_specs=(P(("groups", "chan"), None), P(("groups", "chan")), P()),
        out_specs=P("groups", None, None, "chan"),
        check_vma=False,
    )
```

```python
import functools
import math

import jax
import jax.numpy as jnp
import ml_dtypes
import numpy as np
from jax import lax
from jax.experimental import pallas as pl
from jax.experimental.pallas import tpu as pltpu
from jax.sharding import PartitionSpec as P

SEGMENT_LENGTH = 512
NF = 128
LAGS = 256
SRC = 16
ROUNDS = 2
SEGMENT_TALLY = 28

SOURCES = SRC * ROUNDS
BINS = 2 * NF
SUB = 8
TILES = NF // SUB
TEAM = 4
TEAM_WINDOWS = 7
STEP = 128
HELD = TEAM_WINDOWS * SEGMENT_LENGTH // TEAM
STRADDLE = HELD - SEGMENT_LENGTH
HALF = SEGMENT_LENGTH // 2
WHOLE = 16
SPLIT = 12
PACKED = 1024
SHARE = SOURCES // TEAM
DEPTH = 512
LARGE = 56 << 20


def angles(times):
    bins = np.arange(NF)[:, None] + 1
    turn = bins * times[None, :] % SEGMENT_LENGTH * (2.0 * np.pi / SEGMENT_LENGTH)
    table = np.stack([np.cos(turn), -np.sin(turn)])
    table = table.reshape(2, TILES, SUB, times.size).transpose(1, 0, 2, 3)
    return table.reshape(BINS, times.size)


def forward_table():
    table = angles(np.arange(SEGMENT_LENGTH)) / math.sqrt(SEGMENT_LENGTH)
    return jnp.asarray(table.astype(ml_dtypes.bfloat16))


def inverse_table():
    table = angles(np.arange(LAGS) - LAGS // 2)
    return jnp.asarray(np.ascontiguousarray(table.T).astype(ml_dtypes.bfloat16))


def position():
    me = lax.axis_index("chan")
    return me // TEAM, me % TEAM


def transform(table_ref, block):
    return jnp.dot(table_ref[...], block, preferred_element_type=jnp.float32).astype(jnp.bfloat16)


def free(size):
    return pl.CostEstimate(flops=0, bytes_accessed=0, transcendentals=0)


def window(data_ref, row, column, depth, width):
    row = pl.ds(pl.multiple_of(row, STEP), depth)
    return data_ref.at[row, pl.ds(pl.multiple_of(column, 128), width)]


def straddling(data_ref, j, place, column, width):
    row = jnp.where(j < place, j, j + SEGMENT_LENGTH // STEP) * STEP
    return window(data_ref, row, column * width, STEP, width)


def prepare_kernel(data_ref, rows_ref, whole_ref, block_ref, out_ref, table_ref, in_sems, out_sems, sem):
    _, place = position()
    planes, _, _, width = out_ref.shape
    copies = []
    table = pltpu.make_async_copy(rows_ref, table_ref, sem)
    table.start()
    for plane in range(planes):
        source = window(data_ref, place * STEP, plane * TEAM * width, SEGMENT_LENGTH, TEAM * width)
        copies.append(pltpu.make_async_copy(source, block_ref.at[plane], in_sems.at[plane]))
        copies[plane].start()
    table.wait()
    for plane in range(planes):
        copies[plane].wait()
        for member in range(TEAM):
            column = pl.ds(pl.multiple_of((place ^ member) * width, width), width)
            out_ref[plane, member] = transform(table_ref, block_ref[plane, :, column])
        copies.append(pltpu.make_async_copy(out_ref.at[plane], whole_ref.at[plane], out_sems.at[plane]))
        copies[-1].start()
    for copy in copies[planes:]:
        copy.wait()


def prepare(data, table, count):
    width = data.shape[1] // count
    planes = count // TEAM
    return pl.pallas_call(
        prepare_kernel,
        in_specs=[pl.BlockSpec(memory_space=pl.ANY)] * 2,
        scratch_shapes=[
            pltpu.VMEM((planes, SEGMENT_LENGTH, TEAM * width), jnp.bfloat16),
            pltpu.VMEM((planes, TEAM, BINS, width), jnp.bfloat16),
            pltpu.VMEM((BINS, SEGMENT_LENGTH), jnp.bfloat16),
            pltpu.SemaphoreType.DMA((planes,)),
            pltpu.SemaphoreType.DMA((planes,)),
            pltpu.SemaphoreType.DMA,
        ],
        out_specs=pl.BlockSpec(memory_space=pl.ANY),
        out_shape=jax.ShapeDtypeStruct((planes, TEAM, BINS, width), jnp.bfloat16),
        compiler_params=pltpu.CompilerParams(vmem_limit_bytes=LARGE),
        name="prepare",
    )(data, table)


def regroup_kernel(whole_ref, *out_refs):
    for member, out_ref in enumerate(out_refs, 1):
        out_ref[...] = whole_ref[:, member]


def regroup(whole):
    planes, _, rows, width = whole.shape
    return pl.pallas_call(
        regroup_kernel,
        out_shape=[jax.ShapeDtypeStruct((planes, rows, width), jnp.bfloat16)] * (TEAM - 1),
        compiler_params=pltpu.CompilerParams(vmem_limit_bytes=16 << 20),
        cost_estimate=free(1 << 20),
        name="regroup",
    )(whole)


def lend_kernel(data_ref, out_ref, sems):
    _, place = position()
    width = out_ref.shape[2]
    copies = []
    for target in range(out_ref.shape[0]):
        column = target // 2 * TEAM + target % 2 * 2 + 1 - place % 2
        for j in range(STRADDLE // STEP):
            source = straddling(data_ref, j, place, column, width)
            copy = pltpu.make_async_copy(source, out_ref.at[target, pl.ds(j * STEP, STEP)], sems.at[target, j])
            copy.start()
            copies.append(copy)
    for copy in copies:
        copy.wait()


def lend(data, count):
    width = data.shape[1] // count
    return pl.pallas_call(
        lend_kernel,
        in_specs=[pl.BlockSpec(memory_space=pl.ANY)],
        scratch_shapes=[pltpu.SemaphoreType.DMA((count // 2, STRADDLE // STEP))],
        out_shape=jax.ShapeDtypeStruct((count // 2, STRADDLE, width), jnp.bfloat16),
        compiler_params=pltpu.CompilerParams(vmem_limit_bytes=LARGE),
        cost_estimate=free(1 << 20),
        name="lend",
    )(data)


def halves_kernel(planes, data_ref, lent_ref, table_ref, keep_ref, give_ref, chip_ref, sems):
    mine, place = position()
    side, core = place // 2, place % 2
    width = keep_ref.shape[2]
    copies = []
    for i, k in enumerate(planes):
        plane = mine ^ k
        for t, target in enumerate((side, 1 - side)):
            for j in range(STRADDLE // STEP):
                source = straddling(data_ref, j, place, plane * TEAM + target * 2 + core, width)
                start = pl.multiple_of(core * STRADDLE + j * STEP, STEP)
                copies.append(pltpu.make_async_copy(source, chip_ref.at[i, t, pl.ds(start, STEP)], sems.at[i, t, j]))
            start = pl.multiple_of((1 - core) * STRADDLE, STEP)
            part = chip_ref.at[i, t, pl.ds(start, STRADDLE)]
            copies.append(pltpu.make_async_copy(lent_ref.at[plane * 2 + target], part, sems.at[i, t, STRADDLE // STEP]))
    for copy in copies:
        copy.start()
    for copy in copies:
        copy.wait()
    for i in range(len(planes)):
        for t, out_ref in enumerate((keep_ref, give_ref)):
            start = pl.multiple_of(side * HALF, HALF)
            out_ref[i, :BINS, :] = transform(table_ref, chip_ref[i, t, pl.ds(start, SEGMENT_LENGTH), :])
            start = pl.multiple_of((1 - side) * SEGMENT_LENGTH, HALF)
            out_ref[i, BINS:, :] = chip_ref[i, t, pl.ds(start, HALF), :]


def halves(planes, data, lent, table, count):
    width = data.shape[1] // count
    shape = jax.ShapeDtypeStruct((len(planes), BINS + HALF, width), jnp.bfloat16)
    return pl.pallas_call(
        functools.partial(halves_kernel, planes),
        in_specs=[
            pl.BlockSpec(memory_space=pl.ANY),
            pl.BlockSpec(memory_space=pl.ANY),
            pl.BlockSpec(memory_space=pltpu.VMEM),
        ],
        scratch_shapes=[
            pltpu.VMEM((len(planes), 2, 2 * STRADDLE, width), jnp.bfloat16),
            pltpu.SemaphoreType.DMA((len(planes), 2, STRADDLE // STEP + 1)),
        ],
        out_shape=[shape, shape],
        compiler_params=pltpu.CompilerParams(vmem_limit_bytes=LARGE),
        cost_estimate=free(1 << 20),
        name="halves",
    )(data, lent, table)


def straddle_kernel(keep_ref, got_ref, table_ref, *refs):
    out_refs, scratch_ref = refs[:-1], refs[-1]
    side = position()[1] // 2
    for k, out_ref in enumerate(out_refs):
        out_ref[2 * side] = keep_ref[k, :BINS, :]
        out_ref[2 - 2 * side] = got_ref[k, :BINS, :]
        scratch_ref[k, pl.ds(pl.multiple_of(side * HALF, HALF), HALF), :] = keep_ref[k, BINS:, :]
        scratch_ref[k, pl.ds(pl.multiple_of((1 - side) * HALF, HALF), HALF), :] = got_ref[k, BINS:, :]
        out_ref[1] = transform(table_ref, scratch_ref[k])


def straddle(keep, got, table):
    planes, _, width = keep.shape
    shape = jax.ShapeDtypeStruct((SPLIT // TEAM, BINS, width), jnp.bfloat16)
    return pl.pallas_call(
        straddle_kernel,
        out_shape=[shape] * planes,
        scratch_shapes=[pltpu.VMEM((planes, SEGMENT_LENGTH, width), jnp.bfloat16)],
        compiler_params=pltpu.CompilerParams(vmem_limit_bytes=16 << 20),
        cost_estimate=free(1 << 20),
        name="straddle",
    )(keep, got, table)


def pick_kernel(width, sources_ref, alive_ref, data_ref, *refs):
    out_refs, acc_ref, picked_ref = refs[:-2], refs[-2], refs[-1]
    step = pl.program_id(0)
    columns = data_ref.shape[1]
    lane = lax.broadcasted_iota(jnp.int32, (1, 128), 1)
    ids = jnp.full((1, 128), -1, jnp.int32)
    for q in range(SOURCES):
        ids = jnp.where(lane == q, sources_ref[q // SRC, q % SRC], ids)
    channel = lax.broadcasted_iota(jnp.int32, (columns, 128), 0)
    chosen = jnp.where(channel == ids - step * columns, 1.0, 0.0).astype(jnp.bfloat16)
    part = jnp.dot(data_ref[...], chosen, preferred_element_type=jnp.float32)

    @pl.when(step == 0)
    def _():
        acc_ref[...] = part

    @pl.when(step > 0)
    def _():
        acc_ref[...] += part

    @pl.when(step == pl.num_programs(0) - 1)
    def _():
        row = lax.broadcasted_iota(jnp.int32, (SOURCES, PACKED - HELD), 0)
        flags = jnp.zeros((SOURCES, PACKED - HELD), jnp.float32)
        for q in range(SOURCES):
            local = sources_ref[q // SRC, q % SRC] - lax.axis_index("chan") * width
            inside = (local >= 0) & (local < width)
            flag = jnp.where(inside, alive_ref[jnp.clip(local, 0, width - 1)], 0)
            flags = jnp.where(row == q, flag.astype(jnp.float32), flags)
        picked_ref[:, :HELD] = acc_ref[...].T[:SOURCES, :]
        picked_ref[:, HELD:] = flags
        for k, out_ref in enumerate(out_refs):
            start = pl.multiple_of((position()[1] ^ k) * SHARE, SHARE)
            out_ref[...] = picked_ref[pl.ds(start, SHARE), :].astype(jnp.bfloat16)


def pick(sources, alive, data, count):
    width = data.shape[1] // count
    columns = TEAM * width
    return pl.pallas_call(
        functools.partial(pick_kernel, width),
        grid=(count // TEAM,),
        in_specs=[
            pl.BlockSpec(memory_space=pltpu.SMEM),
            pl.BlockSpec(memory_space=pltpu.SMEM),
            pl.BlockSpec((HELD, columns), lambda i: (0, i)),
        ],
        out_specs=[pl.BlockSpec((SHARE, PACKED), lambda i: (0, 0))] * TEAM,
        scratch_shapes=[pltpu.VMEM((HELD, 128), jnp.float32), pltpu.VMEM((SOURCES, PACKED), jnp.float32)],
        out_shape=[jax.ShapeDtypeStruct((SHARE, PACKED), jnp.bfloat16)] * TEAM,
        compiler_params=pltpu.CompilerParams(vmem_limit_bytes=LARGE),
        cost_estimate=free(1 << 20),
        name="pick",
    )(sources, alive, data)


def sources_kernel(*refs):
    picked_refs, table_ref, out_ref, samples_ref = refs[:TEAM], refs[TEAM], refs[TEAM + 1], refs[TEAM + 2]
    place = position()[1]
    flags = jnp.zeros((SHARE, PACKED - HELD), jnp.float32)
    for k, picked_ref in enumerate(picked_refs):
        picked = picked_ref[...].astype(jnp.float32)
        flags += picked[:, HELD:]
        samples_ref[:, pl.ds(pl.multiple_of((place ^ k) * HELD, 128), HELD)] = picked[:, :HELD]
    samples = [samples_ref[:, w * SEGMENT_LENGTH : (w + 1) * SEGMENT_LENGTH] for w in range(TEAM_WINDOWS)]
    spectra = lax.dot_general(
        jnp.concatenate(samples, axis=0).astype(jnp.bfloat16),
        table_ref[...],
        (((1,), (1,)), ((), ())),
        preferred_element_type=jnp.float32,
    )
    flags = jnp.concatenate([flags] * (BINS // 128), axis=1)
    out_ref[...] = jnp.concatenate([spectra, flags], axis=0).astype(jnp.bfloat16)


def source_spectra(picked, table):
    return pl.pallas_call(
        sources_kernel,
        scratch_shapes=[pltpu.VMEM((SHARE, TEAM * HELD), jnp.float32)],
        out_shape=jax.ShapeDtypeStruct(((TEAM_WINDOWS + 1) * SHARE, BINS), jnp.bfloat16),
        cost_estimate=free(1 << 18),
        name="source_spectra",
    )(*picked, table)


def whiten_kernel(*refs):
    spectra_refs, out_ref, planes_ref = refs[:TEAM], refs[TEAM], refs[TEAM + 1]
    mine, _ = position()
    flags = jnp.zeros((SHARE, BINS), jnp.float32)
    for k, spectra_ref in enumerate(spectra_refs):
        spectra = spectra_ref[...].astype(jnp.float32)
        flags += spectra[TEAM_WINDOWS * SHARE :]
        planes_ref[mine ^ k] = spectra[: TEAM_WINDOWS * SHARE]
    spectra = planes_ref[...].reshape(SEGMENT_TALLY, SHARE, BINS)
    power = jnp.sum(jnp.square(spectra), axis=0)
    lane = lax.broadcasted_iota(jnp.int32, (SHARE, BINS), 1)
    other = jnp.where(lane % (2 * SUB) < SUB, pltpu.roll(power, BINS - SUB, 1), pltpu.roll(power, SUB, 1))
    level = (power + other) / SEGMENT_TALLY
    factor = flags / jnp.sqrt(level + 0.01)
    src = (spectra * factor[None]).astype(jnp.bfloat16).astype(jnp.float32)
    lane = lax.broadcasted_iota(jnp.int32, (SHARE, 128), 1) // (2 * SUB)
    each = 128 // (2 * SUB)
    for tile in range(TILES):
        half, at = divmod(tile, each)
        for group in range(DEPTH // 128):
            out = jnp.zeros((SHARE, 128), jnp.float32)
            for k in range(each):
                window = group * each + k
                if window < SEGMENT_TALLY:
                    piece = src[window, :, half * 128 : (half + 1) * 128]
                    shift = (k - at) * 2 * SUB % 128
                    piece = pltpu.roll(piece, shift, 1) if shift else piece
                    out = jnp.where(lane == k, piece, out)
            out_ref[tile, :, group * 128 : (group + 1) * 128] = out.astype(jnp.bfloat16)


def whiten(spectra):
    return pl.pallas_call(
        whiten_kernel,
        scratch_shapes=[pltpu.VMEM((TEAM, TEAM_WINDOWS * SHARE, BINS), jnp.float32)],
        out_shape=jax.ShapeDtypeStruct((TILES, SHARE, DEPTH), jnp.bfloat16),
        compiler_params=pltpu.CompilerParams(vmem_limit_bytes=16 << 20),
        cost_estimate=free(1 << 18),
        name="whiten",
    )(*spectra)


def left_kernel(*refs):
    src_refs, left_ref = refs[:-1], refs[-1]
    src = jnp.concatenate([ref[0].astype(jnp.float32) for ref in src_refs], axis=0)
    lane = lax.broadcasted_iota(jnp.int32, (SOURCES, DEPTH), 1)
    turned = jnp.where(lane % (2 * SUB) < SUB, -pltpu.roll(src, DEPTH - SUB, 1), pltpu.roll(src, SUB, 1))
    row = lax.broadcasted_iota(jnp.int32, (1, 2 * SUB, DEPTH), 1)
    lane = lax.broadcasted_iota(jnp.int32, (1, 2 * SUB, DEPTH), 2)
    both = jnp.where(row < SUB, src[:, None, :], turned[:, None, :])
    both = jnp.where(lane % SUB == row % SUB, both, 0.0)
    left_ref[0] = both.reshape(SOURCES * 2 * SUB, DEPTH).astype(jnp.bfloat16)


def left_factor(src):
    return pl.pallas_call(
        left_kernel,
        grid=(TILES,),
        in_specs=[pl.BlockSpec((1, SHARE, DEPTH), lambda i: (i, 0, 0))] * TEAM,
        out_specs=pl.BlockSpec((1, SOURCES * 2 * SUB, DEPTH), lambda i: (i, 0, 0)),
        out_shape=jax.ShapeDtypeStruct((TILES, SOURCES * 2 * SUB, DEPTH), jnp.bfloat16),
        compiler_params=pltpu.CompilerParams(vmem_limit_bytes=16 << 20),
        cost_estimate=pl.CostEstimate(flops=0, bytes_accessed=1 << 20, transcendentals=0),
        name="left",
    )(*src)


def whiten_all(samples, alive, table):
    samples = samples.reshape(SOURCES, SEGMENT_TALLY, SEGMENT_LENGTH)
    spectra = jnp.einsum("qwt,kt->qwk", samples, table, preferred_element_type=jnp.float32)
    power = jnp.mean(spectra**2, axis=1).reshape(SOURCES, TILES, 2, SUB)
    level = power[:, :, :1] + power[:, :, 1:]
    factor = alive[:, None, None, None] / jnp.sqrt(level + 0.01)
    factor = jnp.broadcast_to(factor, (SOURCES, TILES, 2, SUB)).reshape(SOURCES, BINS)
    src = (spectra * factor[:, None, :]).astype(jnp.bfloat16)
    src = jnp.transpose(src.reshape(SOURCES, SEGMENT_TALLY, TILES, 2 * SUB), (2, 0, 1, 3))
    src = src.reshape(TILES, SOURCES, SEGMENT_TALLY * 2 * SUB)
    src = jnp.pad(src, ((0, 0), (0, 0), (0, DEPTH - SEGMENT_TALLY * 2 * SUB)))
    return [src[:, k * SHARE : (k + 1) * SHARE] for k in range(TEAM)]


BATCH = 8


def correlate_kernel(relative, left_ref, whole_ref, *refs):
    other_refs, split_refs = refs[: TEAM - 1], refs[TEAM - 1 : 2 * TEAM - 1]
    alive_ref, inverse_ref, out_ref, right_ref, cross_ref, done_ref, sems = refs[2 * TEAM - 1 :]
    mine, place = position() if relative else (0, 0)
    width = right_ref.shape[2]
    rows = 2 * SUB
    span = TEAM_WINDOWS * rows
    pad = DEPTH - SEGMENT_TALLY * rows
    alive = alive_ref[...].astype(jnp.float32)

    for index in range(TILES):
        tile = slice(index * rows, (index + 1) * rows)
        right_ref[index, DEPTH - pad :, :] = jnp.zeros((pad, width), jnp.bfloat16)
        for plane in range(TEAM):
            for member in range(TEAM):
                at = pl.multiple_of(plane * span + (member ^ place) * 2 * rows, rows)
                piece = other_refs[member - 1][plane, tile, :] if member else whole_ref[plane, 0, tile, :]
                right_ref[index, pl.ds(at, rows), :] = piece
            for j in range(SPLIT // TEAM):
                at = pl.multiple_of((plane ^ mine) * span + (2 * j + 1) * rows, rows)
                right_ref[index, pl.ds(at, rows), :] = split_refs[plane][j, tile, :]
        right = right_ref[index]
        held = right[: DEPTH - pad].astype(jnp.float32)
        power = jnp.square(held).reshape(SEGMENT_TALLY, rows, width)
        power = jnp.sum(power, axis=0)
        level = (power[:SUB] + power[SUB:]) / SEGMENT_TALLY
        factor = alive / jnp.sqrt(level + 0.01)
        factor = jnp.concatenate([factor, factor], axis=0)[None]
        cross = jnp.dot(left_ref[index], right, preferred_element_type=jnp.float32)
        cross = cross.reshape(SOURCES, rows, width)
        cross_ref[:, tile, :] = jnp.where(factor > 0.0, cross * factor, 0.0).astype(jnp.bfloat16)

    def copy(step):
        part = pl.ds(step * BATCH, BATCH)
        return pltpu.make_async_copy(done_ref.at[part], out_ref.at[part], sems.at[step])

    @pl.loop(0, SOURCES // BATCH)
    def _(step):
        for k in range(BATCH):
            index = step * BATCH + k
            held = (index // SHARE ^ place) * SHARE + index % SHARE
            lagged = jnp.dot(inverse_ref[...], cross_ref[held], preferred_element_type=jnp.float32)
            done_ref[index] = (lagged * (1.0 / math.sqrt(NF * SEGMENT_TALLY))).astype(jnp.bfloat16)
        copy(step).start()

    @pl.loop(0, SOURCES // BATCH)
    def _(step):
        copy(step).wait()


def correlate(relative, left, whole, others, split, alive, inverse):
    width = whole.shape[3]
    return pl.pallas_call(
        functools.partial(correlate_kernel, relative),
        out_specs=pl.BlockSpec(memory_space=pl.ANY),
        scratch_shapes=[
            pltpu.VMEM((TILES, DEPTH, width), jnp.bfloat16),
            pltpu.VMEM((SOURCES, BINS, width), jnp.bfloat16),
            pltpu.VMEM((SOURCES, LAGS, width), jnp.bfloat16),
            pltpu.SemaphoreType.DMA((SOURCES // BATCH,)),
        ],
        out_shape=jax.ShapeDtypeStruct((SOURCES, LAGS, width), jnp.bfloat16),
        compiler_params=pltpu.CompilerParams(vmem_limit_bytes=18 << 20),
        name="correlate",
    )(left, whole, *others, *split, alive, inverse)


def body(data, alive, sources):
    count = lax.axis_size("chan")
    width = data.shape[1] // count
    table = forward_table()
    relative = data.shape[0] == HELD and count == TEAM * TEAM
    if relative:
        swap = lambda x, k: lax.ppermute(x, "chan", [(i, i ^ k) for i in range(count)])
        team = range(1, TEAM)
        across = [[z * TEAM + p for z in range(count // TEAM)] for p in range(TEAM)]
        whole = prepare(data, table, count)
        data, whole = lax.optimization_barrier((data, whole))
        lent = lend(data, count)
        data, lent = lax.optimization_barrier((data, lent))
        lent = swap(lent, 1)
        whole = lax.all_to_all(whole, "chan", 0, 0, tiled=True, axis_index_groups=across)
        picked = pick(sources, alive, data, count)
        data, picked = lax.optimization_barrier((data, picked))
        picked = [picked[0]] + [swap(picked[k], k) for k in team]
        spectra = source_spectra(picked, table)
        keep_far, give_far = halves((2, 3), data, lent, table, count)
        give_far, spectra, data = lax.optimization_barrier((give_far, spectra, data))
        arrived = [swap(spectra, k * TEAM) for k in team]
        keep_near, give_near = halves((0, 1), data, lent, table, count)
        far = straddle(keep_far, swap(give_far, 2), table)
        arrived, whole, far = lax.optimization_barrier((arrived, whole, far))
        others = regroup(whole)
        src = whiten([spectra] + arrived)
        keep_near, src, others = lax.optimization_barrier((keep_near, src, others))
        others = [swap(others[k - 1], k) for k in team]
        near = straddle(keep_near, swap(give_near, 2), table)
        split = [near[0], swap(near[1], TEAM), swap(far[0], 2 * TEAM), swap(far[1], 3 * TEAM)]
        src = [src] + [swap(src, k) for k in team]
    else:
        me = lax.axis_index("chan")
        ids = sources.reshape(-1)
        near = ids[:, None] == me * width + jnp.arange(width, dtype=jnp.int32)[None, :]
        flags = jnp.sum(jnp.where(near, alive[None, :], 0), axis=1).astype(jnp.float32)
        chosen = jnp.where(jnp.arange(data.shape[1], dtype=jnp.int32)[:, None] == ids[None, :], 1.0, 0.0)
        picked = jnp.dot(data, chosen.astype(jnp.bfloat16), preferred_element_type=jnp.float32)
        picked = lax.all_gather(picked.astype(jnp.bfloat16), "chan", axis=0)
        alive_sources = lax.psum(flags, "chan")
        blocks = data.reshape(data.shape[0], count, width)
        blocks = lax.all_to_all(blocks, "chan", split_axis=1, concat_axis=0, tiled=True)
        blocks = blocks.reshape(SEGMENT_TALLY, SEGMENT_LENGTH, width)
        spectra = jnp.einsum("kt,wtc->wkc", table, blocks, preferred_element_type=jnp.float32)
        spectra = spectra.astype(jnp.bfloat16).reshape(TEAM, TEAM_WINDOWS, BINS, width)
        whole = spectra[:, 0:1]
        others = [spectra[:, 2 * k] for k in range(1, TEAM)]
        split = [spectra[z, 1::2] for z in range(TEAM)]
        src = whiten_all(jnp.transpose(picked, (2, 0, 1)), alive_sources, table)
    left = left_factor(src)
    out = correlate(relative, left, whole, others, split, alive[None, :], inverse_table())
    return out.reshape(ROUNDS, SRC, LAGS, width)


def solution(mesh):
    return jax.shard_map(
        body,
        mesh=mesh,
        in_specs=(P(("groups", "chan"), None), P(("groups", "chan")), P()),
        out_specs=P("groups", None, None, "chan"),
        check_vma=False,
    )
```
